128 devices in a mesh: wide: 32 (over y, x, core), narrow: 4 (over z).
Axes of the slice: x: 4, y: 4, z: 4, core: 2. Of those that a mesh axis runs over, the one named last changes fastest.
Arguments:
- volume: bfloat16 [256, 256, 128], P('wide', 'narrow'), may hold values from -6 to 6
- angles: float32 [2, 8], replicated, may hold values from -3.140625 to 3.140625
- tile_points: int32 [32768, 128], P(('wide', 'narrow')), may hold values from 0 to 65535
- tile_dest: int32 [32768, 1], P(('wide', 'narrow')), may hold values from 0 to 127; in each aligned block of 256 rows (0 to 255, 256 to 511, ...) at most 4 rows name the same one
Outputs:
- responses: bfloat16 [16, 256, 256, 128], P(None, 'wide', 'narrow')
- fiber_out: bfloat16 [16384, 4, 16, 128], P(('wide', 'narrow'))
The draws below stay inside these ranges and needn't reach their ends.
Inputs may be any that keep to these rules, and one draw needn't show every extreme that they name: `tile_dest`: among the 256 tiles of one device no owner is named more than 4 times, and in every draw some owner is named exactly 4 times by the tiles of some device.
All inputs are finite; a program needn't handle non-finite values.
Results may differ from the reference program's by a relative error of at most 0.0076.
Values may be sent and summed in bfloat16 or wider, within the bound.
No kernel may reach another device: no remote copies, remote signals or barrier semaphores. Data moves between devices by JAX's collectives and lax.ppermute only.
A program may use at most 64 MiB of HBM per device.

```python
import math
import jax
import jax.numpy as jnp
import numpy as np
from jax import lax

SZ = 8
CY = 64
NX = 128
NORI = 8
CHAN = 16
TAPS_PER_SIDE = 3
DILATION_SECOND = 2
PTS = 128
CAP = 4
NZ = 256
NY = 256
NBLOCKS = 128
TILE_DEV = 256
TILES = 32768
N_WIDE = 32
N_NARROW = 4


def with_ends(result, rng, smallest, largest):
    longest = result.shape.index(max(result.shape))
    spots = []
    for shift in (0, 1):
        where = [jax.random.randint(jax.random.fold_in(rng, axis), (), 0, length) for axis, length in enumerate(result.shape)]
        where[longest] = (where[longest] + shift) % result.shape[longest]
        spots.append(tuple(where))
    return result.at[spots[0]].set(smallest).at[spots[1]].set(largest)


def steps_of(rng, extent, shards, smallest, high):
    factor_of = 1.0
    for dim, shards_of in shards:
        heights = jax.random.uniform(jax.random.fold_in(jax.random.fold_in(rng, 6), dim), (shards_of,), jnp.float32, smallest / len(shards), high / len(shards))
        factor_of = factor_of * jnp.repeat(jnp.exp(heights), extent[dim] // shards_of).reshape((-1,) + (1,) * (len(extent) - 1 - dim))
    return factor_of


def shared_out(key, own, number, rows, count, top, most, slope):
    ranking = jax.random.permutation(key, count)
    crowded, common = shares(count, rows * top, most, slope, True), shares(count, rows * top, most, slope, False)
    places = jnp.arange(count)

    def named(sizes, offset_by):
        used = int((sizes > 0).sum())
        fixed = max(1, used // 4)
        passed = fixed + (places - fixed + offset_by * (used - fixed)) % max(1, count - fixed)
        return jnp.zeros((count,), jnp.int32).at[ranking[jnp.where(places < fixed, places, passed)]].set(jnp.asarray(sizes, jnp.int32))

    sizes = jnp.where(number % 4 == 0, named(crowded, number // 4), named(common, number - number // 4 - 1))
    mixed = jax.random.permutation(jax.random.fold_in(own, 3), count)
    source_of, receiver = mixed[0:count // 2 * 2:2], mixed[1:count // 2 * 2:2]
    slack = jnp.minimum(sizes[source_of] - 1, most - sizes[receiver]) // 2
    slack = jnp.where((source_of == ranking[0]) | (receiver == ranking[0]) | (sizes[receiver] == 0), 0, jnp.maximum(slack, 0))
    passed = jax.random.randint(jax.random.fold_in(own, 4), (count // 2,), 0, 1 << 20) % (slack + 1)
    sizes = sizes.at[source_of].add(-passed).at[receiver].add(passed)
    labels = jnp.searchsorted(jnp.cumsum(sizes), jnp.arange(rows * top), side="right").astype(jnp.int32)
    grid = labels.reshape(top, rows).T
    grid = grid[jax.random.permutation(jax.random.fold_in(own, 1), rows)]
    offset_by = jax.random.randint(jax.random.fold_in(own, 2), (rows, 1), 0, top)
    return jnp.take_along_axis(grid, (jnp.arange(top)[None, :] + offset_by) % top, axis=1)


def shares(number_of, total, most, slope, full):
    weights = [(1 << 20) // math.isqrt(grade ** slope) + 1 for grade in range(1, number_of + 1)]
    largest = most if full else min(most, max(-(-total // number_of), total * weights[0] // sum(weights)))
    least = 1 if total - largest >= number_of - 1 else 0
    given, spare = [largest] + [least] * (number_of - 1), total - largest - least * (number_of - 1)
    while spare > 0:
        movable = [i for i in range(1, number_of) if given[i] < largest] or [i for i in range(1, number_of) if given[i] < most]
        pool, budget = sum([weights[i] for i in movable]), spare
        for i in movable:
            extra = min(most - given[i], max(1, budget * weights[i] // pool), spare)
            given[i] = given[i] + extra
            spare = spare - extra
    return np.array(given)


def centred(rng, extent, scale, most, shards=(), dtype=jnp.bfloat16):
    values = jax.random.normal(rng, extent, jnp.float32) * scale
    if len(shards) > 0:
        values = steps_of(rng, extent, shards, -0.22, 0.18) * values
    return jnp.clip(values, min=-most, max=most).astype(dtype)


def setup_inputs(seed: int = 0) -> dict:
    arg_keys = jax.random.split(jax.random.key(seed), 5)
    volume = centred(arg_keys[0], (NZ, NY, NX), 1.0, 6.0, ((0, 32), (1, 4)))
    angles = jnp.clip(jax.random.uniform(arg_keys[1], (2, NORI), jnp.float32, -3.140625, 3.140625), -3.140625, 3.140625)
    tile_points = with_ends(jax.random.randint(arg_keys[2], (TILES, PTS), 0, min(SZ * CY * NX, 258112)), jax.random.fold_in(arg_keys[2], 1), 0, (min(SZ * CY * NX, 258112)) - 1).astype(jnp.int32)
    tile_dest_keys = jax.random.split(jax.random.fold_in(arg_keys[3], 1), TILES // TILE_DEV)
    tile_dest_turns = jax.random.permutation(jax.random.fold_in(arg_keys[3], 3), TILES // TILE_DEV)
    tile_dest = jax.vmap(lambda own, number: shared_out(jax.random.fold_in(arg_keys[3], 2), own, number, TILE_DEV, NBLOCKS, 1, CAP, 2))(tile_dest_keys, tile_dest_turns).reshape((TILES, 1))
    return {"volume": volume, "angles": angles, "tile_points": tile_points, "tile_dest": tile_dest}


response_gain = 6.0
smooth_sigma = 4.0


def tap_table():
    offsets = jnp.arange(-TAPS_PER_SIDE, TAPS_PER_SIDE + 1).astype(jnp.float32)
    gauss_bell = jnp.exp(-0.5 * offsets * offsets)
    normalized = gauss_bell / jnp.sum(gauss_bell)
    return jnp.stack([normalized, -offsets * normalized, (offsets * offsets - 1.0) * normalized]).astype(jnp.bfloat16)


def pass_along(field_in, tap_floats, tap_kind, tap_spacing, along_axis, output_count, border_depth):
    summed = None
    for offset in range(2 * TAPS_PER_SIDE + 1):
        shift = (offset - TAPS_PER_SIDE) * tap_spacing
        contribution = tap_floats[tap_kind, offset] * lax.slice_in_dim(field_in, border_depth - shift, border_depth - shift + output_count, axis=along_axis)
        summed = contribution if summed is None else summed + contribution
    return summed


def hessian_mix(along_x, tap_floats, tap_spacing, orient_weights, border_depth):
    z_count = along_x[0].shape[0] - 2 * border_depth
    y_count = along_x[0].shape[1] - 2 * border_depth

    def along_z(field_in, tap_kind):
        return pass_along(field_in, tap_floats, tap_kind, tap_spacing, 0, z_count, border_depth)

    def along_y(field_in, tap_kind):
        return pass_along(field_in, tap_floats, tap_kind, tap_spacing, 1, y_count, border_depth)

    z_plain = along_z(along_x[0], 0)
    hessian_terms = [
        along_y(along_z(along_x[2], 0), 0),
        along_y(z_plain, 2),
        along_y(along_z(along_x[0], 2), 0),
        along_y(along_z(along_x[1], 0), 1),
        along_y(along_z(along_x[1], 1), 0),
        along_y(along_z(along_x[0], 1), 1),
    ]
    stacked = jnp.stack(hessian_terms)
    return jnp.einsum("ok,kzyx->ozyx", orient_weights, stacked, precision=lax.Precision.HIGHEST)


def orientation_weights(angles):
    polar_angle = angles[0]
    azimuth = angles[1]
    dir_x = jnp.sin(polar_angle) * jnp.cos(azimuth)
    dir_y = jnp.sin(polar_angle) * jnp.sin(azimuth)
    dir_z = jnp.cos(polar_angle)
    return response_gain * jnp.stack([dir_x * dir_x, dir_y * dir_y, dir_z * dir_z, 2.0 * dir_x * dir_y, 2.0 * dir_x * dir_z, 2.0 * dir_y * dir_z], axis=1)


def smooth_matrix(points_count):
    source_pos = lax.broadcasted_iota(jnp.int32, (points_count, points_count), 0).astype(jnp.float32)
    target_pos = lax.broadcasted_iota(jnp.int32, (points_count, points_count), 1).astype(jnp.float32)
    distance = target_pos - source_pos
    gauss_bell = jnp.exp(-distance * distance / (2.0 * smooth_sigma * smooth_sigma))
    return (gauss_bell / jnp.sum(gauss_bell, axis=0, keepdims=True)).astype(jnp.bfloat16)


def smooth_tiles(bundle, smoothing_matrix):
    reshaped = bundle.reshape(-1, bundle.shape[-1])
    return jnp.dot(reshaped, smoothing_matrix, preferred_element_type=jnp.float32).astype(jnp.bfloat16).reshape(bundle.shape)


def sample_tiles(responses, points_here):
    channels = responses.shape[0]
    flattened = responses.reshape(channels, -1)
    picked = jnp.take(flattened, points_here.reshape(-1), axis=1)
    return picked.reshape(channels, points_here.shape[0], points_here.shape[1]).transpose(1, 0, 2)


def place_tiles(tile_rows, destination, block_count):
    tile_total = destination.shape[0]
    earlier = lax.broadcasted_iota(jnp.int32, (tile_total, tile_total), 0)
    later = lax.broadcasted_iota(jnp.int32, (tile_total, tile_total), 1)
    same_owner = (destination[:, None] == destination[None, :]) & (earlier < later)
    slot_rank = jnp.sum(same_owner.astype(jnp.int32), axis=0)
    slot_index = destination * CAP + slot_rank
    slot_ids = lax.broadcasted_iota(jnp.int32, (block_count * CAP, tile_total), 0)
    selector = (slot_ids == slot_index[None, :]).astype(jnp.bfloat16)
    moved = jnp.dot(selector, tile_rows.reshape(tile_total, -1), preferred_element_type=jnp.float32)
    return moved.astype(jnp.bfloat16).reshape((block_count, CAP) + tile_rows.shape[1:])


def reference(volume, angles, tile_points, tile_dest):
    border_depth = TAPS_PER_SIDE * DILATION_SECOND
    padded_volume = jnp.pad(volume, ((border_depth, border_depth), (border_depth, border_depth), (border_depth, border_depth)))
    tap_floats = tap_table().astype(jnp.float32)
    orient_weights = orientation_weights(angles)
    smoothing_matrix = smooth_matrix(PTS)
    block_count = N_WIDE * N_NARROW
    point_blocks = tile_points.reshape(block_count, TILE_DEV, PTS)
    dest_blocks = tile_dest.reshape(block_count, TILE_DEV)

    def one_block(inputs):
        block_index, points_here, dest_here = inputs
        wide_index = (block_index // N_NARROW).astype(jnp.int32)
        narrow_index = (block_index % N_NARROW).astype(jnp.int32)
        extended = lax.dynamic_slice(padded_volume, (wide_index * SZ, narrow_index * CY, jnp.int32(0)), (SZ + 2 * border_depth, CY + 2 * border_depth, NX + 2 * border_depth)).astype(jnp.float32)
        outputs = []
        for tap_spacing in (1, DILATION_SECOND):
            along_x = [pass_along(extended, tap_floats, tap_kind, tap_spacing, 2, NX, border_depth) for tap_kind in range(3)]
            outputs.append(hessian_mix(along_x, tap_floats, tap_spacing, orient_weights, border_depth))
        responses = jnp.concatenate(outputs, axis=0).astype(jnp.bfloat16)
        tile_rows = smooth_tiles(sample_tiles(responses, points_here), smoothing_matrix)
        outgoing = place_tiles(tile_rows, dest_here, block_count)
        return responses, outgoing

    block_ids = jnp.arange(block_count).astype(jnp.int32)
    resp_all, sent_all = lax.map(one_block, (block_ids, point_blocks, dest_blocks))
    responses = resp_all.reshape(N_WIDE, N_NARROW, CHAN, SZ, CY, NX).transpose(2, 0, 3, 1, 4, 5).reshape(CHAN, NZ, NY, NX)
    fiber_out = sent_all.transpose(1, 0, 2, 3, 4).reshape(block_count * block_count, CAP, CHAN, PTS)
    return responses, fiber_out
```

```python
import jax
import jax.numpy as jnp
import ml_dtypes
import numpy as np
from jax import lax
from jax.experimental import pallas as pl
from jax.experimental.pallas import tpu as pltpu
from jax.sharding import PartitionSpec as P

TAPS_PER_SIDE = 3
SPACINGS = (1, 2)
CAP = 4
BORDER = 6
Y_PAD = 8
RESPONSE_GAIN = 6.0
SMOOTH_SIGMA = 4.0

SZ, CY, NX = 8, 64, 128
ROWS = SZ * CY
DEEP = SZ + 2 * BORDER
TALL = CY + 2 * Y_PAD
COMPS = 6
LANES = 128
TILES = 256
PTS = 128
STEP_TILES = 16
STEPS = TILES // STEP_TILES
OWNERS = 128
SLOTS = OWNERS * CAP
SEND_ROWS = CAP * 2 * COMPS

KINDS = ((2, 0, 0), (0, 2, 0), (0, 0, 2), (1, 1, 0), (1, 0, 1), (0, 1, 1))


def tap_table():
    offsets = np.arange(-TAPS_PER_SIDE, TAPS_PER_SIDE + 1).astype(np.float32)
    bell = np.exp(np.float32(-0.5) * offsets * offsets)
    normalized = bell / np.sum(bell)
    taps = np.stack([normalized, -offsets * normalized, (offsets * offsets - 1.0) * normalized])
    return taps.astype(ml_dtypes.bfloat16).astype(np.float32)


TAPS = tap_table()


def band(kind, spacing, rows_in, count_out, start):
    result = np.zeros((count_out, rows_in), np.float32)
    for tap in range(2 * TAPS_PER_SIDE + 1):
        shift = (tap - TAPS_PER_SIDE) * spacing
        for out in range(count_out):
            source = out + start - shift
            if 0 <= source < rows_in:
                result[out, source] += TAPS[kind, tap]
    return result


def y_bands():
    return np.concatenate(
        [band(kind, d, TALL, CY, Y_PAD) for d in SPACINGS for kind in range(3)], axis=0
    ).astype(ml_dtypes.bfloat16)


def x_bands():
    return np.stack(
        [np.stack([band(kind, d, NX, NX, 0).T for kind in range(3)]) for d in SPACINGS]
    ).astype(ml_dtypes.bfloat16)


def table_bands():
    bands = np.stack([np.stack([band(kind, d, NX, NX, 0).T for kind in range(3)]) for d in SPACINGS])
    result = np.zeros((2, COMPS, NX, NX * 8), np.float32)
    for s in range(2):
        for x in range(NX):
            half = ((x // 8) % 2) ^ s
            column = (x // 16) * 128 + half * 64 + (x % 8) * 8
            for comp in range(COMPS):
                result[s, comp, :, column + comp] = bands[s, KINDS[comp][0], :, x]
    return result.reshape(2, COMPS * NX, NX * 8).astype(ml_dtypes.bfloat16)


def pack_matrix():
    result = np.zeros((4 * SEND_ROWS, 4 * CAP * 16), np.float32)
    for slot in range(4 * CAP):
        for s in range(2):
            for comp in range(COMPS):
                result[slot * 12 + s * COMPS + comp, slot * 16 + s * 8 + comp] = 1.0
    return result.astype(ml_dtypes.bfloat16)


def z_pass(y_fields, s, kind_y, kinds_z, z):
    d = SPACINGS[s]
    planes = [y_fields[z + BORDER - k * d, s, kind_y] for k in range(-TAPS_PER_SIDE, TAPS_PER_SIDE + 1)]
    results = {}
    for kind in kinds_z:
        total = None
        for side in range(TAPS_PER_SIDE):
            pair = planes[side] - planes[6 - side] if kind == 1 else planes[side] + planes[6 - side]
            if TAPS[kind, side] == 0.0:
                continue
            term = float(TAPS[kind, side]) * pair
            total = term if total is None else total + term
        if kind != 1:
            total = total + float(TAPS[kind, TAPS_PER_SIDE]) * planes[TAPS_PER_SIDE]
        results[kind] = total
    return results


def sample_kernel(
    slot_ref, rows_hbm, block_ref, low_ref, high_ref, left_ref, right_ref, column_ref, y_band_ref, table_band_ref,
    smoother_ref, pack_ref, send_ref, fields_ref, ext, y_fields, table, tiles, index_rows, sem, *gathered
):
    def copy_rows(step, side):
        return pltpu.make_async_copy(
            rows_hbm.at[pl.ds(pl.multiple_of(step * STEP_TILES, STEP_TILES), STEP_TILES)], index_rows[side], sem.at[side]
        )

    copy_rows(0, 0).start()
    copy_rows(1, 1).start()

    ext[BORDER:BORDER + SZ, Y_PAD:Y_PAD + CY, :] = block_ref[...]
    ext[0:BORDER, Y_PAD:Y_PAD + CY, :] = low_ref[...]
    ext[BORDER + SZ:DEEP, Y_PAD:Y_PAD + CY, :] = high_ref[...]
    ext[:, 0:Y_PAD, :] = left_ref[...]
    ext[:, Y_PAD + CY:TALL, :] = right_ref[...]
    tiles[...] = jnp.zeros_like(tiles)
    gathered[1][...] = jnp.zeros_like(gathered[1])

    for z in range(0, DEEP, 2):
        pair = jnp.concatenate([ext[z], ext[z + 1]], axis=1)
        out = jnp.dot(y_band_ref[...], pair, preferred_element_type=jnp.float32)
        for s in range(2):
            for kind in range(3):
                rows = slice((s * 3 + kind) * CY, (s * 3 + kind + 1) * CY)
                y_fields[z, s, kind] = out[rows, 0:NX]
                y_fields[z + 1, s, kind] = out[rows, NX:2 * NX]

    for s in range(2):
        for z in range(SZ):
            passed = [z_pass(y_fields, s, 0, (0, 1, 2), z), z_pass(y_fields, s, 1, (0, 1), z), z_pass(y_fields, s, 2, (0,), z)]
            for comp, (_, kind_y, kind_z) in enumerate(KINDS):
                fields_ref[s, z * CY:(z + 1) * CY, comp * NX:(comp + 1) * NX] = passed[kind_y][kind_z].astype(jnp.bfloat16)

    lower = lax.broadcasted_iota(jnp.int32, (ROWS, LANES), 1) < 64
    for m in range(0, NX // 16, 2):
        outs = [
            jnp.dot(fields_ref[s], table_band_ref[s, :, m * 128:(m + 2) * 128], preferred_element_type=jnp.float32)
            for s in range(2)
        ]
        for half in range(2):
            first, second = (out[:, half * 128:(half + 1) * 128] for out in outs)
            group = (m + half) * 2
            table[group * ROWS:(group + 1) * ROWS, :] = jnp.where(lower, first, second)
            table[(group + 1) * ROWS:(group + 2) * ROWS, :] = jnp.where(lower, second, first)

    eye = (
        lax.broadcasted_iota(jnp.int32, (LANES, LANES), 0) == lax.broadcasted_iota(jnp.int32, (LANES, LANES), 1)
    ).astype(jnp.bfloat16)

    def gather(step, side):
        copy_rows(0, side).wait()
        for tile in range(STEP_TILES):
            for p in range(PTS):
                row = index_rows[side][tile, p]
                gathered[side][pl.ds(tile * PTS + p, 1), :] = table[pl.ds(row, 1), :]
        copy_rows(jnp.minimum(step + 2, STEPS - 1), side).start()

    def finish(step, side):
        flat = gathered[side][...].astype(jnp.bfloat16)
        turned = lax.dot_general(eye, flat, (((1,), (1,)), ((), ())), preferred_element_type=jnp.float32)
        picked = []
        for tile in range(STEP_TILES):
            column = column_ref[pl.ds(jnp.maximum(step, 0) * STEP_TILES + tile, 1), :]
            column = jnp.broadcast_to(column, (8, PTS))
            here = turned[:, tile * PTS:(tile + 1) * PTS]
            lane = [(0, 64), (64, 0)]
            both = [here[0:8], here[64:72]]
            for x in range(1, 16):
                hit = column == x
                for s in range(2):
                    start = lane[x // 8][s] + (x % 8) * 8
                    both[s] = jnp.where(hit, here[start:start + 8], both[s])
            picked.append(jnp.concatenate(both, axis=0).astype(jnp.bfloat16))
        smooth = jnp.dot(
            jnp.concatenate(picked, axis=0), smoother_ref[...], preferred_element_type=jnp.float32
        ).astype(jnp.bfloat16)
        for tile in range(STEP_TILES):
            tiles[slot_ref[(step + 1) * STEP_TILES + tile]] = smooth[tile * 16:(tile + 1) * 16]

    @pl.loop(0, STEPS // 2)
    def _(i):
        gather(2 * i, 0)
        finish(2 * i - 1, 1)
        gather(2 * i + 1, 1)
        finish(2 * i, 0)

    finish(STEPS - 1, 1)
    copy_rows(0, 0).wait()
    copy_rows(0, 1).wait()

    @pl.loop(0, OWNERS // 4)
    def _(quad):
        here = tiles[pl.ds(quad * 16, 16)].reshape(256, PTS)
        packed = jnp.dot(pack_ref[...], here, preferred_element_type=jnp.float32).astype(jnp.bfloat16)
        send_ref[pl.ds(pl.multiple_of(quad * 4 * SEND_ROWS, 4 * SEND_ROWS), 4 * SEND_ROWS), :] = packed


def response_kernel(weight_ref, fields_ref, x_band_ref, out_ref):
    for s in range(2):
        parts = [
            jnp.dot(
                fields_ref[s, :, comp * NX:(comp + 1) * NX], x_band_ref[s, KINDS[comp][0]], preferred_element_type=jnp.float32
            )
            for comp in range(COMPS)
        ]
        for o in range(8):
            total = parts[0] * weight_ref[o, 0]
            for comp in range(1, COMPS):
                total = total + parts[comp] * weight_ref[o, comp]
            out_ref[s * 8 + o, 0] = total.astype(jnp.bfloat16)


def mix_kernel(high_ref, low_ref, arrived_ref, out_ref):
    here = arrived_ref[...]
    for quad in range(8):
        part = here[quad * 4 * SEND_ROWS:(quad + 1) * 4 * SEND_ROWS]
        mixed = jnp.dot(high_ref[...], part, preferred_element_type=jnp.float32)
        mixed = mixed + jnp.dot(low_ref[...], part, preferred_element_type=jnp.float32)
        out_ref[quad * 256:(quad + 1) * 256, :] = mixed.astype(jnp.bfloat16)


def orientation_weights(angles):
    polar_angle = angles[0]
    azimuth = angles[1]
    dir_x = jnp.sin(polar_angle) * jnp.cos(azimuth)
    dir_y = jnp.sin(polar_angle) * jnp.sin(azimuth)
    dir_z = jnp.cos(polar_angle)
    return RESPONSE_GAIN * jnp.stack(
        [
            dir_x * dir_x,
            dir_y * dir_y,
            dir_z * dir_z,
            2.0 * dir_x * dir_y,
            2.0 * dir_x * dir_z,
            2.0 * dir_y * dir_z,
        ],
        axis=1,
    )


def smooth_matrix():
    source = np.arange(PTS, dtype=np.float32)[:, None]
    target = np.arange(PTS, dtype=np.float32)[None, :]
    distance = target - source
    bell = np.exp(-distance * distance / np.float32(2.0 * SMOOTH_SIGMA * SMOOTH_SIGMA))
    return (bell / np.sum(bell, axis=0, keepdims=True)).astype(ml_dtypes.bfloat16)


def shifted(value, axis, step):
    count = lax.axis_size(axis)
    forward = [(i, i + 1) for i in range(count - 1)]
    backward = [(i + 1, i) for i in range(count - 1)]
    return lax.ppermute(value, axis, forward if step > 0 else backward)


def mix_matrix(weights):
    scales = jnp.zeros((16, 12), jnp.float32)
    scales = scales.at[0:8, 0:6].set(weights).at[8:16, 6:12].set(weights)
    rows = lax.broadcasted_iota(jnp.int32, (256, 192), 0) // 16
    columns = lax.broadcasted_iota(jnp.int32, (256, 192), 1) // 12
    full = jnp.where(rows == columns, jnp.tile(scales, (16, 16)), 0.0)
    high = full.astype(jnp.bfloat16)
    low = (full - high.astype(jnp.float32)).astype(jnp.bfloat16)
    return high, low


def per_device(volume, angles, tile_points, tile_dest):
    low = shifted(volume[SZ - BORDER:], "wide", 1)
    high = shifted(volume[:BORDER], "wide", -1)
    edge_low = jnp.concatenate([part[:, CY - Y_PAD:] for part in (low, volume, high)], axis=0)
    edge_high = jnp.concatenate([part[:, :Y_PAD] for part in (low, volume, high)], axis=0)
    left = shifted(edge_low, "narrow", 1)
    right = shifted(edge_high, "narrow", -1)

    table_rows = ((tile_points >> 3) & 15) * ROWS + (tile_points >> 7)
    columns = tile_points & 15
    dest = tile_dest[:, 0]
    earlier = lax.broadcasted_iota(jnp.int32, (TILES, TILES), 0)
    later = lax.broadcasted_iota(jnp.int32, (TILES, TILES), 1)
    same_owner = (dest[:, None] == dest[None, :]) & (earlier < later)
    slot = dest * CAP + jnp.sum(same_owner.astype(jnp.int32), axis=0)
    slot = jnp.concatenate([jnp.full((STEP_TILES,), SLOTS, jnp.int32), slot])

    weights = orientation_weights(angles)
    mix_high, mix_low = mix_matrix(weights)

    vmem = pl.BlockSpec(memory_space=pltpu.VMEM)
    send, fields = pl.pallas_call(
        sample_kernel,
        out_shape=(
            jax.ShapeDtypeStruct((OWNERS * SEND_ROWS, PTS), jnp.bfloat16),
            jax.ShapeDtypeStruct((2, ROWS, COMPS * NX), jnp.bfloat16),
        ),
        in_specs=[pl.BlockSpec(memory_space=pltpu.SMEM), pl.BlockSpec(memory_space=pl.ANY)] + [vmem] * 10,
        out_specs=(vmem, vmem),
        scratch_shapes=[
            pltpu.VMEM((DEEP, TALL, NX), jnp.bfloat16),
            pltpu.VMEM((DEEP, 2, 3, CY, NX), jnp.float32),
            pltpu.VMEM((NX // 8 * ROWS, LANES), jnp.float32),
            pltpu.VMEM((SLOTS + 1, 16, PTS), jnp.bfloat16),
            [pltpu.SMEM((STEP_TILES, PTS), jnp.int32)] * 2,
            pltpu.SemaphoreType.DMA((2,)),
            pltpu.VMEM((STEP_TILES * PTS, LANES), jnp.float32),
            pltpu.VMEM((STEP_TILES * PTS, LANES), jnp.float32),
        ],
        compiler_params=pltpu.CompilerParams(vmem_limit_bytes=48 << 20),
        cost_estimate=pl.CostEstimate(flops=4_000_000_000, bytes_accessed=8_000_000, transcendentals=0),
        name="sample",
    )(
        slot, table_rows, volume, low, high, left, right, columns,
        jnp.asarray(y_bands()), jnp.asarray(table_bands()), jnp.asarray(smooth_matrix()), jnp.asarray(pack_matrix()),
    )

    arrived = lax.all_to_all(
        send.reshape(OWNERS, SEND_ROWS, PTS), ("wide", "narrow"), split_axis=0, concat_axis=0, tiled=True
    )

    responses = pl.pallas_call(
        response_kernel,
        grid=(SZ,),
        out_shape=jax.ShapeDtypeStruct((16, SZ, CY, NX), jnp.bfloat16),
        in_specs=[
            pl.BlockSpec(memory_space=pltpu.SMEM),
            pl.BlockSpec((2, CY, COMPS * NX), lambda z: (0, z, 0)),
            pl.BlockSpec((2, 3, NX, NX), lambda z: (0, 0, 0, 0)),
        ],
        out_specs=pl.BlockSpec((16, 1, CY, NX), lambda z: (0, z, 0, 0)),
        compiler_params=pltpu.CompilerParams(vmem_limit_bytes=16 << 20),
        cost_estimate=pl.CostEstimate(flops=200_000_000, bytes_accessed=4_000_000, transcendentals=0),
        name="respond",
    )(weights, fields, jnp.asarray(x_bands()))

    fibers = pl.pallas_call(
        mix_kernel,
        grid=(4,),
        out_shape=jax.ShapeDtypeStruct((SLOTS * 16, PTS), jnp.bfloat16),
        in_specs=[
            pl.BlockSpec((256, 192), lambda i: (0, 0)),
            pl.BlockSpec((256, 192), lambda i: (0, 0)),
            pl.BlockSpec((32 * SEND_ROWS, PTS), lambda i: (i, 0)),
        ],
        out_specs=pl.BlockSpec((SLOTS * 4, PTS), lambda i: (i, 0)),
        compiler_params=pltpu.CompilerParams(vmem_limit_bytes=16 << 20),
        cost_estimate=pl.CostEstimate(flops=1_600_000_000, bytes_accessed=4_000_000, transcendentals=0),
        name="mix",
    )(mix_high, mix_low, arrived.reshape(OWNERS * SEND_ROWS, PTS))
    return responses, fibers.reshape(OWNERS, CAP, 16, PTS)


def solution(mesh):
    return jax.shard_map(
        per_device,
        mesh=mesh,
        in_specs=(
            P("wide", "narrow", None),
            P(),
            P(("wide", "narrow"), None),
            P(("wide", "narrow"), None),
        ),
        out_specs=(P(None, "wide", "narrow", None), P(("wide", "narrow"), None, None, None)),
        check_vma=False,
    )
```

```python
import jax
import jax.numpy as jnp
import ml_dtypes
import numpy as np
from jax import lax
from jax.experimental import pallas as pl
from jax.experimental.pallas import tpu as pltpu
from jax.sharding import PartitionSpec as P

TAPS_PER_SIDE = 3
SPACINGS = (1, 2)
CAP = 4
BORDER = 6
Y_PAD = 8
RESPONSE_GAIN = 6.0
SMOOTH_SIGMA = 4.0

SZ, CY, NX = 8, 64, 128
ROWS = SZ * CY
DEEP = SZ + 2 * BORDER
TALL = CY + 2 * Y_PAD
COMPS = 6
LANES = 128
TILES = 256
PTS = 128
STEP_TILES = 16
STEPS = TILES // STEP_TILES
OWNERS = 128
SLOTS = OWNERS * CAP
SEND_ROWS = CAP * 2 * COMPS
MIX_PARTS = 4

KINDS = ((2, 0, 0), (0, 2, 0), (0, 0, 2), (1, 1, 0), (1, 0, 1), (0, 1, 1))


def tap_table():
    offsets = np.arange(-TAPS_PER_SIDE, TAPS_PER_SIDE + 1).astype(np.float32)
    bell = np.exp(np.float32(-0.5) * offsets * offsets)
    normalized = bell / np.sum(bell)
    taps = np.stack([normalized, -offsets * normalized, (offsets * offsets - 1.0) * normalized])
    return taps.astype(ml_dtypes.bfloat16).astype(np.float32)


TAPS = tap_table()


def band(kind, spacing, rows_in, count_out, start):
    result = np.zeros((count_out, rows_in), np.float32)
    for tap in range(2 * TAPS_PER_SIDE + 1):
        shift = (tap - TAPS_PER_SIDE) * spacing
        for out in range(count_out):
            source = out + start - shift
            if 0 <= source < rows_in:
                result[out, source] += TAPS[kind, tap]
    return result


def y_bands():
    return np.concatenate(
        [band(kind, d, TALL, CY, Y_PAD) for d in SPACINGS for kind in range(3)], axis=0
    ).astype(ml_dtypes.bfloat16)


def x_bands():
    return np.stack(
        [np.stack([band(kind, d, NX, NX, 0).T for kind in range(3)]) for d in SPACINGS]
    ).astype(ml_dtypes.bfloat16)


def table_bands():
    result = np.zeros((2, COMPS, 48, LANES), np.float32)
    for s in range(2):
        for x in range(16):
            column = ((x // 8) ^ s) * 64 + (x % 8) * 8
            for comp in range(COMPS):
                bands = band(KINDS[comp][0], SPACINGS[s], 48, 48, 0)
                result[s, comp, :, column + comp] = bands[x + 16]
    return result.astype(ml_dtypes.bfloat16)


def pack_matrix():
    result = np.zeros((4 * SEND_ROWS, 4 * CAP * 16), np.float32)
    for slot in range(4 * CAP):
        for s in range(2):
            for comp in range(COMPS):
                result[slot * 12 + s * COMPS + comp, slot * 16 + s * 8 + comp] = 1.0
    return result.astype(ml_dtypes.bfloat16)


def z_pass(y_fields, s, kind_y, kinds_z, z):
    d = SPACINGS[s]
    planes = [y_fields[z + BORDER - k * d, s, kind_y] for k in range(-TAPS_PER_SIDE, TAPS_PER_SIDE + 1)]
    results = {}
    for kind in kinds_z:
        total = None
        for side in range(TAPS_PER_SIDE):
            pair = planes[side] - planes[6 - side] if kind == 1 else planes[side] + planes[6 - side]
            if TAPS[kind, side] == 0.0:
                continue
            term = float(TAPS[kind, side]) * pair
            total = term if total is None else total + term
        if kind != 1:
            total = total + float(TAPS[kind, TAPS_PER_SIDE]) * planes[TAPS_PER_SIDE]
        results[kind] = total
    return results


def sample_kernel(
    slot_ref, rows_ref, block_hbm, low_ref, high_ref, left_ref, right_ref, column_ref, y_band_hbm, table_band_hbm,
    smoother_hbm, pack_hbm, send_ref, fields_ref, ext, y_fields, bands, table, tiles, y_band, base_band, smoother, pack,
    index_rows, sem, load_sem, *gathered
):
    def copy_rows(step, side):
        return pltpu.make_async_copy(
            rows_ref.at[pl.ds(pl.multiple_of(step * STEP_TILES, STEP_TILES), STEP_TILES)], index_rows[side], sem.at[side]
        )

    inside = (slice(BORDER, BORDER + SZ), slice(Y_PAD, Y_PAD + CY))
    loads = [
        pltpu.make_async_copy(source, target, load_sem.at[i])
        for i, (source, target) in enumerate((
            (block_hbm, ext.at[inside[0], inside[1], :]), (y_band_hbm, y_band), (table_band_hbm, base_band),
            (smoother_hbm, smoother), (pack_hbm, pack),
        ))
    ]
    for load in loads:
        load.start()
    copy_rows(0, 0).start()
    copy_rows(1, 1).start()

    ext[0:BORDER, Y_PAD:Y_PAD + CY, :] = low_ref[...]
    ext[BORDER + SZ:DEEP, Y_PAD:Y_PAD + CY, :] = high_ref[...]
    ext[:, 0:Y_PAD, :] = left_ref[...]
    ext[:, Y_PAD + CY:TALL, :] = right_ref[...]
    bands[...] = jnp.zeros_like(bands)
    tiles[...] = jnp.zeros_like(tiles)
    gathered[1][...] = jnp.zeros_like(gathered[1])
    for load in loads:
        load.wait()

    for s in range(2):
        for comp in range(COMPS):
            for m in range(NX // 16):
                first, last = max(0, 16 * m - 16), min(NX, 16 * m + 32)
                skip = first - (16 * m - 16)
                bands[s, comp * NX + first:comp * NX + last, m * LANES:(m + 1) * LANES] = (
                    base_band[s, comp, skip:skip + last - first, :]
                )

    for z in range(0, DEEP, 2):
        pair = jnp.concatenate([ext[z], ext[z + 1]], axis=1)
        for s in range(2):
            out = jnp.dot(y_band[s * 3 * CY:(s + 1) * 3 * CY, :], pair, preferred_element_type=jnp.float32)
            for kind in range(3):
                y_fields[z, s, kind] = out[kind * CY:(kind + 1) * CY, 0:NX]
                y_fields[z + 1, s, kind] = out[kind * CY:(kind + 1) * CY, NX:2 * NX]

    for s in range(2):
        for z in range(SZ):
            passed = [z_pass(y_fields, s, 0, (0, 1, 2), z), z_pass(y_fields, s, 1, (0, 1), z), z_pass(y_fields, s, 2, (0,), z)]
            for comp, (_, kind_y, kind_z) in enumerate(KINDS):
                fields_ref[s, z * CY:(z + 1) * CY, comp * NX:(comp + 1) * NX] = passed[kind_y][kind_z].astype(jnp.bfloat16)

    lower = lax.broadcasted_iota(jnp.int32, (ROWS // 2, LANES), 1) < 64
    for m in range(0, NX // 16, 2):
        for part in range(0, ROWS, ROWS // 2):
            outs = [
                jnp.dot(
                    fields_ref[s, part:part + ROWS // 2, :], bands[s, :, m * LANES:(m + 2) * LANES],
                    preferred_element_type=jnp.float32,
                )
                for s in range(2)
            ]
            for half in range(2):
                first, second = (out[:, half * LANES:(half + 1) * LANES] for out in outs)
                start = (m + half) * 2 * ROWS + part
                table[start:start + ROWS // 2, :] = jnp.where(lower, first, second)
                table[start + ROWS:start + ROWS + ROWS // 2, :] = jnp.where(lower, second, first)

    eye = (
        lax.broadcasted_iota(jnp.int32, (LANES, LANES), 0) == lax.broadcasted_iota(jnp.int32, (LANES, LANES), 1)
    ).astype(jnp.bfloat16)

    def gather(side, tile):
        for p in range(PTS):
            row = index_rows[side][tile, p]
            gathered[side][pl.ds(tile * PTS + p, 1), :] = table[pl.ds(row, 1), :]

    def finish(step, side, group):
        flat = gathered[side][group * 4 * PTS:(group + 1) * 4 * PTS, :].astype(jnp.bfloat16)
        turned = lax.dot_general(eye, flat, (((1,), (1,)), ((), ())), preferred_element_type=jnp.float32)
        picked = []
        for t in range(4):
            column = column_ref[pl.ds(jnp.maximum(step, 0) * STEP_TILES + group * 4 + t, 1), :]
            column = jnp.broadcast_to(column, (8, PTS))
            here = turned[:, t * PTS:(t + 1) * PTS]
            both = [here[0:8], here[64:72]]
            for x in range(1, 16):
                hit = column == x
                for s in range(2):
                    start = ((x // 8) ^ s) * 64 + (x % 8) * 8
                    both[s] = jnp.where(hit, here[start:start + 8], both[s])
            picked.append(jnp.concatenate(both, axis=0).astype(jnp.bfloat16))
        smooth = jnp.dot(
            jnp.concatenate(picked, axis=0), smoother[...], preferred_element_type=jnp.float32
        ).astype(jnp.bfloat16)
        for t in range(4):
            tiles[slot_ref[(step + 1) * STEP_TILES + group * 4 + t]] = smooth[t * 16:(t + 1) * 16]

    def advance(step, side):
        copy_rows(0, side).wait()
        for tile in range(STEP_TILES):
            gather(side, tile)
        for group in range(STEP_TILES // 4):
            finish(step - 1, 1 - side, group)
        copy_rows(jnp.minimum(step + 2, STEPS - 1), side).start()

    @pl.loop(0, STEPS // 2)
    def _(i):
        advance(2 * i, 0)
        advance(2 * i + 1, 1)

    for group in range(STEP_TILES // 4):
        finish(STEPS - 1, 1, group)
    copy_rows(0, 0).wait()
    copy_rows(0, 1).wait()

    @pl.loop(0, OWNERS // 4)
    def _(quad):
        here = tiles[pl.ds(quad * 16, 16)].reshape(256, PTS)
        packed = jnp.dot(pack[...], here, preferred_element_type=jnp.float32).astype(jnp.bfloat16)
        send_ref[pl.ds(pl.multiple_of(quad * 4 * SEND_ROWS, 4 * SEND_ROWS), 4 * SEND_ROWS), :] = packed


def response_kernel(weight_ref, fields_ref, x_band_ref, out_ref):
    for s in range(2):
        parts = [
            jnp.dot(
                fields_ref[s, :, comp * NX:(comp + 1) * NX], x_band_ref[s, KINDS[comp][0]], preferred_element_type=jnp.float32
            )
            for comp in range(COMPS)
        ]
        for o in range(8):
            total = parts[0] * weight_ref[o, 0]
            for comp in range(1, COMPS):
                total = total + parts[comp] * weight_ref[o, comp]
            out_ref[s * 8 + o, 0] = total.astype(jnp.bfloat16)


def mix_kernel(mix_ref, arrived_ref, out_hbm, out, sem):
    copies = []
    for part in range(MIX_PARTS):
        pairs = 16 // MIX_PARTS
        for pair in range(part * pairs, (part + 1) * pairs):
            first = arrived_ref[pair * 8 * SEND_ROWS:(pair * 8 + 4) * SEND_ROWS]
            second = arrived_ref[(pair * 8 + 4) * SEND_ROWS:(pair * 8 + 8) * SEND_ROWS]
            here = jnp.concatenate([first, second], axis=1)
            mixed = jnp.dot(mix_ref[0], here, preferred_element_type=jnp.float32)
            mixed = (mixed + jnp.dot(mix_ref[1], here, preferred_element_type=jnp.float32)).astype(jnp.bfloat16)
            out[pair * 512:pair * 512 + 256, :] = mixed[:, 0:PTS]
            out[pair * 512 + 256:pair * 512 + 512, :] = mixed[:, PTS:2 * PTS]
        rows = slice(part * pairs * 512, (part + 1) * pairs * 512)
        copy = pltpu.make_async_copy(out.at[rows, :], out_hbm.at[rows, :], sem.at[part])
        copy.start()
        copies.append(copy)
    for copy in copies:
        copy.wait()


def orientation_weights(angles):
    polar_angle = angles[0]
    azimuth = angles[1]
    dir_x = jnp.sin(polar_angle) * jnp.cos(azimuth)
    dir_y = jnp.sin(polar_angle) * jnp.sin(azimuth)
    dir_z = jnp.cos(polar_angle)
    return RESPONSE_GAIN * jnp.stack(
        [
            dir_x * dir_x,
            dir_y * dir_y,
            dir_z * dir_z,
            2.0 * dir_x * dir_y,
            2.0 * dir_x * dir_z,
            2.0 * dir_y * dir_z,
        ],
        axis=1,
    )


def smooth_matrix():
    source = np.arange(PTS, dtype=np.float32)[:, None]
    target = np.arange(PTS, dtype=np.float32)[None, :]
    distance = target - source
    bell = np.exp(-distance * distance / np.float32(2.0 * SMOOTH_SIGMA * SMOOTH_SIGMA))
    return (bell / np.sum(bell, axis=0, keepdims=True)).astype(ml_dtypes.bfloat16)


def shifted(value, axis, step):
    count = lax.axis_size(axis)
    forward = [(i, i + 1) for i in range(count - 1)]
    backward = [(i + 1, i) for i in range(count - 1)]
    return lax.ppermute(value, axis, forward if step > 0 else backward)


def mix_matrix(weights):
    scales = jnp.zeros((16, 12), jnp.float32)
    scales = scales.at[0:8, 0:6].set(weights).at[8:16, 6:12].set(weights)
    rows = lax.broadcasted_iota(jnp.int32, (256, 192), 0) // 16
    columns = lax.broadcasted_iota(jnp.int32, (256, 192), 1) // 12
    full = jnp.where(rows == columns, jnp.tile(scales, (16, 16)), 0.0)
    high = full.astype(jnp.bfloat16)
    low = (full - high.astype(jnp.float32)).astype(jnp.bfloat16)
    return jnp.stack([high, low])


def per_device(volume, angles, tile_points, tile_dest):
    low = shifted(volume[SZ - BORDER:], "wide", 1)
    high = shifted(volume[:BORDER], "wide", -1)
    edge_low = jnp.concatenate([part[:, CY - Y_PAD:] for part in (low, volume, high)], axis=0)
    edge_high = jnp.concatenate([part[:, :Y_PAD] for part in (low, volume, high)], axis=0)
    left = shifted(edge_low, "narrow", 1)
    right = shifted(edge_high, "narrow", -1)

    table_rows = ((tile_points >> 3) & 15) * ROWS + (tile_points >> 7)
    columns = tile_points & 15
    dest = tile_dest[:, 0]
    earlier = lax.broadcasted_iota(jnp.int32, (TILES, TILES), 0)
    later = lax.broadcasted_iota(jnp.int32, (TILES, TILES), 1)
    same_owner = (dest[:, None] == dest[None, :]) & (earlier < later)
    slot = dest * CAP + jnp.sum(same_owner.astype(jnp.int32), axis=0)
    slot = jnp.concatenate([jnp.full((STEP_TILES,), SLOTS, jnp.int32), slot])

    weights = orientation_weights(angles)
    mix = mix_matrix(weights)

    vmem = pl.BlockSpec(memory_space=pltpu.VMEM)
    hbm = pl.BlockSpec(memory_space=pltpu.HBM)
    send, fields = pl.pallas_call(
        sample_kernel,
        out_shape=(
            jax.ShapeDtypeStruct((OWNERS * SEND_ROWS, PTS), jnp.bfloat16),
            jax.ShapeDtypeStruct((2, ROWS, COMPS * NX), jnp.bfloat16),
        ),
        in_specs=[pl.BlockSpec(memory_space=pltpu.SMEM), vmem, hbm] + [vmem] * 5 + [hbm] * 4,
        out_specs=(vmem, vmem),
        scratch_shapes=[
            pltpu.VMEM((DEEP, TALL, NX), jnp.bfloat16),
            pltpu.VMEM((DEEP, 2, 3, CY, NX), jnp.float32),
            pltpu.VMEM((2, COMPS * NX, NX * 8), jnp.bfloat16),
            pltpu.VMEM((NX // 8 * ROWS, LANES), jnp.float32),
            pltpu.VMEM((SLOTS + 1, 16, PTS), jnp.bfloat16),
            pltpu.VMEM((6 * CY, TALL), jnp.bfloat16),
            pltpu.VMEM((2, COMPS, 48, LANES), jnp.bfloat16),
            pltpu.VMEM((PTS, PTS), jnp.bfloat16),
            pltpu.VMEM((4 * SEND_ROWS, 4 * CAP * 16), jnp.bfloat16),
            [pltpu.SMEM((STEP_TILES, PTS), jnp.int32)] * 2,
            pltpu.SemaphoreType.DMA((2,)),
            pltpu.SemaphoreType.DMA((5,)),
            pltpu.VMEM((STEP_TILES * PTS, LANES), jnp.float32),
            pltpu.VMEM((STEP_TILES * PTS, LANES), jnp.float32),
        ],
        compiler_params=pltpu.CompilerParams(vmem_limit_bytes=32 << 20),
        cost_estimate=pl.CostEstimate(flops=4_000_000_000, bytes_accessed=8_000_000, transcendentals=0),
        name="sample",
    )(
        slot, table_rows, volume, low, high, left, right, columns,
        jnp.asarray(y_bands()), jnp.asarray(table_bands()), jnp.asarray(smooth_matrix()), jnp.asarray(pack_matrix()),
    )

    arrived = lax.all_to_all(
        send.reshape(OWNERS, SEND_ROWS, PTS), ("wide", "narrow"), split_axis=0, concat_axis=0, tiled=True
    )

    responses = pl.pallas_call(
        response_kernel,
        grid=(SZ,),
        out_shape=jax.ShapeDtypeStruct((16, SZ, CY, NX), jnp.bfloat16),
        in_specs=[
            pl.BlockSpec(memory_space=pltpu.SMEM),
            pl.BlockSpec((2, CY, COMPS * NX), lambda z: (0, z, 0)),
            pl.BlockSpec((2, 3, NX, NX), lambda z: (0, 0, 0, 0)),
        ],
        out_specs=pl.BlockSpec((16, 1, CY, NX), lambda z: (0, z, 0, 0)),
        compiler_params=pltpu.CompilerParams(vmem_limit_bytes=16 << 20),
        cost_estimate=pl.CostEstimate(flops=200_000_000, bytes_accessed=4_000_000, transcendentals=0),
        name="respond",
    )(weights, fields, jnp.asarray(x_bands()))

    fibers = pl.pallas_call(
        mix_kernel,
        out_shape=jax.ShapeDtypeStruct((SLOTS * 16, PTS), jnp.bfloat16),
        in_specs=[vmem, vmem],
        out_specs=hbm,
        scratch_shapes=[pltpu.VMEM((SLOTS * 16, PTS), jnp.bfloat16), pltpu.SemaphoreType.DMA((MIX_PARTS,))],
        compiler_params=pltpu.CompilerParams(vmem_limit_bytes=16 << 20),
        cost_estimate=pl.CostEstimate(flops=1_600_000_000, bytes_accessed=4_000_000, transcendentals=0),
        name="mix",
    )(mix, arrived.reshape(OWNERS * SEND_ROWS, PTS))
    return responses, fibers.reshape(OWNERS, CAP, 16, PTS)


def solution(mesh):
    return jax.shard_map(
        per_device,
        mesh=mesh,
        in_specs=(
            P("wide", "narrow", None),
            P(),
            P(("wide", "narrow"), None),
            P(("wide", "narrow"), None),
        ),
        out_specs=(P(None, "wide", "narrow", None), P(("wide", "narrow"), None, None, None)),
        check_vma=False,
    )
```

```python
import jax
import jax.numpy as jnp
import ml_dtypes
import numpy as np
from jax import lax
from jax.experimental import pallas as pl
from jax.experimental.pallas import tpu as pltpu
from jax.sharding import PartitionSpec as P

TAPS_PER_SIDE = 3
SPACINGS = (1, 2)
CAP = 4
BORDER = 6
Y_PAD = 8
RESPONSE_GAIN = 6.0
SMOOTH_SIGMA = 4.0

SZ, CY, NX = 8, 64, 128
ROWS = SZ * CY
DEEP = SZ + 2 * BORDER
TALL = CY + 2 * Y_PAD
COMPS = 6
LANES = 128
TILES = 256
PTS = 128
STEP_TILES = 16
STEPS = TILES // STEP_TILES
GROUP = 4
OWNERS = 128
SLOTS = OWNERS * CAP
SEND_ROWS = CAP * 2 * COMPS
MIX_PARTS = 4

KINDS = ((2, 0, 0), (0, 2, 0), (0, 0, 2), (1, 1, 0), (1, 0, 1), (0, 1, 1))


def tap_table():
    offsets = np.arange(-TAPS_PER_SIDE, TAPS_PER_SIDE + 1).astype(np.float32)
    bell = np.exp(np.float32(-0.5) * offsets * offsets)
    normalized = bell / np.sum(bell)
    taps = np.stack([normalized, -offsets * normalized, (offsets * offsets - 1.0) * normalized])
    return taps.astype(ml_dtypes.bfloat16).astype(np.float32)


TAPS = tap_table()


def tap_values(distance, kind, spacing):
    total = jnp.zeros(distance.shape, jnp.float32)
    for tap in range(2 * TAPS_PER_SIDE + 1):
        if TAPS[kind, tap] != 0.0:
            hit = distance == (tap - TAPS_PER_SIDE) * spacing
            total = jnp.where(hit, float(TAPS[kind, tap]), total)
    return total


def index(shape, axis):
    return lax.broadcasted_iota(jnp.int32, shape, axis)


def fill_y_band(y_band):
    distance = index((CY, TALL), 0) + Y_PAD - index((CY, TALL), 1)
    for s in range(2):
        for kind in range(3):
            start = (s * 3 + kind) * CY
            y_band[start:start + CY, :] = tap_values(distance, kind, SPACINGS[s]).astype(jnp.bfloat16)


def fill_x_bands(bands):
    bands[...] = jnp.zeros_like(bands)
    column = index((48, LANES), 1)
    for s in range(2):
        local = (((column >> 6) ^ s) << 3) + ((column >> 3) & 7)
        distance = local + 16 - index((48, LANES), 0)
        taps = [tap_values(distance, kind, SPACINGS[s]) for kind in range(3)]
        for comp in range(COMPS):
            base = jnp.where((column & 7) == comp, taps[KINDS[comp][0]], 0.0).astype(jnp.bfloat16)
            for m in range(NX // 16):
                first, last = max(0, 16 * m - 16), min(NX, 16 * m + 32)
                skip = first - (16 * m - 16)
                bands[s, comp * NX + first:comp * NX + last, m * LANES:(m + 1) * LANES] = base[skip:skip + last - first]


def smooth_matrix():
    distance = (index((PTS, PTS), 1) - index((PTS, PTS), 0)).astype(jnp.float32)
    bell = jnp.exp(-distance * distance / (2.0 * SMOOTH_SIGMA * SMOOTH_SIGMA))
    return (bell / jnp.sum(bell, axis=0, keepdims=True)).astype(jnp.bfloat16)


def pack_matrix():
    shape = (4 * SEND_ROWS, 4 * CAP * 16)
    row = index(shape, 0)
    slot = (row * 43691) >> 19
    six = (row * 43691) >> 18
    source = slot * 16 + (six - 2 * slot) * 8 + (row - 6 * six)
    return jnp.where(source == index(shape, 1), 1.0, 0.0).astype(jnp.bfloat16)


def x_bands():
    result = np.zeros((2, 3, NX, NX), np.float32)
    for s in range(2):
        for kind in range(3):
            for tap in range(2 * TAPS_PER_SIDE + 1):
                result[s, kind] += TAPS[kind, tap] * np.eye(NX, k=(tap - TAPS_PER_SIDE) * SPACINGS[s], dtype=np.float32)
    return result.astype(ml_dtypes.bfloat16)


def z_pass(y_fields, s, kind_y, kinds_z, z):
    d = SPACINGS[s]
    planes = [y_fields[z + BORDER - k * d, s, kind_y] for k in range(-TAPS_PER_SIDE, TAPS_PER_SIDE + 1)]
    results = {}
    for kind in kinds_z:
        total = None
        for side in range(TAPS_PER_SIDE):
            pair = planes[side] - planes[6 - side] if kind == 1 else planes[side] + planes[6 - side]
            if TAPS[kind, side] == 0.0:
                continue
            term = float(TAPS[kind, side]) * pair
            total = term if total is None else total + term
        if kind != 1:
            total = total + float(TAPS[kind, TAPS_PER_SIDE]) * planes[TAPS_PER_SIDE]
        results[kind] = total
    return results


def sample_kernel(
    slot_ref, rows_ref, center_ref, left_ref, right_ref, column_ref, send_ref, fields_ref, ext, y_fields, bands, table, tiles,
    y_band, smoother, index_rows, sem
):
    def copy_rows(step, side):
        return pltpu.make_async_copy(
            rows_ref.at[pl.ds(pl.multiple_of(step * STEP_TILES, STEP_TILES), STEP_TILES)], index_rows[side], sem.at[side]
        )

    copy_rows(0, 0).start()
    copy_rows(1, 1).start()

    ext[:, Y_PAD:Y_PAD + CY, :] = center_ref[...]
    ext[:, 0:Y_PAD, :] = left_ref[...]
    ext[:, Y_PAD + CY:TALL, :] = right_ref[...]
    tiles[...] = jnp.zeros_like(tiles)
    fill_y_band(y_band)
    fill_x_bands(bands)
    smoother[...] = smooth_matrix()

    for z in range(0, DEEP, 2):
        pair = jnp.concatenate([ext[z], ext[z + 1]], axis=1)
        for s in range(2):
            out = jnp.dot(y_band[s * 3 * CY:(s + 1) * 3 * CY, :], pair, preferred_element_type=jnp.float32)
            for kind in range(3):
                y_fields[z, s, kind] = out[kind * CY:(kind + 1) * CY, 0:NX]
                y_fields[z + 1, s, kind] = out[kind * CY:(kind + 1) * CY, NX:2 * NX]

    for s in range(2):
        for z in range(SZ):
            passed = [z_pass(y_fields, s, 0, (0, 1, 2), z), z_pass(y_fields, s, 1, (0, 1), z), z_pass(y_fields, s, 2, (0,), z)]
            for comp, (_, kind_y, kind_z) in enumerate(KINDS):
                fields_ref[s, z * CY:(z + 1) * CY, comp * NX:(comp + 1) * NX] = passed[kind_y][kind_z].astype(jnp.bfloat16)

    lower = index((ROWS // 2, LANES), 1) < 64
    for m in range(0, NX // 16, 2):
        for part in range(0, ROWS, ROWS // 2):
            outs = [
                jnp.dot(
                    fields_ref[s, part:part + ROWS // 2, :], bands[s, :, m * LANES:(m + 2) * LANES],
                    preferred_element_type=jnp.float32,
                )
                for s in range(2)
            ]
            for half in range(2):
                first, second = (out[:, half * LANES:(half + 1) * LANES] for out in outs)
                start = 8 + (m + half) * 2 * ROWS + part
                table[start:start + ROWS // 2, :] = jnp.where(lower, first, second)
                table[start + ROWS:start + ROWS + ROWS // 2, :] = jnp.where(lower, second, first)

    eye = (index((LANES, LANES), 0) == index((LANES, LANES), 1)).astype(jnp.bfloat16)
    sublane = index((8, LANES), 0)

    def advance(step, side):
        copy_rows(0, side).wait()
        for group in range(STEP_TILES // GROUP):
            blocks = []
            for tile in range(group * GROUP, (group + 1) * GROUP):
                for p in range(0, PTS, 8):
                    merged = None
                    for k in range(8):
                        row = index_rows[side][tile, p + k]
                        loaded = table[pl.ds(row + (8 - k), 8), :]
                        merged = loaded if merged is None else jnp.where(sublane == k, loaded, merged)
                    blocks.append(merged)
            flat = jnp.concatenate(blocks, axis=0).astype(jnp.bfloat16)
            turned = lax.dot_general(eye, flat, (((1,), (1,)), ((), ())), preferred_element_type=jnp.float32)
            picked = []
            for t in range(GROUP):
                column = jnp.broadcast_to(column_ref[pl.ds(step * STEP_TILES + group * GROUP + t, 1), :], (8, PTS))
                here = turned[:, t * PTS:(t + 1) * PTS]
                both = [here[0:8], here[64:72]]
                for x in range(1, 16):
                    hit = column == x
                    for s in range(2):
                        start = ((x // 8) ^ s) * 64 + (x % 8) * 8
                        both[s] = jnp.where(hit, here[start:start + 8], both[s])
                picked.append(jnp.concatenate(both, axis=0).astype(jnp.bfloat16))
            smooth = jnp.dot(
                jnp.concatenate(picked, axis=0), smoother[...], preferred_element_type=jnp.float32
            ).astype(jnp.bfloat16)
            for t in range(GROUP):
                tiles[slot_ref[step * STEP_TILES + group * GROUP + t]] = smooth[t * 16:(t + 1) * 16]
        copy_rows(jnp.minimum(step + 2, STEPS - 1), side).start()

    @pl.loop(0, STEPS // 2)
    def _(i):
        advance(2 * i, 0)
        advance(2 * i + 1, 1)

    copy_rows(0, 0).wait()
    copy_rows(0, 1).wait()
    pack = pack_matrix()

    @pl.loop(0, OWNERS // 8)
    def _(oct):
        for quad in range(2):
            here = tiles[pl.ds(oct * 32 + quad * 16, 16)].reshape(256, PTS)
            packed = jnp.dot(pack, here, preferred_element_type=jnp.float32).astype(jnp.bfloat16)
            start = pl.multiple_of(oct * 8 * SEND_ROWS, 8 * SEND_ROWS) + quad * 4 * SEND_ROWS
            send_ref[pl.ds(start, 4 * SEND_ROWS), :] = packed


def response_kernel(weight_ref, fields_ref, x_band_ref, out_ref):
    for s in range(2):
        parts = [
            jnp.dot(
                fields_ref[s, :, comp * NX:(comp + 1) * NX], x_band_ref[s, KINDS[comp][0]], preferred_element_type=jnp.float32
            )
            for comp in range(COMPS)
        ]
        for o in range(8):
            total = parts[0] * weight_ref[o, 0]
            for comp in range(1, COMPS):
                total = total + parts[comp] * weight_ref[o, comp]
            out_ref[s * 8 + o, 0] = total.astype(jnp.bfloat16)


def mix_kernel(mix_ref, arrived_ref, out_hbm, out, sem):
    copies = []
    for part in range(MIX_PARTS):
        pairs = 16 // MIX_PARTS
        for pair in range(part * pairs, (part + 1) * pairs):
            first = arrived_ref[pair * 8 * SEND_ROWS:(pair * 8 + 4) * SEND_ROWS]
            second = arrived_ref[(pair * 8 + 4) * SEND_ROWS:(pair * 8 + 8) * SEND_ROWS]
            here = jnp.concatenate([first, second], axis=1)
            mixed = jnp.dot(mix_ref[0], here, preferred_element_type=jnp.float32)
            mixed = (mixed + jnp.dot(mix_ref[1], here, preferred_element_type=jnp.float32)).astype(jnp.bfloat16)
            out[pair * 512:pair * 512 + 256, :] = mixed[:, 0:PTS]
            out[pair * 512 + 256:pair * 512 + 512, :] = mixed[:, PTS:2 * PTS]
        rows = slice(part * pairs * 512, (part + 1) * pairs * 512)
        copy = pltpu.make_async_copy(out.at[rows, :], out_hbm.at[rows, :], sem.at[part])
        copy.start()
        copies.append(copy)
    for copy in copies:
        copy.wait()


def orientation_weights(angles):
    polar_angle = angles[0]
    azimuth = angles[1]
    dir_x = jnp.sin(polar_angle) * jnp.cos(azimuth)
    dir_y = jnp.sin(polar_angle) * jnp.sin(azimuth)
    dir_z = jnp.cos(polar_angle)
    return RESPONSE_GAIN * jnp.stack(
        [
            dir_x * dir_x,
            dir_y * dir_y,
            dir_z * dir_z,
            2.0 * dir_x * dir_y,
            2.0 * dir_x * dir_z,
            2.0 * dir_y * dir_z,
        ],
        axis=1,
    )


def shifted(value, axis, step):
    count = lax.axis_size(axis)
    forward = [(i, i + 1) for i in range(count - 1)]
    backward = [(i + 1, i) for i in range(count - 1)]
    return lax.ppermute(value, axis, forward if step > 0 else backward)


def mix_matrix(weights):
    scales = jnp.zeros((16, 12), jnp.float32)
    scales = scales.at[0:8, 0:6].set(weights).at[8:16, 6:12].set(weights)
    rows = lax.broadcasted_iota(jnp.int32, (256, 192), 0) // 16
    columns = lax.broadcasted_iota(jnp.int32, (256, 192), 1) // 12
    full = jnp.where(rows == columns, jnp.tile(scales, (16, 16)), 0.0)
    high = full.astype(jnp.bfloat16)
    low = (full - high.astype(jnp.float32)).astype(jnp.bfloat16)
    return jnp.stack([high, low])


def per_device(volume, angles, tile_points, tile_dest):
    low = shifted(volume[SZ - BORDER:], "wide", 1)
    high = shifted(volume[:BORDER], "wide", -1)
    edge_low = jnp.concatenate([part[:, CY - Y_PAD:] for part in (low, volume, high)], axis=0)
    edge_high = jnp.concatenate([part[:, :Y_PAD] for part in (low, volume, high)], axis=0)
    left = shifted(edge_low, "narrow", 1)
    right = shifted(edge_high, "narrow", -1)

    table_rows = ((tile_points >> 3) & 15) * ROWS + (tile_points >> 7)
    columns = tile_points & 15
    dest = tile_dest[:, 0]
    earlier = lax.broadcasted_iota(jnp.int32, (TILES, TILES), 0)
    later = lax.broadcasted_iota(jnp.int32, (TILES, TILES), 1)
    same_owner = (dest[:, None] == dest[None, :]) & (earlier < later)
    slot = dest * CAP + jnp.sum(same_owner.astype(jnp.int32), axis=0)
    center = jnp.concatenate([low, volume, high], axis=0)

    weights = orientation_weights(angles)
    mix = mix_matrix(weights)

    vmem = pl.BlockSpec(memory_space=pltpu.VMEM)
    hbm = pl.BlockSpec(memory_space=pltpu.HBM)
    send, fields = pl.pallas_call(
        sample_kernel,
        out_shape=(
            jax.ShapeDtypeStruct((OWNERS * SEND_ROWS, PTS), jnp.bfloat16),
            jax.ShapeDtypeStruct((2, ROWS, COMPS * NX), jnp.bfloat16),
        ),
        in_specs=[pl.BlockSpec(memory_space=pltpu.SMEM)] + [vmem] * 5,
        out_specs=(vmem, vmem),
        scratch_shapes=[
            pltpu.VMEM((DEEP, TALL, NX), jnp.bfloat16),
            pltpu.VMEM((DEEP, 2, 3, CY, NX), jnp.float32),
            pltpu.VMEM((2, COMPS * NX, NX * 8), jnp.bfloat16),
            pltpu.VMEM((NX // 8 * ROWS + 16, LANES), jnp.float32),
            pltpu.VMEM((SLOTS, 16, PTS), jnp.bfloat16),
            pltpu.VMEM((6 * CY, TALL), jnp.bfloat16),
            pltpu.VMEM((PTS, PTS), jnp.bfloat16),
            [pltpu.SMEM((STEP_TILES, PTS), jnp.int32)] * 2,
            pltpu.SemaphoreType.DMA((2,)),
        ],
        compiler_params=pltpu.CompilerParams(vmem_limit_bytes=32 << 20),
        cost_estimate=pl.CostEstimate(flops=4_000_000_000, bytes_accessed=8_000_000, transcendentals=0),
        name="sample",
    )(
        slot, table_rows, center, left, right, columns,
    )

    arrived = lax.all_to_all(
        send.reshape(OWNERS, SEND_ROWS, PTS), ("wide", "narrow"), split_axis=0, concat_axis=0, tiled=True
    )

    responses = pl.pallas_call(
        response_kernel,
        grid=(SZ,),
        out_shape=jax.ShapeDtypeStruct((16, SZ, CY, NX), jnp.bfloat16),
        in_specs=[
            pl.BlockSpec(memory_space=pltpu.SMEM),
            pl.BlockSpec((2, CY, COMPS * NX), lambda z: (0, z, 0)),
            pl.BlockSpec((2, 3, NX, NX), lambda z: (0, 0, 0, 0)),
        ],
        out_specs=pl.BlockSpec((16, 1, CY, NX), lambda z: (0, z, 0, 0)),
        compiler_params=pltpu.CompilerParams(vmem_limit_bytes=16 << 20),
        cost_estimate=pl.CostEstimate(flops=200_000_000, bytes_accessed=4_000_000, transcendentals=0),
        name="respond",
    )(weights, fields, jnp.asarray(x_bands()))

    fibers = pl.pallas_call(
        mix_kernel,
        out_shape=jax.ShapeDtypeStruct((SLOTS * 16, PTS), jnp.bfloat16),
        in_specs=[vmem, vmem],
        out_specs=hbm,
        scratch_shapes=[pltpu.VMEM((SLOTS * 16, PTS), jnp.bfloat16), pltpu.SemaphoreType.DMA((MIX_PARTS,))],
        compiler_params=pltpu.CompilerParams(vmem_limit_bytes=16 << 20),
        cost_estimate=pl.CostEstimate(flops=1_600_000_000, bytes_accessed=4_000_000, transcendentals=0),
        name="mix",
    )(mix, arrived.reshape(OWNERS * SEND_ROWS, PTS))
    return responses, fibers.reshape(OWNERS, CAP, 16, PTS)


def solution(mesh):
    return jax.shard_map(
        per_device,
        mesh=mesh,
        in_specs=(
            P("wide", "narrow", None),
            P(),
            P(("wide", "narrow"), None),
            P(("wide", "narrow"), None),
        ),
        out_specs=(P(None, "wide", "narrow", None), P(("wide", "narrow"), None, None, None)),
        check_vma=False,
    )
```

```python
import jax
import jax.numpy as jnp
import ml_dtypes
import numpy as np
from jax import lax
from jax.experimental import pallas as pl
from jax.experimental.pallas import tpu as pltpu
from jax.sharding import PartitionSpec as P

TAPS_PER_SIDE = 3
SPACINGS = (1, 2)
CAP = 4
BORDER = 6
Y_PAD = 8
RESPONSE_GAIN = 6.0
SMOOTH_SIGMA = 4.0

SZ, CY, NX = 8, 64, 128
ROWS = SZ * CY
DEEP = SZ + 2 * BORDER
TALL = CY + 2 * Y_PAD
COMPS = 6
LANES = 128
TILES = 256
PTS = 128
STEP_TILES = 32
STEPS = TILES // STEP_TILES
GROUP = 4
PART = 512
PACK_PARTS = 4
OWNERS = 128
SLOTS = OWNERS * CAP
SEND_ROWS = CAP * 2 * COMPS
MIX_PARTS = 4

KINDS = ((2, 0, 0), (0, 2, 0), (0, 0, 2), (1, 1, 0), (1, 0, 1), (0, 1, 1))


def tap_table():
    offsets = np.arange(-TAPS_PER_SIDE, TAPS_PER_SIDE + 1).astype(np.float32)
    bell = np.exp(np.float32(-0.5) * offsets * offsets)
    normalized = bell / np.sum(bell)
    taps = np.stack([normalized, -offsets * normalized, (offsets * offsets - 1.0) * normalized])
    return taps.astype(ml_dtypes.bfloat16).astype(np.float32)


TAPS = tap_table()


def tap_values(distance, kind, spacing):
    total = jnp.zeros(distance.shape, jnp.float32)
    for tap in range(2 * TAPS_PER_SIDE + 1):
        if TAPS[kind, tap] != 0.0:
            hit = distance == (tap - TAPS_PER_SIDE) * spacing
            total = jnp.where(hit, float(TAPS[kind, tap]), total)
    return total


def index(shape, axis):
    return lax.broadcasted_iota(jnp.int32, shape, axis)


def fill_y_band(y_band):
    distance = index((CY, TALL), 0) + Y_PAD - index((CY, TALL), 1)
    for s in range(2):
        for kind in range(3):
            start = (s * 3 + kind) * CY
            y_band[start:start + CY, :] = tap_values(distance, kind, SPACINGS[s]).astype(jnp.bfloat16)


def fill_x_bands(bands):
    bands[...] = jnp.zeros_like(bands)
    column = index((48, LANES), 1)
    for s in range(2):
        local = (((column >> 6) ^ s) << 3) + ((column >> 3) & 7)
        distance = local + 16 - index((48, LANES), 0)
        taps = [tap_values(distance, kind, SPACINGS[s]) for kind in range(3)]
        for comp in range(COMPS):
            base = jnp.where((column & 7) == comp, taps[KINDS[comp][0]], 0.0).astype(jnp.bfloat16)
            for m in range(NX // 16):
                first, last = max(0, 16 * m - 16), min(NX, 16 * m + 32)
                skip = first - (16 * m - 16)
                bands[s, comp * NX + first:comp * NX + last, m * LANES:(m + 1) * LANES] = base[skip:skip + last - first]


def smooth_matrix():
    distance = (index((PTS, PTS), 1) - index((PTS, PTS), 0)).astype(jnp.float32)
    bell = jnp.exp(-distance * distance / (2.0 * SMOOTH_SIGMA * SMOOTH_SIGMA))
    return (bell / jnp.sum(bell, axis=0, keepdims=True)).astype(jnp.bfloat16)


def pack_matrix():
    shape = (4 * SEND_ROWS, 4 * CAP * 16)
    row = index(shape, 0)
    slot = (row * 43691) >> 19
    six = (row * 43691) >> 18
    source = slot * 16 + (six - 2 * slot) * 8 + (row - 6 * six)
    return jnp.where(source == index(shape, 1), 1.0, 0.0).astype(jnp.bfloat16)


def x_bands():
    result = np.zeros((2, 3, NX, NX), np.float32)
    for s in range(2):
        for kind in range(3):
            for tap in range(2 * TAPS_PER_SIDE + 1):
                result[s, kind] += TAPS[kind, tap] * np.eye(NX, k=(tap - TAPS_PER_SIDE) * SPACINGS[s], dtype=np.float32)
    return result.astype(ml_dtypes.bfloat16)


def z_pass(planes, s, kinds, z):
    d = SPACINGS[s]
    results = {}
    for kind in kinds:
        total = None
        for side in range(TAPS_PER_SIDE):
            if TAPS[kind, side] == 0.0:
                continue
            shift = (side - TAPS_PER_SIDE) * d
            near, far = planes[z + BORDER - shift], planes[z + BORDER + shift]
            term = float(TAPS[kind, side]) * (near - far if kind == 1 else near + far)
            total = term if total is None else total + term
        if kind != 1:
            total = total + float(TAPS[kind, TAPS_PER_SIDE]) * planes[z + BORDER]
        results[kind] = total
    return results


def sample_kernel(
    slot_ref, rows_ref, center_ref, first_ref, second_ref, column_ref, send_hbm, fields_ref, ext, y_fields, bands, table, tiles,
    y_band, smoother, send, index_rows, sem, send_sem
):
    def copy_rows(step, side):
        return pltpu.make_async_copy(
            rows_ref.at[pl.ds(pl.multiple_of(step * STEP_TILES, STEP_TILES), STEP_TILES)], index_rows[side], sem.at[side]
        )

    copy_rows(0, 0).start()
    copy_rows(1, 1).start()

    ext[:, Y_PAD:Y_PAD + CY, :] = center_ref[...]
    even = (lax.axis_index("narrow") & 1) == 0
    ext[:, 0:Y_PAD, :] = jnp.where(even, second_ref[...], first_ref[...])
    ext[:, Y_PAD + CY:TALL, :] = jnp.where(even, first_ref[...], second_ref[...])
    tiles[...] = jnp.zeros_like(tiles)
    fill_y_band(y_band)
    fill_x_bands(bands)
    smoother[...] = smooth_matrix()

    for z in range(0, DEEP, 2):
        pair = jnp.concatenate([ext[z], ext[z + 1]], axis=1)
        for s in range(2):
            out = jnp.dot(y_band[s * 3 * CY:(s + 1) * 3 * CY, :], pair, preferred_element_type=jnp.float32)
            for kind in range(3):
                y_fields[z, s, kind] = out[kind * CY:(kind + 1) * CY, 0:NX]
                y_fields[z + 1, s, kind] = out[kind * CY:(kind + 1) * CY, NX:2 * NX]

    for s in range(2):
        for y in range(0, CY, 8):
            for kind_y, kinds_z in ((0, (0, 1, 2)), (1, (0, 1)), (2, (0,))):
                planes = [y_fields[z, s, kind_y, y:y + 8, :] for z in range(DEEP)]
                for z in range(SZ):
                    passed = z_pass(planes, s, kinds_z, z)
                    for comp, (_, comp_y, comp_z) in enumerate(KINDS):
                        if comp_y == kind_y:
                            fields_ref[s, z * CY + y:z * CY + y + 8, comp * NX:(comp + 1) * NX] = (
                                passed[comp_z].astype(jnp.bfloat16)
                            )

    lower = index((PART, LANES), 1) < 64
    for m in range(0, NX // 16, 2):
        for part in range(0, ROWS, PART):
            outs = [
                jnp.dot(
                    fields_ref[s, part:part + PART, :], bands[s, :, m * LANES:(m + 2) * LANES],
                    preferred_element_type=jnp.float32,
                )
                for s in range(2)
            ]
            for half in range(2):
                first, second = (out[:, half * LANES:(half + 1) * LANES] for out in outs)
                start = 8 + (m + half) * 2 * ROWS + part
                table[start:start + PART, :] = jnp.where(lower, first, second)
                table[start + ROWS:start + ROWS + PART, :] = jnp.where(lower, second, first)

    eye = (index((LANES, LANES), 0) == index((LANES, LANES), 1)).astype(jnp.bfloat16)
    sublane = index((8, LANES), 0)

    def advance(step, side):
        copy_rows(0, side).wait()
        for group in range(STEP_TILES // GROUP):
            blocks = []
            for tile in range(group * GROUP, (group + 1) * GROUP):
                for p in range(0, PTS, 8):
                    merged = None
                    for k in range(8):
                        row = index_rows[side][tile, p + k]
                        loaded = table[pl.ds(row + (8 - k), 8), :]
                        merged = loaded if merged is None else jnp.where(sublane == k, loaded, merged)
                    blocks.append(merged)
            flat = jnp.concatenate(blocks, axis=0).astype(jnp.bfloat16)
            turned = lax.dot_general(eye, flat, (((1,), (1,)), ((), ())), preferred_element_type=jnp.float32)
            picked = []
            for t in range(GROUP):
                column = jnp.broadcast_to(column_ref[pl.ds(step * STEP_TILES + group * GROUP + t, 1), :], (8, PTS))
                here = turned[:, t * PTS:(t + 1) * PTS]
                both = [here[0:8], here[64:72]]
                for x in range(1, 16):
                    hit = column == x
                    for s in range(2):
                        start = ((x // 8) ^ s) * 64 + (x % 8) * 8
                        both[s] = jnp.where(hit, here[start:start + 8], both[s])
                picked.append(jnp.concatenate(both, axis=0).astype(jnp.bfloat16))
            smooth = jnp.dot(
                jnp.concatenate(picked, axis=0), smoother[...], preferred_element_type=jnp.float32
            ).astype(jnp.bfloat16)
            for t in range(GROUP):
                tiles[slot_ref[step * STEP_TILES + group * GROUP + t]] = smooth[t * 16:(t + 1) * 16]
        copy_rows(jnp.minimum(step + 2, STEPS - 1), side).start()

    @pl.loop(0, STEPS // 2)
    def _(i):
        advance(2 * i, 0)
        advance(2 * i + 1, 1)

    copy_rows(0, 0).wait()
    copy_rows(0, 1).wait()
    pack = pack_matrix()
    rows = SEND_ROWS * OWNERS // PACK_PARTS
    copies = []
    for part in range(PACK_PARTS):
        for pair in range(part * 16 // PACK_PARTS, (part + 1) * 16 // PACK_PARTS):
            quads = [tiles[pair * 32 + quad * 16:pair * 32 + (quad + 1) * 16].reshape(256, PTS) for quad in range(2)]
            packed = jnp.dot(pack, jnp.concatenate(quads, axis=1), preferred_element_type=jnp.float32).astype(jnp.bfloat16)
            for quad in range(2):
                start = (pair * 2 + quad) * 4 * SEND_ROWS
                send[start:start + 4 * SEND_ROWS, :] = packed[:, quad * PTS:(quad + 1) * PTS]
        here = slice(part * rows, (part + 1) * rows)
        copy = pltpu.make_async_copy(send.at[here, :], send_hbm.at[here, :], send_sem.at[part])
        copy.start()
        copies.append(copy)
    for copy in copies:
        copy.wait()


def response_kernel(weight_ref, fields_ref, x_band_ref, out_ref):
    for s in range(2):
        parts = [
            jnp.dot(
                fields_ref[s, :, comp * NX:(comp + 1) * NX], x_band_ref[s, KINDS[comp][0]], preferred_element_type=jnp.float32
            )
            for comp in range(COMPS)
        ]
        for o in range(8):
            total = parts[0] * weight_ref[o, 0]
            for comp in range(1, COMPS):
                total = total + parts[comp] * weight_ref[o, comp]
            out_ref[s * 8 + o, 0] = total.astype(jnp.bfloat16)


def mix_kernel(mix_ref, arrived_ref, out_hbm, out, sem):
    copies = []
    for part in range(MIX_PARTS):
        pairs = 16 // MIX_PARTS
        for pair in range(part * pairs, (part + 1) * pairs):
            first = arrived_ref[pair * 8 * SEND_ROWS:(pair * 8 + 4) * SEND_ROWS]
            second = arrived_ref[(pair * 8 + 4) * SEND_ROWS:(pair * 8 + 8) * SEND_ROWS]
            here = jnp.concatenate([first, second], axis=1)
            mixed = jnp.dot(mix_ref[0], here, preferred_element_type=jnp.float32)
            mixed = (mixed + jnp.dot(mix_ref[1], here, preferred_element_type=jnp.float32)).astype(jnp.bfloat16)
            out[pair * 512:pair * 512 + 256, :] = mixed[:, 0:PTS]
            out[pair * 512 + 256:pair * 512 + 512, :] = mixed[:, PTS:2 * PTS]
        rows = slice(part * pairs * 512, (part + 1) * pairs * 512)
        copy = pltpu.make_async_copy(out.at[rows, :], out_hbm.at[rows, :], sem.at[part])
        copy.start()
        copies.append(copy)
    for copy in copies:
        copy.wait()


def orientation_weights(angles):
    polar_angle = angles[0]
    azimuth = angles[1]
    dir_x = jnp.sin(polar_angle) * jnp.cos(azimuth)
    dir_y = jnp.sin(polar_angle) * jnp.sin(azimuth)
    dir_z = jnp.cos(polar_angle)
    return RESPONSE_GAIN * jnp.stack(
        [
            dir_x * dir_x,
            dir_y * dir_y,
            dir_z * dir_z,
            2.0 * dir_x * dir_y,
            2.0 * dir_x * dir_z,
            2.0 * dir_y * dir_z,
        ],
        axis=1,
    )


def swap(value, axis, first):
    pairs = []
    for i in range(first, lax.axis_size(axis) - 1, 2):
        pairs += [(i, i + 1), (i + 1, i)]
    return lax.ppermute(value, axis, pairs)


def mix_matrix(weights):
    scales = jnp.zeros((16, 12), jnp.float32)
    scales = scales.at[0:8, 0:6].set(weights).at[8:16, 6:12].set(weights)
    rows = lax.broadcasted_iota(jnp.int32, (256, 192), 0) // 16
    columns = lax.broadcasted_iota(jnp.int32, (256, 192), 1) // 12
    full = jnp.where(rows == columns, jnp.tile(scales, (16, 16)), 0.0)
    high = full.astype(jnp.bfloat16)
    low = (full - high.astype(jnp.float32)).astype(jnp.bfloat16)
    return jnp.stack([high, low])


def per_device(volume, angles, tile_points, tile_dest):
    even_wide = (lax.axis_index("wide") & 1) == 0
    even_narrow = (lax.axis_index("narrow") & 1) == 0
    first, second = swap(volume, "wide", 0), swap(volume, "wide", 1)
    low = jnp.where(even_wide, second, first)[SZ - BORDER:]
    high = jnp.where(even_wide, first, second)[:BORDER]
    center = jnp.concatenate([low, volume, high], axis=0)
    edge_low, edge_high = center[:, :Y_PAD], center[:, CY - Y_PAD:]
    side_first = swap(jnp.where(even_narrow, edge_high, edge_low), "narrow", 0)
    side_second = swap(jnp.where(even_narrow, edge_low, edge_high), "narrow", 1)

    table_rows = ((tile_points >> 3) & 15) * ROWS + (tile_points >> 7)
    columns = tile_points & 15
    dest = tile_dest[:, 0]
    earlier = lax.broadcasted_iota(jnp.int32, (TILES, TILES), 0)
    later = lax.broadcasted_iota(jnp.int32, (TILES, TILES), 1)
    same_owner = (dest[:, None] == dest[None, :]) & (earlier < later)
    slot = dest * CAP + jnp.sum(same_owner.astype(jnp.int32), axis=0)

    weights = orientation_weights(angles)
    mix = mix_matrix(weights)

    vmem = pl.BlockSpec(memory_space=pltpu.VMEM)
    hbm = pl.BlockSpec(memory_space=pltpu.HBM)
    send, fields = pl.pallas_call(
        sample_kernel,
        out_shape=(
            jax.ShapeDtypeStruct((OWNERS * SEND_ROWS, PTS), jnp.bfloat16),
            jax.ShapeDtypeStruct((2, ROWS, COMPS * NX), jnp.bfloat16),
        ),
        in_specs=[pl.BlockSpec(memory_space=pltpu.SMEM)] + [vmem] * 5,
        out_specs=(hbm, vmem),
        scratch_shapes=[
            pltpu.VMEM((DEEP, TALL, NX), jnp.bfloat16),
            pltpu.VMEM((DEEP, 2, 3, CY, NX), jnp.float32),
            pltpu.VMEM((2, COMPS * NX, NX * 8), jnp.bfloat16),
            pltpu.VMEM((NX // 8 * ROWS + 16, LANES), jnp.float32),
            pltpu.VMEM((SLOTS, 16, PTS), jnp.bfloat16),
            pltpu.VMEM((6 * CY, TALL), jnp.bfloat16),
            pltpu.VMEM((PTS, PTS), jnp.bfloat16),
            pltpu.VMEM((OWNERS * SEND_ROWS, PTS), jnp.bfloat16),
            [pltpu.SMEM((STEP_TILES, PTS), jnp.int32)] * 2,
            pltpu.SemaphoreType.DMA((2,)),
            pltpu.SemaphoreType.DMA((PACK_PARTS,)),
        ],
        compiler_params=pltpu.CompilerParams(vmem_limit_bytes=32 << 20),
        cost_estimate=pl.CostEstimate(flops=4_000_000_000, bytes_accessed=8_000_000, transcendentals=0),
        name="sample",
    )(
        slot, table_rows, center, side_first, side_second, columns,
    )

    arrived = lax.all_to_all(
        send.reshape(OWNERS, SEND_ROWS, PTS), ("wide", "narrow"), split_axis=0, concat_axis=0, tiled=True
    )

    responses = pl.pallas_call(
        response_kernel,
        grid=(SZ,),
        out_shape=jax.ShapeDtypeStruct((16, SZ, CY, NX), jnp.bfloat16),
        in_specs=[
            pl.BlockSpec(memory_space=pltpu.SMEM),
            pl.BlockSpec((2, CY, COMPS * NX), lambda z: (0, z, 0)),
            pl.BlockSpec((2, 3, NX, NX), lambda z: (0, 0, 0, 0)),
        ],
        out_specs=pl.BlockSpec((16, 1, CY, NX), lambda z: (0, z, 0, 0)),
        compiler_params=pltpu.CompilerParams(vmem_limit_bytes=16 << 20),
        cost_estimate=pl.CostEstimate(flops=200_000_000, bytes_accessed=4_000_000, transcendentals=0),
        name="respond",
    )(weights, fields, jnp.asarray(x_bands()))

    fibers = pl.pallas_call(
        mix_kernel,
        out_shape=jax.ShapeDtypeStruct((SLOTS * 16, PTS), jnp.bfloat16),
        in_specs=[vmem, vmem],
        out_specs=hbm,
        scratch_shapes=[pltpu.VMEM((SLOTS * 16, PTS), jnp.bfloat16), pltpu.SemaphoreType.DMA((MIX_PARTS,))],
        compiler_params=pltpu.CompilerParams(vmem_limit_bytes=16 << 20),
        cost_estimate=pl.CostEstimate(flops=1_600_000_000, bytes_accessed=4_000_000, transcendentals=0),
        name="mix",
    )(mix, arrived.reshape(OWNERS * SEND_ROWS, PTS))
    return responses, fibers.reshape(OWNERS, CAP, 16, PTS)


def solution(mesh):
    return jax.shard_map(
        per_device,
        mesh=mesh,
        in_specs=(
            P("wide", "narrow", None),
            P(),
            P(("wide", "narrow"), None),
            P(("wide", "narrow"), None),
        ),
        out_specs=(P(None, "wide", "narrow", None), P(("wide", "narrow"), None, None, None)),
        check_vma=False,
    )
```

```python
import jax
import jax.numpy as jnp
import ml_dtypes
import numpy as np
from jax import lax
from jax.experimental import pallas as pl
from jax.experimental.pallas import tpu as pltpu
from jax.sharding import PartitionSpec as P

TAPS_PER_SIDE = 3
SPACINGS = (1, 2)
CAP = 4
BORDER = 6
Y_PAD = 8
RESPONSE_GAIN = 6.0
SMOOTH_SIGMA = 4.0

SZ, CY, NX = 8, 64, 128
ROWS = SZ * CY
DEEP = SZ + 2 * BORDER
TALL = CY + 2 * Y_PAD
COMPS = 6
LANES = 128
TILES = 256
PTS = 128
STEP_TILES = 32
STEPS = TILES // STEP_TILES
GROUP = 4
PART = 512
PACK_PARTS = 4
OWNERS = 128
SLOTS = OWNERS * CAP
SEND_ROWS = CAP * 2 * COMPS
MIX_PARTS = 4

KINDS = ((2, 0, 0), (0, 2, 0), (0, 0, 2), (1, 1, 0), (1, 0, 1), (0, 1, 1))


def tap_table():
    offsets = np.arange(-TAPS_PER_SIDE, TAPS_PER_SIDE + 1).astype(np.float32)
    bell = np.exp(np.float32(-0.5) * offsets * offsets)
    normalized = bell / np.sum(bell)
    taps = np.stack([normalized, -offsets * normalized, (offsets * offsets - 1.0) * normalized])
    return taps.astype(ml_dtypes.bfloat16).astype(np.float32)


TAPS = tap_table()


def tap_values(distance, kind, spacing):
    total = jnp.zeros(distance.shape, jnp.float32)
    for tap in range(2 * TAPS_PER_SIDE + 1):
        if TAPS[kind, tap] != 0.0:
            hit = distance == (tap - TAPS_PER_SIDE) * spacing
            total = jnp.where(hit, float(TAPS[kind, tap]), total)
    return total


def index(shape, axis):
    return lax.broadcasted_iota(jnp.int32, shape, axis)


def fill_y_band(y_band):
    distance = index((CY, TALL), 0) + Y_PAD - index((CY, TALL), 1)
    for s in range(2):
        for kind in range(3):
            start = (s * 3 + kind) * CY
            y_band[start:start + CY, :] = tap_values(distance, kind, SPACINGS[s]).astype(jnp.bfloat16)


def fill_x_bands(bands):
    bands[...] = jnp.zeros_like(bands)
    column = index((48, LANES), 1)
    for s in range(2):
        local = (((column >> 6) ^ s) << 3) + ((column >> 3) & 7)
        distance = local + 16 - index((48, LANES), 0)
        taps = [tap_values(distance, kind, SPACINGS[s]) for kind in range(3)]
        for comp in range(COMPS):
            base = jnp.where((column & 7) == comp, taps[KINDS[comp][0]], 0.0).astype(jnp.bfloat16)
            for m in range(NX // 16):
                first, last = max(0, 16 * m - 16), min(NX, 16 * m + 32)
                skip = first - (16 * m - 16)
                bands[s, m, comp * NX + first:comp * NX + last, :] = base[skip:skip + last - first]


def smooth_matrix():
    distance = (index((PTS, PTS), 1) - index((PTS, PTS), 0)).astype(jnp.float32)
    bell = jnp.exp(-distance * distance / (2.0 * SMOOTH_SIGMA * SMOOTH_SIGMA))
    return (bell / jnp.sum(bell, axis=0, keepdims=True)).astype(jnp.bfloat16)


def pack_matrix():
    shape = (4 * SEND_ROWS, 4 * CAP * 16)
    row = index(shape, 0)
    slot = (row * 43691) >> 19
    six = (row * 43691) >> 18
    source = slot * 16 + (six - 2 * slot) * 8 + (row - 6 * six)
    return jnp.where(source == index(shape, 1), 1.0, 0.0).astype(jnp.bfloat16)


def x_bands():
    result = np.zeros((2, 3, NX, NX), np.float32)
    for s in range(2):
        for kind in range(3):
            for tap in range(2 * TAPS_PER_SIDE + 1):
                result[s, kind] += TAPS[kind, tap] * np.eye(NX, k=(tap - TAPS_PER_SIDE) * SPACINGS[s], dtype=np.float32)
    return result.astype(ml_dtypes.bfloat16)


def z_pass(planes, s, kinds, z):
    d = SPACINGS[s]
    results = {}
    for kind in kinds:
        total = None
        for side in range(TAPS_PER_SIDE):
            if TAPS[kind, side] == 0.0:
                continue
            shift = (side - TAPS_PER_SIDE) * d
            near, far = planes[z + BORDER - shift], planes[z + BORDER + shift]
            term = float(TAPS[kind, side]) * (near - far if kind == 1 else near + far)
            total = term if total is None else total + term
        if kind != 1:
            total = total + float(TAPS[kind, TAPS_PER_SIDE]) * planes[z + BORDER]
        results[kind] = total
    return results


def sample_kernel(
    slot_ref, rows_ref, center_ref, first_ref, second_ref, column_ref, send_hbm, fields_ref, ext, y_fields, bands, table, tiles,
    y_band, smoother, send, index_rows, sem, send_sem
):
    def copy_rows(step, side):
        return pltpu.make_async_copy(
            rows_ref.at[pl.ds(pl.multiple_of(step * STEP_TILES, STEP_TILES), STEP_TILES)], index_rows[side], sem.at[side]
        )

    copy_rows(0, 0).start()
    copy_rows(1, 1).start()

    ext[:, Y_PAD:Y_PAD + CY, :] = center_ref[...]
    even = (lax.axis_index("narrow") & 1) == 0
    ext[:, 0:Y_PAD, :] = jnp.where(even, second_ref[...], first_ref[...])
    ext[:, Y_PAD + CY:TALL, :] = jnp.where(even, first_ref[...], second_ref[...])
    tiles[...] = jnp.zeros_like(tiles)
    fill_y_band(y_band)
    fill_x_bands(bands)
    smoother[...] = smooth_matrix()

    for z in range(0, DEEP, 2):
        pair = jnp.concatenate([ext[z], ext[z + 1]], axis=1)
        for s in range(2):
            out = jnp.dot(y_band[s * 3 * CY:(s + 1) * 3 * CY, :], pair, preferred_element_type=jnp.float32)
            for kind in range(3):
                y_fields[z, s, kind] = out[kind * CY:(kind + 1) * CY, 0:NX]
                y_fields[z + 1, s, kind] = out[kind * CY:(kind + 1) * CY, NX:2 * NX]

    @pl.loop(0, CY // 8)
    def _(block):
        y = pl.multiple_of(block * 8, 8)
        for s in range(2):
            for kind_y, kinds_z in ((0, (0, 1, 2)), (1, (0, 1)), (2, (0,))):
                planes = [y_fields[z, s, kind_y, pl.ds(y, 8), :] for z in range(DEEP)]
                for z in range(SZ):
                    passed = z_pass(planes, s, kinds_z, z)
                    for comp, (_, comp_y, comp_z) in enumerate(KINDS):
                        if comp_y == kind_y:
                            fields_ref[s, comp, pl.ds(z * CY + y, 8), :] = passed[comp_z].astype(jnp.bfloat16)

    lower = index((PART, LANES), 1) < 64
    for m in range(0, NX // 16, 2):
        for part in range(0, ROWS, PART):
            outs = [
                jnp.dot(
                    jnp.concatenate([fields_ref[s, comp, part:part + PART, :] for comp in range(COMPS)], axis=1),
                    jnp.concatenate([bands[s, m], bands[s, m + 1]], axis=1),
                    preferred_element_type=jnp.float32,
                )
                for s in range(2)
            ]
            for half in range(2):
                first, second = (out[:, half * LANES:(half + 1) * LANES] for out in outs)
                start = 8 + (m + half) * 2 * ROWS + part
                table[start:start + PART, :] = jnp.where(lower, first, second)
                table[start + ROWS:start + ROWS + PART, :] = jnp.where(lower, second, first)

    eye = (index((LANES, LANES), 0) == index((LANES, LANES), 1)).astype(jnp.bfloat16)
    sublane = index((8, LANES), 0)

    def advance(step, side):
        copy_rows(0, side).wait()
        for group in range(STEP_TILES // GROUP):
            blocks = []
            for tile in range(group * GROUP, (group + 1) * GROUP):
                for p in range(0, PTS, 8):
                    merged = None
                    for k in range(8):
                        row = index_rows[side][tile, p + k]
                        loaded = table[pl.ds(row + (8 - k), 8), :]
                        merged = loaded if merged is None else jnp.where(sublane == k, loaded, merged)
                    blocks.append(merged)
            flat = jnp.concatenate(blocks, axis=0).astype(jnp.bfloat16)
            turned = lax.dot_general(eye, flat, (((1,), (1,)), ((), ())), preferred_element_type=jnp.float32)
            picked = []
            for t in range(GROUP):
                column = jnp.broadcast_to(column_ref[pl.ds(step * STEP_TILES + group * GROUP + t, 1), :], (8, PTS))
                here = turned[:, t * PTS:(t + 1) * PTS]
                both = [here[0:8], here[64:72]]
                for x in range(1, 16):
                    hit = column == x
                    for s in range(2):
                        start = ((x // 8) ^ s) * 64 + (x % 8) * 8
                        both[s] = jnp.where(hit, here[start:start + 8], both[s])
                picked.append(jnp.concatenate(both, axis=0).astype(jnp.bfloat16))
            smooth = jnp.dot(
                jnp.concatenate(picked, axis=0), smoother[...], preferred_element_type=jnp.float32
            ).astype(jnp.bfloat16)
            for t in range(GROUP):
                tiles[slot_ref[step * STEP_TILES + group * GROUP + t]] = smooth[t * 16:(t + 1) * 16]
        copy_rows(jnp.minimum(step + 2, STEPS - 1), side).start()

    @pl.loop(0, STEPS // 2)
    def _(i):
        advance(2 * i, 0)
        advance(2 * i + 1, 1)

    copy_rows(0, 0).wait()
    copy_rows(0, 1).wait()
    pack = pack_matrix()
    rows = SEND_ROWS * OWNERS // PACK_PARTS
    copies = []
    for part in range(PACK_PARTS):
        for pair in range(part * 16 // PACK_PARTS, (part + 1) * 16 // PACK_PARTS):
            quads = [tiles[pair * 32 + quad * 16:pair * 32 + (quad + 1) * 16].reshape(256, PTS) for quad in range(2)]
            packed = jnp.dot(pack, jnp.concatenate(quads, axis=1), preferred_element_type=jnp.float32).astype(jnp.bfloat16)
            for quad in range(2):
                start = (pair * 2 + quad) * 4 * SEND_ROWS
                send[start:start + 4 * SEND_ROWS, :] = packed[:, quad * PTS:(quad + 1) * PTS]
        here = slice(part * rows, (part + 1) * rows)
        copy = pltpu.make_async_copy(send.at[here, :], send_hbm.at[here, :], send_sem.at[part])
        copy.start()
        copies.append(copy)
    for copy in copies:
        copy.wait()


def response_kernel(weight_ref, fields_ref, x_band_ref, out_ref):
    for s in range(2):
        parts = [
            jnp.dot(
                fields_ref[s, comp], x_band_ref[s, KINDS[comp][0]], preferred_element_type=jnp.float32
            )
            for comp in range(COMPS)
        ]
        for o in range(8):
            total = parts[0] * weight_ref[o, 0]
            for comp in range(1, COMPS):
                total = total + parts[comp] * weight_ref[o, comp]
            out_ref[s * 8 + o, 0] = total.astype(jnp.bfloat16)


def mix_kernel(mix_ref, arrived_ref, out_hbm, out, sem):
    copies = []
    for part in range(MIX_PARTS):
        pairs = 16 // MIX_PARTS
        for pair in range(part * pairs, (part + 1) * pairs):
            first = arrived_ref[pair * 8 * SEND_ROWS:(pair * 8 + 4) * SEND_ROWS]
            second = arrived_ref[(pair * 8 + 4) * SEND_ROWS:(pair * 8 + 8) * SEND_ROWS]
            here = jnp.concatenate([first, second], axis=1)
            mixed = jnp.dot(mix_ref[0], here, preferred_element_type=jnp.float32)
            mixed = (mixed + jnp.dot(mix_ref[1], here, preferred_element_type=jnp.float32)).astype(jnp.bfloat16)
            out[pair * 512:pair * 512 + 256, :] = mixed[:, 0:PTS]
            out[pair * 512 + 256:pair * 512 + 512, :] = mixed[:, PTS:2 * PTS]
        rows = slice(part * pairs * 512, (part + 1) * pairs * 512)
        copy = pltpu.make_async_copy(out.at[rows, :], out_hbm.at[rows, :], sem.at[part])
        copy.start()
        copies.append(copy)
    for copy in copies:
        copy.wait()


def orientation_weights(angles):
    polar_angle = angles[0]
    azimuth = angles[1]
    dir_x = jnp.sin(polar_angle) * jnp.cos(azimuth)
    dir_y = jnp.sin(polar_angle) * jnp.sin(azimuth)
    dir_z = jnp.cos(polar_angle)
    return RESPONSE_GAIN * jnp.stack(
        [
            dir_x * dir_x,
            dir_y * dir_y,
            dir_z * dir_z,
            2.0 * dir_x * dir_y,
            2.0 * dir_x * dir_z,
            2.0 * dir_y * dir_z,
        ],
        axis=1,
    )


def swap(value, axis, first):
    pairs = []
    for i in range(first, lax.axis_size(axis) - 1, 2):
        pairs += [(i, i + 1), (i + 1, i)]
    return lax.ppermute(value, axis, pairs)


def mix_matrix(weights):
    scales = jnp.zeros((16, 12), jnp.float32)
    scales = scales.at[0:8, 0:6].set(weights).at[8:16, 6:12].set(weights)
    rows = lax.broadcasted_iota(jnp.int32, (256, 192), 0) // 16
    columns = lax.broadcasted_iota(jnp.int32, (256, 192), 1) // 12
    full = jnp.where(rows == columns, jnp.tile(scales, (16, 16)), 0.0)
    high = full.astype(jnp.bfloat16)
    low = (full - high.astype(jnp.float32)).astype(jnp.bfloat16)
    return jnp.stack([high, low])


def per_device(volume, angles, tile_points, tile_dest):
    even_wide = (lax.axis_index("wide") & 1) == 0
    even_narrow = (lax.axis_index("narrow") & 1) == 0
    first, second = swap(volume, "wide", 0), swap(volume, "wide", 1)
    def extended(rows):
        below, above = first[:, rows], second[:, rows]
        low = jnp.where(even_wide, above, below)[SZ - BORDER:]
        high = jnp.where(even_wide, below, above)[:BORDER]
        return jnp.concatenate([low, volume[:, rows], high], axis=0)

    edge_low, edge_high = extended(slice(0, Y_PAD)), extended(slice(CY - Y_PAD, CY))
    side_first = swap(jnp.where(even_narrow, edge_high, edge_low), "narrow", 0)
    side_second = swap(jnp.where(even_narrow, edge_low, edge_high), "narrow", 1)
    first, second, side_first = lax.optimization_barrier((first, second, side_first))
    center = extended(slice(0, CY))

    table_rows = ((tile_points >> 3) & 15) * ROWS + (tile_points >> 7)
    columns = tile_points & 15
    dest = tile_dest[:, 0]
    earlier = lax.broadcasted_iota(jnp.int32, (TILES, TILES), 0)
    later = lax.broadcasted_iota(jnp.int32, (TILES, TILES), 1)
    same_owner = (dest[:, None] == dest[None, :]) & (earlier < later)
    slot = dest * CAP + jnp.sum(same_owner.astype(jnp.int32), axis=0)

    weights = orientation_weights(angles)
    mix = mix_matrix(weights)

    vmem = pl.BlockSpec(memory_space=pltpu.VMEM)
    hbm = pl.BlockSpec(memory_space=pltpu.HBM)
    send, fields = pl.pallas_call(
        sample_kernel,
        out_shape=(
            jax.ShapeDtypeStruct((OWNERS * SEND_ROWS, PTS), jnp.bfloat16),
            jax.ShapeDtypeStruct((2, COMPS, ROWS, NX), jnp.bfloat16),
        ),
        in_specs=[pl.BlockSpec(memory_space=pltpu.SMEM)] + [vmem] * 5,
        out_specs=(hbm, vmem),
        scratch_shapes=[
            pltpu.VMEM((DEEP, TALL, NX), jnp.bfloat16),
            pltpu.VMEM((DEEP, 2, 3, CY, NX), jnp.float32),
            pltpu.VMEM((2, NX // 16, COMPS * NX, LANES), jnp.bfloat16),
            pltpu.VMEM((NX // 8 * ROWS + 16, LANES), jnp.float32),
            pltpu.VMEM((SLOTS, 16, PTS), jnp.bfloat16),
            pltpu.VMEM((6 * CY, TALL), jnp.bfloat16),
            pltpu.VMEM((PTS, PTS), jnp.bfloat16),
            pltpu.VMEM((OWNERS * SEND_ROWS, PTS), jnp.bfloat16),
            [pltpu.SMEM((STEP_TILES, PTS), jnp.int32)] * 2,
            pltpu.SemaphoreType.DMA((2,)),
            pltpu.SemaphoreType.DMA((PACK_PARTS,)),
        ],
        compiler_params=pltpu.CompilerParams(vmem_limit_bytes=32 << 20),
        cost_estimate=pl.CostEstimate(flops=4_000_000_000, bytes_accessed=8_000_000, transcendentals=0),
        name="sample",
    )(
        slot, table_rows, center, side_first, side_second, columns,
    )

    arrived = lax.all_to_all(
        send.reshape(OWNERS, SEND_ROWS, PTS), ("wide", "narrow"), split_axis=0, concat_axis=0, tiled=True
    )

    responses = pl.pallas_call(
        response_kernel,
        grid=(SZ,),
        out_shape=jax.ShapeDtypeStruct((16, SZ, CY, NX), jnp.bfloat16),
        in_specs=[
            pl.BlockSpec(memory_space=pltpu.SMEM),
            pl.BlockSpec((2, COMPS, CY, NX), lambda z: (0, 0, z, 0)),
            pl.BlockSpec((2, 3, NX, NX), lambda z: (0, 0, 0, 0)),
        ],
        out_specs=pl.BlockSpec((16, 1, CY, NX), lambda z: (0, z, 0, 0)),
        compiler_params=pltpu.CompilerParams(vmem_limit_bytes=16 << 20),
        cost_estimate=pl.CostEstimate(flops=200_000_000, bytes_accessed=4_000_000, transcendentals=0),
        name="respond",
    )(weights, fields, jnp.asarray(x_bands()))

    fibers = pl.pallas_call(
        mix_kernel,
        out_shape=jax.ShapeDtypeStruct((SLOTS * 16, PTS), jnp.bfloat16),
        in_specs=[vmem, vmem],
        out_specs=hbm,
        scratch_shapes=[pltpu.VMEM((SLOTS * 16, PTS), jnp.bfloat16), pltpu.SemaphoreType.DMA((MIX_PARTS,))],
        compiler_params=pltpu.CompilerParams(vmem_limit_bytes=16 << 20),
        cost_estimate=pl.CostEstimate(flops=1_600_000_000, bytes_accessed=4_000_000, transcendentals=0),
        name="mix",
    )(mix, arrived.reshape(OWNERS * SEND_ROWS, PTS))
    return responses, fibers.reshape(OWNERS, CAP, 16, PTS)


def solution(mesh):
    return jax.shard_map(
        per_device,
        mesh=mesh,
        in_specs=(
            P("wide", "narrow", None),
            P(),
            P(("wide", "narrow"), None),
            P(("wide", "narrow"), None),
        ),
        out_specs=(P(None, "wide", "narrow", None), P(("wide", "narrow"), None, None, None)),
        check_vma=False,
    )
```

```python
import jax
import jax.numpy as jnp
import ml_dtypes
import numpy as np
from jax import lax
from jax.experimental import pallas as pl
from jax.experimental.pallas import tpu as pltpu
from jax.sharding import PartitionSpec as P

TAPS_PER_SIDE = 3
SPACINGS = (1, 2)
CAP = 4
BORDER = 6
Y_PAD = 8
RESPONSE_GAIN = 6.0
SMOOTH_SIGMA = 4.0

SZ, CY, NX = 8, 64, 128
ROWS = SZ * CY
DEEP = SZ + 2 * BORDER
TALL = CY + 2 * Y_PAD
COMPS = 6
LANES = 128
TILES = 256
PTS = 128
STEP_TILES = 32
STEPS = TILES // STEP_TILES
GROUP = 4
PART = 512
PACK_PARTS = 4
OWNERS = 128
SLOTS = OWNERS * CAP
SEND_ROWS = CAP * 2 * COMPS
MIX_PARTS = 4

KINDS = ((2, 0, 0), (0, 2, 0), (0, 0, 2), (1, 1, 0), (1, 0, 1), (0, 1, 1))


def tap_table():
    offsets = np.arange(-TAPS_PER_SIDE, TAPS_PER_SIDE + 1).astype(np.float32)
    bell = np.exp(np.float32(-0.5) * offsets * offsets)
    normalized = bell / np.sum(bell)
    taps = np.stack([normalized, -offsets * normalized, (offsets * offsets - 1.0) * normalized])
    return taps.astype(ml_dtypes.bfloat16).astype(np.float32)


TAPS = tap_table()


def tap_values(distance, kind, spacing):
    total = jnp.zeros(distance.shape, jnp.float32)
    for tap in range(2 * TAPS_PER_SIDE + 1):
        if TAPS[kind, tap] != 0.0:
            hit = distance == (tap - TAPS_PER_SIDE) * spacing
            total = jnp.where(hit, float(TAPS[kind, tap]), total)
    return total


def index(shape, axis):
    return lax.broadcasted_iota(jnp.int32, shape, axis)


def fill_y_band(y_band):
    distance = index((CY, TALL), 0) + Y_PAD - index((CY, TALL), 1)
    for s in range(2):
        for kind in range(3):
            start = (s * 3 + kind) * CY
            y_band[start:start + CY, :] = tap_values(distance, kind, SPACINGS[s]).astype(jnp.bfloat16)


def fill_x_bands(bands):
    bands[...] = jnp.zeros_like(bands)
    column = index((48, LANES), 1)
    for s in range(2):
        local = (((column >> 6) ^ s) << 3) + ((column >> 3) & 7)
        distance = local + 16 - index((48, LANES), 0)
        taps = [tap_values(distance, kind, SPACINGS[s]) for kind in range(3)]
        for comp in range(COMPS):
            base = jnp.where((column & 7) == comp, taps[KINDS[comp][0]], 0.0).astype(jnp.bfloat16)
            for m in range(NX // 16):
                first, last = max(0, 16 * m - 16), min(NX, 16 * m + 32)
                skip = first - (16 * m - 16)
                bands[s, comp * NX + first:comp * NX + last, m * LANES:(m + 1) * LANES] = base[skip:skip + last - first]


def smooth_matrix():
    distance = (index((PTS, PTS), 1) - index((PTS, PTS), 0)).astype(jnp.float32)
    bell = jnp.exp(-distance * distance / (2.0 * SMOOTH_SIGMA * SMOOTH_SIGMA))
    return (bell / jnp.sum(bell, axis=0, keepdims=True)).astype(jnp.bfloat16)


def pack_matrix():
    shape = (4 * SEND_ROWS, 4 * CAP * 16)
    row = index(shape, 0)
    slot = (row * 43691) >> 19
    six = (row * 43691) >> 18
    source = slot * 16 + (six - 2 * slot) * 8 + (row - 6 * six)
    return jnp.where(source == index(shape, 1), 1.0, 0.0).astype(jnp.bfloat16)


def x_bands():
    result = np.zeros((2, 3, NX, NX), np.float32)
    for s in range(2):
        for kind in range(3):
            for tap in range(2 * TAPS_PER_SIDE + 1):
                result[s, kind] += TAPS[kind, tap] * np.eye(NX, k=(tap - TAPS_PER_SIDE) * SPACINGS[s], dtype=np.float32)
    return result.astype(ml_dtypes.bfloat16)


def tile_slots(dest):
    owner = jnp.broadcast_to(dest.astype(jnp.float32), (TILES, TILES))
    other, tile = index((TILES, TILES), 0), index((TILES, TILES), 1)
    turned = jnp.sum(jnp.where(other == tile, owner, 0.0), axis=1, keepdims=True)
    rank = jnp.sum(jnp.where((turned == owner) & (other < tile), 1.0, 0.0), axis=0, keepdims=True)
    return dest * CAP + rank.astype(jnp.int32)


def z_pass(planes, s, kinds, z):
    d = SPACINGS[s]
    results = {}
    for kind in kinds:
        total = None
        for side in range(TAPS_PER_SIDE):
            if TAPS[kind, side] == 0.0:
                continue
            shift = (side - TAPS_PER_SIDE) * d
            near, far = planes[z + BORDER - shift], planes[z + BORDER + shift]
            term = float(TAPS[kind, side]) * (near - far if kind == 1 else near + far)
            total = term if total is None else total + term
        if kind != 1:
            total = total + float(TAPS[kind, TAPS_PER_SIDE]) * planes[z + BORDER]
        results[kind] = total
    return results


def sample_kernel(
    dest_ref, points_ref, block_ref, first_ref, second_ref, side_first_ref, side_second_ref, send_hbm, fields_ref, ext, y_fields, bands, table, tiles,
    y_band, smoother, send, rows_ref, slots, slot_ref, index_rows, sem, send_sem, slot_sem
):
    def copy_rows(step, side):
        return pltpu.make_async_copy(
            rows_ref.at[pl.ds(pl.multiple_of(step * STEP_TILES, STEP_TILES), STEP_TILES)], index_rows[side], sem.at[side]
        )

    points = points_ref[...]
    rows_ref[...] = ((points >> 3) & 15) * ROWS + (points >> 7)
    copy_rows(0, 0).start()
    copy_rows(1, 1).start()
    slots[...] = tile_slots(dest_ref[...])
    slot_copy = pltpu.make_async_copy(slots, slot_ref, slot_sem)
    slot_copy.start()

    inner = slice(Y_PAD, Y_PAD + CY)
    even = (lax.axis_index("wide") & 1) == 0
    ext[BORDER:BORDER + SZ, inner, :] = block_ref[...]
    ext[0:BORDER, inner, :] = jnp.where(even, second_ref[SZ - BORDER:], first_ref[SZ - BORDER:])
    ext[BORDER + SZ:DEEP, inner, :] = jnp.where(even, first_ref[:BORDER], second_ref[:BORDER])
    even = (lax.axis_index("narrow") & 1) == 0
    ext[:, 0:Y_PAD, :] = jnp.where(even, side_second_ref[...], side_first_ref[...])
    ext[:, Y_PAD + CY:TALL, :] = jnp.where(even, side_first_ref[...], side_second_ref[...])
    tiles[...] = jnp.zeros_like(tiles)
    fill_y_band(y_band)
    fill_x_bands(bands)
    smoother[...] = smooth_matrix()

    for z in range(0, DEEP, 2):
        pair = jnp.concatenate([ext[z], ext[z + 1]], axis=1)
        for s in range(2):
            out = jnp.dot(y_band[s * 3 * CY:(s + 1) * 3 * CY, :], pair, preferred_element_type=jnp.float32)
            for kind in range(3):
                y_fields[z, s, kind] = out[kind * CY:(kind + 1) * CY, 0:NX]
                y_fields[z + 1, s, kind] = out[kind * CY:(kind + 1) * CY, NX:2 * NX]

    for s in range(2):
        for y in range(0, CY, 8):
            for kind_y, kinds_z in ((0, (0, 1, 2)), (1, (0, 1)), (2, (0,))):
                planes = [y_fields[z, s, kind_y, y:y + 8, :] for z in range(DEEP)]
                for z in range(SZ):
                    passed = z_pass(planes, s, kinds_z, z)
                    for comp, (_, comp_y, comp_z) in enumerate(KINDS):
                        if comp_y == kind_y:
                            fields_ref[s, z * CY + y:z * CY + y + 8, comp * NX:(comp + 1) * NX] = (
                                passed[comp_z].astype(jnp.bfloat16)
                            )

    lower = index((PART, LANES), 1) < 64
    for m in range(0, NX // 16, 2):
        for part in range(0, ROWS, PART):
            outs = [
                jnp.dot(
                    fields_ref[s, part:part + PART, :], bands[s, :, m * LANES:(m + 2) * LANES],
                    preferred_element_type=jnp.float32,
                )
                for s in range(2)
            ]
            for half in range(2):
                first, second = (out[:, half * LANES:(half + 1) * LANES] for out in outs)
                start = 8 + (m + half) * 2 * ROWS + part
                table[start:start + PART, :] = jnp.where(lower, first, second)
                table[start + ROWS:start + ROWS + PART, :] = jnp.where(lower, second, first)

    eye = (index((LANES, LANES), 0) == index((LANES, LANES), 1)).astype(jnp.bfloat16)
    sublane = index((8, LANES), 0)
    slot_copy.wait()

    def advance(step, side):
        copy_rows(0, side).wait()
        for group in range(STEP_TILES // GROUP):
            blocks = []
            for tile in range(group * GROUP, (group + 1) * GROUP):
                for p in range(0, PTS, 8):
                    merged = None
                    for k in range(8):
                        row = index_rows[side][tile, p + k]
                        loaded = table[pl.ds(row + (8 - k), 8), :]
                        merged = loaded if merged is None else jnp.where(sublane == k, loaded, merged)
                    blocks.append(merged)
            flat = jnp.concatenate(blocks, axis=0).astype(jnp.bfloat16)
            turned = lax.dot_general(eye, flat, (((1,), (1,)), ((), ())), preferred_element_type=jnp.float32)
            picked = []
            for t in range(GROUP):
                column = jnp.broadcast_to(points_ref[pl.ds(step * STEP_TILES + group * GROUP + t, 1), :] & 15, (8, PTS))
                here = turned[:, t * PTS:(t + 1) * PTS]
                both = [here[0:8], here[64:72]]
                for x in range(1, 16):
                    hit = column == x
                    for s in range(2):
                        start = ((x // 8) ^ s) * 64 + (x % 8) * 8
                        both[s] = jnp.where(hit, here[start:start + 8], both[s])
                picked.append(jnp.concatenate(both, axis=0).astype(jnp.bfloat16))
            smooth = jnp.dot(
                jnp.concatenate(picked, axis=0), smoother[...], preferred_element_type=jnp.float32
            ).astype(jnp.bfloat16)
            for t in range(GROUP):
                tiles[slot_ref[0, step * STEP_TILES + group * GROUP + t]] = smooth[t * 16:(t + 1) * 16]
        copy_rows(jnp.minimum(step + 2, STEPS - 1), side).start()

    @pl.loop(0, STEPS // 2)
    def _(i):
        advance(2 * i, 0)
        advance(2 * i + 1, 1)

    copy_rows(0, 0).wait()
    copy_rows(0, 1).wait()
    pack = pack_matrix()
    rows = SEND_ROWS * OWNERS // PACK_PARTS
    copies = []
    for part in range(PACK_PARTS):
        for pair in range(part * 16 // PACK_PARTS, (part + 1) * 16 // PACK_PARTS):
            quads = [tiles[pair * 32 + quad * 16:pair * 32 + (quad + 1) * 16].reshape(256, PTS) for quad in range(2)]
            packed = jnp.dot(pack, jnp.concatenate(quads, axis=1), preferred_element_type=jnp.float32).astype(jnp.bfloat16)
            for quad in range(2):
                start = (pair * 2 + quad) * 4 * SEND_ROWS
                send[start:start + 4 * SEND_ROWS, :] = packed[:, quad * PTS:(quad + 1) * PTS]
        here = slice(part * rows, (part + 1) * rows)
        copy = pltpu.make_async_copy(send.at[here, :], send_hbm.at[here, :], send_sem.at[part])
        copy.start()
        copies.append(copy)
    for copy in copies:
        copy.wait()


def response_kernel(weight_ref, fields_ref, x_band_ref, out_ref):
    for s in range(2):
        parts = [
            jnp.dot(
                fields_ref[s, :, comp * NX:(comp + 1) * NX], x_band_ref[s, KINDS[comp][0]], preferred_element_type=jnp.float32
            )
            for comp in range(COMPS)
        ]
        for o in range(8):
            total = parts[0] * weight_ref[o, 0]
            for comp in range(1, COMPS):
                total = total + parts[comp] * weight_ref[o, comp]
            out_ref[s * 8 + o, 0] = total.astype(jnp.bfloat16)


def mix_kernel(mix_ref, arrived_ref, out_hbm, out, sem):
    copies = []
    for part in range(MIX_PARTS):
        pairs = 16 // MIX_PARTS
        for pair in range(part * pairs, (part + 1) * pairs):
            first = arrived_ref[pair * 8 * SEND_ROWS:(pair * 8 + 4) * SEND_ROWS]
            second = arrived_ref[(pair * 8 + 4) * SEND_ROWS:(pair * 8 + 8) * SEND_ROWS]
            here = jnp.concatenate([first, second], axis=1)
            mixed = jnp.dot(mix_ref[0], here, preferred_element_type=jnp.float32)
            mixed = (mixed + jnp.dot(mix_ref[1], here, preferred_element_type=jnp.float32)).astype(jnp.bfloat16)
            out[pair * 512:pair * 512 + 256, :] = mixed[:, 0:PTS]
            out[pair * 512 + 256:pair * 512 + 512, :] = mixed[:, PTS:2 * PTS]
        rows = slice(part * pairs * 512, (part + 1) * pairs * 512)
        copy = pltpu.make_async_copy(out.at[rows, :], out_hbm.at[rows, :], sem.at[part])
        copy.start()
        copies.append(copy)
    for copy in copies:
        copy.wait()


def orientation_weights(angles):
    polar_angle = angles[0]
    azimuth = angles[1]
    dir_x = jnp.sin(polar_angle) * jnp.cos(azimuth)
    dir_y = jnp.sin(polar_angle) * jnp.sin(azimuth)
    dir_z = jnp.cos(polar_angle)
    return RESPONSE_GAIN * jnp.stack(
        [
            dir_x * dir_x,
            dir_y * dir_y,
            dir_z * dir_z,
            2.0 * dir_x * dir_y,
            2.0 * dir_x * dir_z,
            2.0 * dir_y * dir_z,
        ],
        axis=1,
    )


def swap(value, axis, first):
    pairs = []
    for i in range(first, lax.axis_size(axis) - 1, 2):
        pairs += [(i, i + 1), (i + 1, i)]
    return lax.ppermute(value, axis, pairs)


def mix_matrix(weights):
    scales = jnp.zeros((16, 12), jnp.float32)
    scales = scales.at[0:8, 0:6].set(weights).at[8:16, 6:12].set(weights)
    rows = lax.broadcasted_iota(jnp.int32, (256, 192), 0) // 16
    columns = lax.broadcasted_iota(jnp.int32, (256, 192), 1) // 12
    full = jnp.where(rows == columns, jnp.tile(scales, (16, 16)), 0.0)
    high = full.astype(jnp.bfloat16)
    low = (full - high.astype(jnp.float32)).astype(jnp.bfloat16)
    return jnp.stack([high, low])


def per_device(volume, angles, tile_points, tile_dest):
    even_wide = (lax.axis_index("wide") & 1) == 0
    even_narrow = (lax.axis_index("narrow") & 1) == 0
    first, second = swap(volume, "wide", 0), swap(volume, "wide", 1)
    def extended(rows):
        below, above = first[:, rows], second[:, rows]
        low = jnp.where(even_wide, above, below)[SZ - BORDER:]
        high = jnp.where(even_wide, below, above)[:BORDER]
        return jnp.concatenate([low, volume[:, rows], high], axis=0)

    edge_low, edge_high = extended(slice(0, Y_PAD)), extended(slice(CY - Y_PAD, CY))
    side_first = swap(jnp.where(even_narrow, edge_high, edge_low), "narrow", 0)
    side_second = swap(jnp.where(even_narrow, edge_low, edge_high), "narrow", 1)
    weights = orientation_weights(angles)
    mix = mix_matrix(weights)

    vmem = pl.BlockSpec(memory_space=pltpu.VMEM)
    hbm = pl.BlockSpec(memory_space=pltpu.HBM)
    send, fields = pl.pallas_call(
        sample_kernel,
        out_shape=(
            jax.ShapeDtypeStruct((OWNERS * SEND_ROWS, PTS), jnp.bfloat16),
            jax.ShapeDtypeStruct((2, ROWS, COMPS * NX), jnp.bfloat16),
        ),
        in_specs=[vmem] * 7,
        out_specs=(hbm, vmem),
        scratch_shapes=[
            pltpu.VMEM((DEEP, TALL, NX), jnp.bfloat16),
            pltpu.VMEM((DEEP, 2, 3, CY, NX), jnp.float32),
            pltpu.VMEM((2, COMPS * NX, NX * 8), jnp.bfloat16),
            pltpu.VMEM((NX // 8 * ROWS + 16, LANES), jnp.float32),
            pltpu.VMEM((SLOTS, 16, PTS), jnp.bfloat16),
            pltpu.VMEM((6 * CY, TALL), jnp.bfloat16),
            pltpu.VMEM((PTS, PTS), jnp.bfloat16),
            pltpu.VMEM((OWNERS * SEND_ROWS, PTS), jnp.bfloat16),
            pltpu.VMEM((TILES, PTS), jnp.int32),
            pltpu.VMEM((1, TILES), jnp.int32),
            pltpu.SMEM((1, TILES), jnp.int32),
            [pltpu.SMEM((STEP_TILES, PTS), jnp.int32)] * 2,
            pltpu.SemaphoreType.DMA((2,)),
            pltpu.SemaphoreType.DMA((PACK_PARTS,)),
            pltpu.SemaphoreType.DMA,
        ],
        compiler_params=pltpu.CompilerParams(vmem_limit_bytes=32 << 20),
        cost_estimate=pl.CostEstimate(flops=4_000_000_000, bytes_accessed=8_000_000, transcendentals=0),
        name="sample",
    )(
        tile_dest.reshape(1, TILES), tile_points, volume, first, second, side_first, side_second,
    )

    arrived = lax.all_to_all(
        send.reshape(OWNERS, SEND_ROWS, PTS), ("wide", "narrow"), split_axis=0, concat_axis=0, tiled=True
    )

    responses = pl.pallas_call(
        response_kernel,
        grid=(SZ,),
        out_shape=jax.ShapeDtypeStruct((16, SZ, CY, NX), jnp.bfloat16),
        in_specs=[
            pl.BlockSpec(memory_space=pltpu.SMEM),
            pl.BlockSpec((2, CY, COMPS * NX), lambda z: (0, z, 0)),
            pl.BlockSpec((2, 3, NX, NX), lambda z: (0, 0, 0, 0)),
        ],
        out_specs=pl.BlockSpec((16, 1, CY, NX), lambda z: (0, z, 0, 0)),
        compiler_params=pltpu.CompilerParams(vmem_limit_bytes=16 << 20),
        cost_estimate=pl.CostEstimate(flops=200_000_000, bytes_accessed=4_000_000, transcendentals=0),
        name="respond",
    )(weights, fields, jnp.asarray(x_bands()))

    fibers = pl.pallas_call(
        mix_kernel,
        out_shape=jax.ShapeDtypeStruct((SLOTS * 16, PTS), jnp.bfloat16),
        in_specs=[vmem, vmem],
        out_specs=hbm,
        scratch_shapes=[pltpu.VMEM((SLOTS * 16, PTS), jnp.bfloat16), pltpu.SemaphoreType.DMA((MIX_PARTS,))],
        compiler_params=pltpu.CompilerParams(vmem_limit_bytes=16 << 20),
        cost_estimate=pl.CostEstimate(flops=1_600_000_000, bytes_accessed=4_000_000, transcendentals=0),
        name="mix",
    )(mix, arrived.reshape(OWNERS * SEND_ROWS, PTS))
    return responses, fibers.reshape(OWNERS, CAP, 16, PTS)


def solution(mesh):
    return jax.shard_map(
        per_device,
        mesh=mesh,
        in_specs=(
            P("wide", "narrow", None),
            P(),
            P(("wide", "narrow"), None),
            P(("wide", "narrow"), None),
        ),
        out_specs=(P(None, "wide", "narrow", None), P(("wide", "narrow"), None, None, None)),
        check_vma=False,
    )
```

```python
import jax
import jax.numpy as jnp
import ml_dtypes
import numpy as np
from jax import lax
from jax.experimental import pallas as pl
from jax.experimental.pallas import tpu as pltpu
from jax.sharding import PartitionSpec as P

TAPS_PER_SIDE = 3
SPACINGS = (1, 2)
CAP = 4
BORDER = 6
Y_PAD = 8
RESPONSE_GAIN = 6.0
SMOOTH_SIGMA = 4.0

SZ, CY, NX = 8, 64, 128
ROWS = SZ * CY
DEEP = SZ + 2 * BORDER
TALL = CY + 2 * Y_PAD
COMPS = 6
LANES = 128
TILES = 256
PTS = 128
STEP_TILES = 32
STEPS = TILES // STEP_TILES
GROUP = 4
PART = 512
PACK_PARTS = 4
OWNERS = 128
SLOTS = OWNERS * CAP
SEND_ROWS = CAP * 2 * COMPS
MIX_PARTS = 4

KINDS = ((2, 0, 0), (0, 2, 0), (0, 0, 2), (1, 1, 0), (1, 0, 1), (0, 1, 1))


def tap_table():
    offsets = np.arange(-TAPS_PER_SIDE, TAPS_PER_SIDE + 1).astype(np.float32)
    bell = np.exp(np.float32(-0.5) * offsets * offsets)
    normalized = bell / np.sum(bell)
    taps = np.stack([normalized, -offsets * normalized, (offsets * offsets - 1.0) * normalized])
    return taps.astype(ml_dtypes.bfloat16).astype(np.float32)


TAPS = tap_table()


def tap_values(distance, kind, spacing):
    total = jnp.zeros(distance.shape, jnp.float32)
    for tap in range(2 * TAPS_PER_SIDE + 1):
        if TAPS[kind, tap] != 0.0:
            hit = distance == (tap - TAPS_PER_SIDE) * spacing
            total = jnp.where(hit, float(TAPS[kind, tap]), total)
    return total


def index(shape, axis):
    return lax.broadcasted_iota(jnp.int32, shape, axis)


def fill_y_band(y_band):
    distance = index((CY, TALL), 0) + Y_PAD - index((CY, TALL), 1)
    for s in range(2):
        for kind in range(3):
            start = (s * 3 + kind) * CY
            y_band[start:start + CY, :] = tap_values(distance, kind, SPACINGS[s]).astype(jnp.bfloat16)


def fill_x_bands(bands):
    bands[...] = jnp.zeros_like(bands)
    column = index((48, LANES), 1)
    for s in range(2):
        local = (((column >> 6) ^ s) << 3) + ((column >> 3) & 7)
        distance = local + 16 - index((48, LANES), 0)
        taps = [tap_values(distance, kind, SPACINGS[s]) for kind in range(3)]
        for comp in range(COMPS):
            base = jnp.where((column & 7) == comp, taps[KINDS[comp][0]], 0.0).astype(jnp.bfloat16)
            for m in range(NX // 16):
                first, last = max(0, 16 * m - 16), min(NX, 16 * m + 32)
                skip = first - (16 * m - 16)
                bands[s, comp * NX + first:comp * NX + last, m * LANES:(m + 1) * LANES] = base[skip:skip + last - first]


def smooth_matrix():
    distance = (index((PTS, PTS), 1) - index((PTS, PTS), 0)).astype(jnp.float32)
    bell = jnp.exp(-distance * distance / (2.0 * SMOOTH_SIGMA * SMOOTH_SIGMA))
    return (bell / jnp.sum(bell, axis=0, keepdims=True)).astype(jnp.bfloat16)


def pack_matrix():
    shape = (4 * SEND_ROWS, 4 * CAP * 16)
    row = index(shape, 0)
    slot = (row * 43691) >> 19
    six = (row * 43691) >> 18
    source = slot * 16 + (six - 2 * slot) * 8 + (row - 6 * six)
    return jnp.where(source == index(shape, 1), 1.0, 0.0).astype(jnp.bfloat16)


def x_bands():
    result = np.zeros((2, 3, NX, NX), np.float32)
    for s in range(2):
        for kind in range(3):
            for tap in range(2 * TAPS_PER_SIDE + 1):
                result[s, kind] += TAPS[kind, tap] * np.eye(NX, k=(tap - TAPS_PER_SIDE) * SPACINGS[s], dtype=np.float32)
    return result.astype(ml_dtypes.bfloat16)


def tile_slots(dest):
    owner = jnp.broadcast_to(dest.astype(jnp.float32), (TILES, TILES))
    other, tile = index((TILES, TILES), 0), index((TILES, TILES), 1)
    turned = jnp.sum(jnp.where(other == tile, owner, 0.0), axis=1, keepdims=True)
    rank = jnp.sum(jnp.where((turned == owner) & (other < tile), 1.0, 0.0), axis=0, keepdims=True)
    return dest * CAP + rank.astype(jnp.int32)


def z_pass(planes, s, kinds, z):
    d = SPACINGS[s]
    results = {}
    for kind in kinds:
        total = None
        for side in range(TAPS_PER_SIDE):
            if TAPS[kind, side] == 0.0:
                continue
            shift = (side - TAPS_PER_SIDE) * d
            near, far = planes[z + BORDER - shift], planes[z + BORDER + shift]
            term = float(TAPS[kind, side]) * (near - far if kind == 1 else near + far)
            total = term if total is None else total + term
        if kind != 1:
            total = total + float(TAPS[kind, TAPS_PER_SIDE]) * planes[z + BORDER]
        results[kind] = total
    return results


def sample_kernel(
    dest_ref, points_ref, center_ref, first_ref, second_ref, send_hbm, fields_ref, ext, y_fields, bands, table, tiles,
    y_band, smoother, send, rows_ref, slots, slot_ref, index_rows, sem, send_sem, slot_sem
):
    def copy_rows(step, side):
        return pltpu.make_async_copy(
            rows_ref.at[pl.ds(pl.multiple_of(step * STEP_TILES, STEP_TILES), STEP_TILES)], index_rows[side], sem.at[side]
        )

    points = points_ref[...]
    rows_ref[...] = ((points >> 3) & 15) * ROWS + (points >> 7)
    copy_rows(0, 0).start()
    copy_rows(1, 1).start()
    slots[...] = tile_slots(dest_ref[...])
    slot_copy = pltpu.make_async_copy(slots, slot_ref, slot_sem)
    slot_copy.start()

    ext[:, Y_PAD:Y_PAD + CY, :] = center_ref[...]
    even = (lax.axis_index("narrow") & 1) == 0
    ext[:, 0:Y_PAD, :] = jnp.where(even, second_ref[...], first_ref[...])
    ext[:, Y_PAD + CY:TALL, :] = jnp.where(even, first_ref[...], second_ref[...])
    tiles[...] = jnp.zeros_like(tiles)
    fill_y_band(y_band)
    fill_x_bands(bands)
    smoother[...] = smooth_matrix()

    for z in range(0, DEEP, 2):
        pair = jnp.concatenate([ext[z], ext[z + 1]], axis=1)
        for s in range(2):
            out = jnp.dot(y_band[s * 3 * CY:(s + 1) * 3 * CY, :], pair, preferred_element_type=jnp.float32)
            for kind in range(3):
                y_fields[z, s, kind] = out[kind * CY:(kind + 1) * CY, 0:NX]
                y_fields[z + 1, s, kind] = out[kind * CY:(kind + 1) * CY, NX:2 * NX]

    for s in range(2):
        for y in range(0, CY, 8):
            for kind_y, kinds_z in ((0, (0, 1, 2)), (1, (0, 1)), (2, (0,))):
                planes = [y_fields[z, s, kind_y, y:y + 8, :] for z in range(DEEP)]
                for z in range(SZ):
                    passed = z_pass(planes, s, kinds_z, z)
                    for comp, (_, comp_y, comp_z) in enumerate(KINDS):
                        if comp_y == kind_y:
                            fields_ref[s, z * CY + y:z * CY + y + 8, comp * NX:(comp + 1) * NX] = (
                                passed[comp_z].astype(jnp.bfloat16)
                            )

    lower = index((PART, LANES), 1) < 64
    for m in range(0, NX // 16, 2):
        for part in range(0, ROWS, PART):
            outs = [
                jnp.dot(
                    fields_ref[s, part:part + PART, :], bands[s, :, m * LANES:(m + 2) * LANES],
                    preferred_element_type=jnp.float32,
                )
                for s in range(2)
            ]
            for half in range(2):
                first, second = (out[:, half * LANES:(half + 1) * LANES] for out in outs)
                start = 8 + (m + half) * 2 * ROWS + part
                table[start:start + PART, :] = jnp.where(lower, first, second)
                table[start + ROWS:start + ROWS + PART, :] = jnp.where(lower, second, first)

    eye = (index((LANES, LANES), 0) == index((LANES, LANES), 1)).astype(jnp.bfloat16)
    sublane = index((8, LANES), 0)
    slot_copy.wait()

    def advance(step, side):
        copy_rows(0, side).wait()
        for group in range(STEP_TILES // GROUP):
            blocks = []
            for tile in range(group * GROUP, (group + 1) * GROUP):
                for p in range(0, PTS, 8):
                    merged = None
                    for k in range(8):
                        row = index_rows[side][tile, p + k]
                        loaded = table[pl.ds(row + (8 - k), 8), :]
                        merged = loaded if merged is None else jnp.where(sublane == k, loaded, merged)
                    blocks.append(merged)
            flat = jnp.concatenate(blocks, axis=0).astype(jnp.bfloat16)
            turned = lax.dot_general(eye, flat, (((1,), (1,)), ((), ())), preferred_element_type=jnp.float32)
            picked = []
            for t in range(GROUP):
                column = jnp.broadcast_to(points_ref[pl.ds(step * STEP_TILES + group * GROUP + t, 1), :] & 15, (8, PTS))
                here = turned[:, t * PTS:(t + 1) * PTS]
                both = [here[0:8], here[64:72]]
                for x in range(1, 16):
                    hit = column == x
                    for s in range(2):
                        start = ((x // 8) ^ s) * 64 + (x % 8) * 8
                        both[s] = jnp.where(hit, here[start:start + 8], both[s])
                picked.append(jnp.concatenate(both, axis=0).astype(jnp.bfloat16))
            smooth = jnp.dot(
                jnp.concatenate(picked, axis=0), smoother[...], preferred_element_type=jnp.float32
            ).astype(jnp.bfloat16)
            for t in range(GROUP):
                tiles[slot_ref[0, step * STEP_TILES + group * GROUP + t]] = smooth[t * 16:(t + 1) * 16]
        copy_rows(jnp.minimum(step + 2, STEPS - 1), side).start()

    @pl.loop(0, STEPS // 2)
    def _(i):
        advance(2 * i, 0)
        advance(2 * i + 1, 1)

    copy_rows(0, 0).wait()
    copy_rows(0, 1).wait()
    pack = pack_matrix()
    rows = SEND_ROWS * OWNERS // PACK_PARTS
    copies = []
    for part in range(PACK_PARTS):
        for pair in range(part * 16 // PACK_PARTS, (part + 1) * 16 // PACK_PARTS):
            quads = [tiles[pair * 32 + quad * 16:pair * 32 + (quad + 1) * 16].reshape(256, PTS) for quad in range(2)]
            packed = jnp.dot(pack, jnp.concatenate(quads, axis=1), preferred_element_type=jnp.float32).astype(jnp.bfloat16)
            for quad in range(2):
                start = (pair * 2 + quad) * 4 * SEND_ROWS
                send[start:start + 4 * SEND_ROWS, :] = packed[:, quad * PTS:(quad + 1) * PTS]
        here = slice(part * rows, (part + 1) * rows)
        copy = pltpu.make_async_copy(send.at[here, :], send_hbm.at[here, :], send_sem.at[part])
        copy.start()
        copies.append(copy)
    for copy in copies:
        copy.wait()


def response_kernel(weight_ref, fields_ref, x_band_ref, out_ref):
    for s in range(2):
        parts = [
            jnp.dot(
                fields_ref[s, :, comp * NX:(comp + 1) * NX], x_band_ref[s, KINDS[comp][0]], preferred_element_type=jnp.float32
            )
            for comp in range(COMPS)
        ]
        for o in range(8):
            total = parts[0] * weight_ref[o, 0]
            for comp in range(1, COMPS):
                total = total + parts[comp] * weight_ref[o, comp]
            out_ref[s * 8 + o, 0] = total.astype(jnp.bfloat16)


def mix_kernel(mix_ref, arrived_ref, out_hbm, out, sem):
    copies = []
    for part in range(MIX_PARTS):
        pairs = 16 // MIX_PARTS
        for pair in range(part * pairs, (part + 1) * pairs):
            first = arrived_ref[pair * 8 * SEND_ROWS:(pair * 8 + 4) * SEND_ROWS]
            second = arrived_ref[(pair * 8 + 4) * SEND_ROWS:(pair * 8 + 8) * SEND_ROWS]
            here = jnp.concatenate([first, second], axis=1)
            mixed = jnp.dot(mix_ref[0], here, preferred_element_type=jnp.float32)
            mixed = (mixed + jnp.dot(mix_ref[1], here, preferred_element_type=jnp.float32)).astype(jnp.bfloat16)
            out[pair * 512:pair * 512 + 256, :] = mixed[:, 0:PTS]
            out[pair * 512 + 256:pair * 512 + 512, :] = mixed[:, PTS:2 * PTS]
        rows = slice(part * pairs * 512, (part + 1) * pairs * 512)
        copy = pltpu.make_async_copy(out.at[rows, :], out_hbm.at[rows, :], sem.at[part])
        copy.start()
        copies.append(copy)
    for copy in copies:
        copy.wait()


def orientation_weights(angles):
    polar_angle = angles[0]
    azimuth = angles[1]
    dir_x = jnp.sin(polar_angle) * jnp.cos(azimuth)
    dir_y = jnp.sin(polar_angle) * jnp.sin(azimuth)
    dir_z = jnp.cos(polar_angle)
    return RESPONSE_GAIN * jnp.stack(
        [
            dir_x * dir_x,
            dir_y * dir_y,
            dir_z * dir_z,
            2.0 * dir_x * dir_y,
            2.0 * dir_x * dir_z,
            2.0 * dir_y * dir_z,
        ],
        axis=1,
    )


def swap(value, axis, first):
    pairs = []
    for i in range(first, lax.axis_size(axis) - 1, 2):
        pairs += [(i, i + 1), (i + 1, i)]
    return lax.ppermute(value, axis, pairs)


def mix_matrix(weights):
    scales = jnp.zeros((16, 12), jnp.float32)
    scales = scales.at[0:8, 0:6].set(weights).at[8:16, 6:12].set(weights)
    rows = lax.broadcasted_iota(jnp.int32, (256, 192), 0) // 16
    columns = lax.broadcasted_iota(jnp.int32, (256, 192), 1) // 12
    full = jnp.where(rows == columns, jnp.tile(scales, (16, 16)), 0.0)
    high = full.astype(jnp.bfloat16)
    low = (full - high.astype(jnp.float32)).astype(jnp.bfloat16)
    return jnp.stack([high, low])


def per_device(volume, angles, tile_points, tile_dest):
    even_wide = (lax.axis_index("wide") & 1) == 0
    even_narrow = (lax.axis_index("narrow") & 1) == 0
    first, second = swap(volume, "wide", 0), swap(volume, "wide", 1)
    def extended(rows):
        below, above = first[:, rows], second[:, rows]
        low = jnp.where(even_wide, above, below)[SZ - BORDER:]
        high = jnp.where(even_wide, below, above)[:BORDER]
        return jnp.concatenate([low, volume[:, rows], high], axis=0)

    edge_low, edge_high = extended(slice(0, Y_PAD)), extended(slice(CY - Y_PAD, CY))
    side_first = swap(jnp.where(even_narrow, edge_high, edge_low), "narrow", 0)
    side_second = swap(jnp.where(even_narrow, edge_low, edge_high), "narrow", 1)
    first, second, side_first = lax.optimization_barrier((first, second, side_first))
    center = extended(slice(0, CY))

    weights = orientation_weights(angles)
    mix = mix_matrix(weights)

    vmem = pl.BlockSpec(memory_space=pltpu.VMEM)
    hbm = pl.BlockSpec(memory_space=pltpu.HBM)
    send, fields = pl.pallas_call(
        sample_kernel,
        out_shape=(
            jax.ShapeDtypeStruct((OWNERS * SEND_ROWS, PTS), jnp.bfloat16),
            jax.ShapeDtypeStruct((2, ROWS, COMPS * NX), jnp.bfloat16),
        ),
        in_specs=[vmem] * 5,
        out_specs=(hbm, vmem),
        scratch_shapes=[
            pltpu.VMEM((DEEP, TALL, NX), jnp.bfloat16),
            pltpu.VMEM((DEEP, 2, 3, CY, NX), jnp.float32),
            pltpu.VMEM((2, COMPS * NX, NX * 8), jnp.bfloat16),
            pltpu.VMEM((NX // 8 * ROWS + 16, LANES), jnp.float32),
            pltpu.VMEM((SLOTS, 16, PTS), jnp.bfloat16),
            pltpu.VMEM((6 * CY, TALL), jnp.bfloat16),
            pltpu.VMEM((PTS, PTS), jnp.bfloat16),
            pltpu.VMEM((OWNERS * SEND_ROWS, PTS), jnp.bfloat16),
            pltpu.VMEM((TILES, PTS), jnp.int32),
            pltpu.VMEM((1, TILES), jnp.int32),
            pltpu.SMEM((1, TILES), jnp.int32),
            [pltpu.SMEM((STEP_TILES, PTS), jnp.int32)] * 2,
            pltpu.SemaphoreType.DMA((2,)),
            pltpu.SemaphoreType.DMA((PACK_PARTS,)),
            pltpu.SemaphoreType.DMA,
        ],
        compiler_params=pltpu.CompilerParams(vmem_limit_bytes=32 << 20),
        cost_estimate=pl.CostEstimate(flops=4_000_000_000, bytes_accessed=8_000_000, transcendentals=0),
        name="sample",
    )(
        tile_dest.reshape(1, TILES), tile_points, center, side_first, side_second,
    )

    arrived = lax.all_to_all(
        send.reshape(OWNERS, SEND_ROWS, PTS), ("wide", "narrow"), split_axis=0, concat_axis=0, tiled=True
    )

    responses = pl.pallas_call(
        response_kernel,
        grid=(SZ,),
        out_shape=jax.ShapeDtypeStruct((16, SZ, CY, NX), jnp.bfloat16),
        in_specs=[
            pl.BlockSpec(memory_space=pltpu.SMEM),
            pl.BlockSpec((2, CY, COMPS * NX), lambda z: (0, z, 0)),
            pl.BlockSpec((2, 3, NX, NX), lambda z: (0, 0, 0, 0)),
        ],
        out_specs=pl.BlockSpec((16, 1, CY, NX), lambda z: (0, z, 0, 0)),
        compiler_params=pltpu.CompilerParams(vmem_limit_bytes=16 << 20),
        cost_estimate=pl.CostEstimate(flops=200_000_000, bytes_accessed=4_000_000, transcendentals=0),
        name="respond",
    )(weights, fields, jnp.asarray(x_bands()))

    fibers = pl.pallas_call(
        mix_kernel,
        out_shape=jax.ShapeDtypeStruct((SLOTS * 16, PTS), jnp.bfloat16),
        in_specs=[vmem, vmem],
        out_specs=hbm,
        scratch_shapes=[pltpu.VMEM((SLOTS * 16, PTS), jnp.bfloat16), pltpu.SemaphoreType.DMA((MIX_PARTS,))],
        compiler_params=pltpu.CompilerParams(vmem_limit_bytes=16 << 20),
        cost_estimate=pl.CostEstimate(flops=1_600_000_000, bytes_accessed=4_000_000, transcendentals=0),
        name="mix",
    )(mix, arrived.reshape(OWNERS * SEND_ROWS, PTS))
    return responses, fibers.reshape(OWNERS, CAP, 16, PTS)


def solution(mesh):
    return jax.shard_map(
        per_device,
        mesh=mesh,
        in_specs=(
            P("wide", "narrow", None),
            P(),
            P(("wide", "narrow"), None),
            P(("wide", "narrow"), None),
        ),
        out_specs=(P(None, "wide", "narrow", None), P(("wide", "narrow"), None, None, None)),
        check_vma=False,
    )
```

```python
import jax
import jax.numpy as jnp
import ml_dtypes
import numpy as np
from jax import lax
from jax.experimental import pallas as pl
from jax.experimental.pallas import tpu as pltpu
from jax.sharding import PartitionSpec as P

TAPS_PER_SIDE = 3
SPACINGS = (1, 2)
CAP = 4
BORDER = 6
Y_PAD = 8
RESPONSE_GAIN = 6.0
SMOOTH_SIGMA = 4.0

SZ, CY, NX = 8, 64, 128
ROWS = SZ * CY
DEEP = SZ + 2 * BORDER
TALL = CY + 2 * Y_PAD
COMPS = 6
LANES = 128
TILES = 256
PTS = 128
STEP_TILES = 32
STEPS = TILES // STEP_TILES
GROUP = 4
PART = 512
PACK_PARTS = 4
OWNERS = 128
SLOTS = OWNERS * CAP
SEND_ROWS = CAP * 2 * COMPS
MIX_PARTS = 4

KINDS = ((2, 0, 0), (0, 2, 0), (0, 0, 2), (1, 1, 0), (1, 0, 1), (0, 1, 1))


def tap_table():
    offsets = np.arange(-TAPS_PER_SIDE, TAPS_PER_SIDE + 1).astype(np.float32)
    bell = np.exp(np.float32(-0.5) * offsets * offsets)
    normalized = bell / np.sum(bell)
    taps = np.stack([normalized, -offsets * normalized, (offsets * offsets - 1.0) * normalized])
    return taps.astype(ml_dtypes.bfloat16).astype(np.float32)


TAPS = tap_table()


def tap_values(distance, kind, spacing):
    total = jnp.zeros(distance.shape, jnp.float32)
    for tap in range(2 * TAPS_PER_SIDE + 1):
        if TAPS[kind, tap] != 0.0:
            hit = distance == (tap - TAPS_PER_SIDE) * spacing
            total = jnp.where(hit, float(TAPS[kind, tap]), total)
    return total


def index(shape, axis):
    return lax.broadcasted_iota(jnp.int32, shape, axis)


def fill_y_band(y_band):
    distance = index((CY, TALL), 0) + Y_PAD - index((CY, TALL), 1)
    for s in range(2):
        for kind in range(3):
            start = (s * 3 + kind) * CY
            y_band[start:start + CY, :] = tap_values(distance, kind, SPACINGS[s]).astype(jnp.bfloat16)


def fill_x_bands(bands):
    bands[...] = jnp.zeros_like(bands)
    column = index((48, LANES), 1)
    for s in range(2):
        local = (((column >> 6) ^ s) << 3) + ((column >> 3) & 7)
        distance = local + 16 - index((48, LANES), 0)
        taps = [tap_values(distance, kind, SPACINGS[s]) for kind in range(3)]
        for comp in range(COMPS):
            base = jnp.where((column & 7) == comp, taps[KINDS[comp][0]], 0.0).astype(jnp.bfloat16)
            for m in range(NX // 16):
                first, last = max(0, 16 * m - 16), min(NX, 16 * m + 32)
                skip = first - (16 * m - 16)
                bands[s, comp * NX + first:comp * NX + last, m * LANES:(m + 1) * LANES] = base[skip:skip + last - first]


def smooth_matrix():
    distance = (index((PTS, PTS), 1) - index((PTS, PTS), 0)).astype(jnp.float32)
    bell = jnp.exp(-distance * distance / (2.0 * SMOOTH_SIGMA * SMOOTH_SIGMA))
    return (bell / jnp.sum(bell, axis=0, keepdims=True)).astype(jnp.bfloat16)


def pack_matrix():
    shape = (4 * SEND_ROWS, 4 * CAP * 16)
    row = index(shape, 0)
    slot = (row * 43691) >> 19
    six = (row * 43691) >> 18
    source = slot * 16 + (six - 2 * slot) * 8 + (row - 6 * six)
    return jnp.where(source == index(shape, 1), 1.0, 0.0).astype(jnp.bfloat16)


def x_bands():
    result = np.zeros((2, 3, NX, NX), np.float32)
    for s in range(2):
        for kind in range(3):
            for tap in range(2 * TAPS_PER_SIDE + 1):
                result[s, kind] += TAPS[kind, tap] * np.eye(NX, k=(tap - TAPS_PER_SIDE) * SPACINGS[s], dtype=np.float32)
    return result.astype(ml_dtypes.bfloat16)


def z_pass(planes, s, kinds, z):
    d = SPACINGS[s]
    results = {}
    for kind in kinds:
        total = None
        for side in range(TAPS_PER_SIDE):
            if TAPS[kind, side] == 0.0:
                continue
            shift = (side - TAPS_PER_SIDE) * d
            near, far = planes[z + BORDER - shift], planes[z + BORDER + shift]
            term = float(TAPS[kind, side]) * (near - far if kind == 1 else near + far)
            total = term if total is None else total + term
        if kind != 1:
            total = total + float(TAPS[kind, TAPS_PER_SIDE]) * planes[z + BORDER]
        results[kind] = total
    return results


def sample_kernel(
    slot_ref, rows_ref, center_ref, first_ref, second_ref, column_ref, send_hbm, fields_ref, ext, y_fields, bands, table, tiles,
    y_band, smoother, send, index_rows, sem, send_sem
):
    def copy_rows(step, side):
        return pltpu.make_async_copy(
            rows_ref.at[pl.ds(pl.multiple_of(step * STEP_TILES, STEP_TILES), STEP_TILES)], index_rows[side], sem.at[side]
        )

    copy_rows(0, 0).start()
    copy_rows(1, 1).start()

    ext[:, Y_PAD:Y_PAD + CY, :] = center_ref[...]
    even = (lax.axis_index("narrow") & 1) == 0
    ext[:, 0:Y_PAD, :] = jnp.where(even, second_ref[...], first_ref[...])
    ext[:, Y_PAD + CY:TALL, :] = jnp.where(even, first_ref[...], second_ref[...])
    fill_y_band(y_band)

    for z in range(0, DEEP, 2):
        pair = jnp.concatenate([ext[z], ext[z + 1]], axis=1)
        for s in range(2):
            out = jnp.dot(y_band[s * 3 * CY:(s + 1) * 3 * CY, :], pair, preferred_element_type=jnp.float32)
            for kind in range(3):
                y_fields[z, s, kind] = out[kind * CY:(kind + 1) * CY, 0:NX]
                y_fields[z + 1, s, kind] = out[kind * CY:(kind + 1) * CY, NX:2 * NX]

    fill_x_bands(bands)
    lower = index((ROWS, LANES), 1) < 64
    for s in range(2):
        for y in range(0, CY, 8):
            for kind_y, kinds_z in ((0, (0, 1, 2)), (1, (0, 1)), (2, (0,))):
                planes = [y_fields[z, s, kind_y, y:y + 8, :] for z in range(DEEP)]
                for z in range(SZ):
                    passed = z_pass(planes, s, kinds_z, z)
                    for comp, (_, comp_y, comp_z) in enumerate(KINDS):
                        if comp_y == kind_y:
                            fields_ref[s, z * CY + y:z * CY + y + 8, comp * NX:(comp + 1) * NX] = (
                                passed[comp_z].astype(jnp.bfloat16)
                            )
        own = lower if s == 0 else jnp.logical_not(lower)
        for m in range(0, NX // 16, 2):
            out = jnp.dot(fields_ref[s], bands[s, :, m * LANES:(m + 2) * LANES], preferred_element_type=jnp.float32)
            for half in range(2):
                here = out[:, half * LANES:(half + 1) * LANES]
                start = 8 + (m + half) * 2 * ROWS
                pltpu.store(table.at[start:start + ROWS, :], here, mask=own)
                pltpu.store(table.at[start + ROWS:start + 2 * ROWS, :], here, mask=jnp.logical_not(own))

    tiles[...] = jnp.zeros_like(tiles)
    smoother[...] = smooth_matrix()
    eye = (index((LANES, LANES), 0) == index((LANES, LANES), 1)).astype(jnp.bfloat16)
    sublane = index((8, LANES), 0)

    def advance(step, side):
        copy_rows(0, side).wait()
        for group in range(STEP_TILES // GROUP):
            blocks = []
            for tile in range(group * GROUP, (group + 1) * GROUP):
                for p in range(0, PTS, 8):
                    merged = None
                    for k in range(8):
                        row = index_rows[side][tile, p + k]
                        loaded = table[pl.ds(row + (8 - k), 8), :]
                        merged = loaded if merged is None else jnp.where(sublane == k, loaded, merged)
                    blocks.append(merged)
            flat = jnp.concatenate(blocks, axis=0).astype(jnp.bfloat16)
            turned = lax.dot_general(eye, flat, (((1,), (1,)), ((), ())), preferred_element_type=jnp.float32)
            picked = []
            for t in range(GROUP):
                column = jnp.broadcast_to(column_ref[pl.ds(step * STEP_TILES + group * GROUP + t, 1), :], (8, PTS))
                here = turned[:, t * PTS:(t + 1) * PTS]
                both = [here[0:8], here[64:72]]
                for x in range(1, 16):
                    hit = column == x
                    for s in range(2):
                        start = ((x // 8) ^ s) * 64 + (x % 8) * 8
                        both[s] = jnp.where(hit, here[start:start + 8], both[s])
                picked.append(jnp.concatenate(both, axis=0).astype(jnp.bfloat16))
            smooth = jnp.dot(
                jnp.concatenate(picked, axis=0), smoother[...], preferred_element_type=jnp.float32
            ).astype(jnp.bfloat16)
            for t in range(GROUP):
                tiles[slot_ref[step * STEP_TILES + group * GROUP + t]] = smooth[t * 16:(t + 1) * 16]
        copy_rows(jnp.minimum(step + 2, STEPS - 1), side).start()

    @pl.loop(0, STEPS // 2)
    def _(i):
        advance(2 * i, 0)
        advance(2 * i + 1, 1)

    copy_rows(0, 0).wait()
    copy_rows(0, 1).wait()
    pack = pack_matrix()
    rows = SEND_ROWS * OWNERS // PACK_PARTS
    copies = []
    for part in range(PACK_PARTS):
        for pair in range(part * 16 // PACK_PARTS, (part + 1) * 16 // PACK_PARTS):
            quads = [tiles[pair * 32 + quad * 16:pair * 32 + (quad + 1) * 16].reshape(256, PTS) for quad in range(2)]
            packed = jnp.dot(pack, jnp.concatenate(quads, axis=1), preferred_element_type=jnp.float32).astype(jnp.bfloat16)
            for quad in range(2):
                start = (pair * 2 + quad) * 4 * SEND_ROWS
                send[start:start + 4 * SEND_ROWS, :] = packed[:, quad * PTS:(quad + 1) * PTS]
        here = slice(part * rows, (part + 1) * rows)
        copy = pltpu.make_async_copy(send.at[here, :], send_hbm.at[here, :], send_sem.at[part])
        copy.start()
        copies.append(copy)
    for copy in copies:
        copy.wait()


def response_kernel(weight_ref, fields_ref, x_band_ref, out_ref):
    for s in range(2):
        parts = [
            jnp.dot(
                fields_ref[s, :, comp * NX:(comp + 1) * NX], x_band_ref[s, KINDS[comp][0]], preferred_element_type=jnp.float32
            )
            for comp in range(COMPS)
        ]
        for o in range(8):
            total = parts[0] * weight_ref[o, 0]
            for comp in range(1, COMPS):
                total = total + parts[comp] * weight_ref[o, comp]
            out_ref[s * 8 + o, 0] = total.astype(jnp.bfloat16)


def mix_kernel(mix_ref, arrived_ref, out_hbm, out, sem):
    copies = []
    for part in range(MIX_PARTS):
        pairs = 16 // MIX_PARTS
        for pair in range(part * pairs, (part + 1) * pairs):
            first = arrived_ref[pair * 8 * SEND_ROWS:(pair * 8 + 4) * SEND_ROWS]
            second = arrived_ref[(pair * 8 + 4) * SEND_ROWS:(pair * 8 + 8) * SEND_ROWS]
            here = jnp.concatenate([first, second], axis=1)
            mixed = jnp.dot(mix_ref[0], here, preferred_element_type=jnp.float32)
            mixed = (mixed + jnp.dot(mix_ref[1], here, preferred_element_type=jnp.float32)).astype(jnp.bfloat16)
            out[pair * 512:pair * 512 + 256, :] = mixed[:, 0:PTS]
            out[pair * 512 + 256:pair * 512 + 512, :] = mixed[:, PTS:2 * PTS]
        rows = slice(part * pairs * 512, (part + 1) * pairs * 512)
        copy = pltpu.make_async_copy(out.at[rows, :], out_hbm.at[rows, :], sem.at[part])
        copy.start()
        copies.append(copy)
    for copy in copies:
        copy.wait()


def orientation_weights(angles):
    polar_angle = angles[0]
    azimuth = angles[1]
    dir_x = jnp.sin(polar_angle) * jnp.cos(azimuth)
    dir_y = jnp.sin(polar_angle) * jnp.sin(azimuth)
    dir_z = jnp.cos(polar_angle)
    return RESPONSE_GAIN * jnp.stack(
        [
            dir_x * dir_x,
            dir_y * dir_y,
            dir_z * dir_z,
            2.0 * dir_x * dir_y,
            2.0 * dir_x * dir_z,
            2.0 * dir_y * dir_z,
        ],
        axis=1,
    )


def swap(value, axis, first):
    pairs = []
    for i in range(first, lax.axis_size(axis) - 1, 2):
        pairs += [(i, i + 1), (i + 1, i)]
    return lax.ppermute(value, axis, pairs)


def mix_matrix(weights):
    scales = jnp.zeros((16, 12), jnp.float32)
    scales = scales.at[0:8, 0:6].set(weights).at[8:16, 6:12].set(weights)
    rows = lax.broadcasted_iota(jnp.int32, (256, 192), 0) // 16
    columns = lax.broadcasted_iota(jnp.int32, (256, 192), 1) // 12
    full = jnp.where(rows == columns, jnp.tile(scales, (16, 16)), 0.0)
    high = full.astype(jnp.bfloat16)
    low = (full - high.astype(jnp.float32)).astype(jnp.bfloat16)
    return jnp.stack([high, low])


def per_device(volume, angles, tile_points, tile_dest):
    even_wide = (lax.axis_index("wide") & 1) == 0
    even_narrow = (lax.axis_index("narrow") & 1) == 0
    first, second = swap(volume, "wide", 0), swap(volume, "wide", 1)
    def extended(rows):
        below, above = first[:, rows], second[:, rows]
        low = jnp.where(even_wide, above, below)[SZ - BORDER:]
        high = jnp.where(even_wide, below, above)[:BORDER]
        return jnp.concatenate([low, volume[:, rows], high], axis=0)

    edge_low, edge_high = extended(slice(0, Y_PAD)), extended(slice(CY - Y_PAD, CY))
    side_first = swap(jnp.where(even_narrow, edge_high, edge_low), "narrow", 0)
    side_second = swap(jnp.where(even_narrow, edge_low, edge_high), "narrow", 1)
    first, second, side_first = lax.optimization_barrier((first, second, side_first))
    center = extended(slice(0, CY))

    table_rows = ((tile_points >> 3) & 15) * ROWS + (tile_points >> 7)
    columns = tile_points & 15
    dest = tile_dest[:, 0]
    earlier = lax.broadcasted_iota(jnp.int32, (TILES, TILES), 0)
    later = lax.broadcasted_iota(jnp.int32, (TILES, TILES), 1)
    same_owner = (dest[:, None] == dest[None, :]) & (earlier < later)
    slot = dest * CAP + jnp.sum(same_owner.astype(jnp.int32), axis=0)

    weights = orientation_weights(angles)
    mix = mix_matrix(weights)

    vmem = pl.BlockSpec(memory_space=pltpu.VMEM)
    hbm = pl.BlockSpec(memory_space=pltpu.HBM)
    send, fields = pl.pallas_call(
        sample_kernel,
        out_shape=(
            jax.ShapeDtypeStruct((OWNERS * SEND_ROWS, PTS), jnp.bfloat16),
            jax.ShapeDtypeStruct((2, ROWS, COMPS * NX), jnp.bfloat16),
        ),
        in_specs=[pl.BlockSpec(memory_space=pltpu.SMEM)] + [vmem] * 5,
        out_specs=(hbm, vmem),
        scratch_shapes=[
            pltpu.VMEM((DEEP, TALL, NX), jnp.bfloat16),
            pltpu.VMEM((DEEP, 2, 3, CY, NX), jnp.float32),
            pltpu.VMEM((2, COMPS * NX, NX * 8), jnp.bfloat16),
            pltpu.VMEM((NX // 8 * ROWS + 16, LANES), jnp.float32),
            pltpu.VMEM((SLOTS, 16, PTS), jnp.bfloat16),
            pltpu.VMEM((6 * CY, TALL), jnp.bfloat16),
            pltpu.VMEM((PTS, PTS), jnp.bfloat16),
            pltpu.VMEM((OWNERS * SEND_ROWS, PTS), jnp.bfloat16),
            [pltpu.SMEM((STEP_TILES, PTS), jnp.int32)] * 2,
            pltpu.SemaphoreType.DMA((2,)),
            pltpu.SemaphoreType.DMA((PACK_PARTS,)),
        ],
        compiler_params=pltpu.CompilerParams(vmem_limit_bytes=32 << 20),
        cost_estimate=pl.CostEstimate(flops=4_000_000_000, bytes_accessed=8_000_000, transcendentals=0),
        name="sample",
    )(
        slot, table_rows, center, side_first, side_second, columns,
    )

    arrived = lax.all_to_all(
        send.reshape(OWNERS, SEND_ROWS, PTS), ("wide", "narrow"), split_axis=0, concat_axis=0, tiled=True
    )

    responses = pl.pallas_call(
        response_kernel,
        grid=(SZ,),
        out_shape=jax.ShapeDtypeStruct((16, SZ, CY, NX), jnp.bfloat16),
        in_specs=[
            pl.BlockSpec(memory_space=pltpu.SMEM),
            pl.BlockSpec((2, CY, COMPS * NX), lambda z: (0, z, 0)),
            pl.BlockSpec((2, 3, NX, NX), lambda z: (0, 0, 0, 0)),
        ],
        out_specs=pl.BlockSpec((16, 1, CY, NX), lambda z: (0, z, 0, 0)),
        compiler_params=pltpu.CompilerParams(vmem_limit_bytes=16 << 20),
        cost_estimate=pl.CostEstimate(flops=200_000_000, bytes_accessed=4_000_000, transcendentals=0),
        name="respond",
    )(weights, fields, jnp.asarray(x_bands()))

    fibers = pl.pallas_call(
        mix_kernel,
        out_shape=jax.ShapeDtypeStruct((SLOTS * 16, PTS), jnp.bfloat16),
        in_specs=[vmem, vmem],
        out_specs=hbm,
        scratch_shapes=[pltpu.VMEM((SLOTS * 16, PTS), jnp.bfloat16), pltpu.SemaphoreType.DMA((MIX_PARTS,))],
        compiler_params=pltpu.CompilerParams(vmem_limit_bytes=16 << 20),
        cost_estimate=pl.CostEstimate(flops=1_600_000_000, bytes_accessed=4_000_000, transcendentals=0),
        name="mix",
    )(mix, arrived.reshape(OWNERS * SEND_ROWS, PTS))
    return responses, fibers.reshape(OWNERS, CAP, 16, PTS)


def solution(mesh):
    return jax.shard_map(
        per_device,
        mesh=mesh,
        in_specs=(
            P("wide", "narrow", None),
            P(),
            P(("wide", "narrow"), None),
            P(("wide", "narrow"), None),
        ),
        out_specs=(P(None, "wide", "narrow", None), P(("wide", "narrow"), None, None, None)),
        check_vma=False,
    )
```

```python
import jax
import jax.numpy as jnp
import ml_dtypes
import numpy as np
from jax import lax
from jax.experimental import pallas as pl
from jax.experimental.pallas import tpu as pltpu
from jax.sharding import PartitionSpec as P

TAPS_PER_SIDE = 3
SPACINGS = (1, 2)
CAP = 4
BORDER = 6
Y_PAD = 8
RESPONSE_GAIN = 6.0
SMOOTH_SIGMA = 4.0

SZ, CY, NX = 8, 64, 128
ROWS = SZ * CY
DEEP = SZ + 2 * BORDER
TALL = CY + 2 * Y_PAD
COMPS = 6
LANES = 128
TILES = 256
PTS = 128
STEP_TILES = 32
STEPS = TILES // STEP_TILES
GROUP = 4
PART = 512
PACK_PARTS = 4
OWNERS = 128
SLOTS = OWNERS * CAP
SEND_ROWS = CAP * 2 * COMPS
MIX_PARTS = 4

KINDS = ((2, 0, 0), (0, 2, 0), (0, 0, 2), (1, 1, 0), (1, 0, 1), (0, 1, 1))


def tap_table():
    offsets = np.arange(-TAPS_PER_SIDE, TAPS_PER_SIDE + 1).astype(np.float32)
    bell = np.exp(np.float32(-0.5) * offsets * offsets)
    normalized = bell / np.sum(bell)
    taps = np.stack([normalized, -offsets * normalized, (offsets * offsets - 1.0) * normalized])
    return taps.astype(ml_dtypes.bfloat16).astype(np.float32)


TAPS = tap_table()


def tap_values(distance, kind, spacing):
    total = jnp.zeros(distance.shape, jnp.float32)
    for tap in range(2 * TAPS_PER_SIDE + 1):
        if TAPS[kind, tap] != 0.0:
            hit = distance == (tap - TAPS_PER_SIDE) * spacing
            total = jnp.where(hit, float(TAPS[kind, tap]), total)
    return total


def index(shape, axis):
    return lax.broadcasted_iota(jnp.int32, shape, axis)


def fill_y_band(y_band):
    distance = index((CY, TALL), 0) + Y_PAD - index((CY, TALL), 1)
    for s in range(2):
        for kind in range(3):
            start = (s * 3 + kind) * CY
            y_band[start:start + CY, :] = tap_values(distance, kind, SPACINGS[s]).astype(jnp.bfloat16)


def fill_x_bands(bands):
    bands[...] = jnp.zeros_like(bands)
    column = index((48, LANES), 1)
    for s in range(2):
        local = (((column >> 6) ^ s) << 3) + ((column >> 3) & 7)
        distance = local + 16 - index((48, LANES), 0)
        taps = [tap_values(distance, kind, SPACINGS[s]) for kind in range(3)]
        for comp in range(COMPS):
            base = jnp.where((column & 7) == comp, taps[KINDS[comp][0]], 0.0).astype(jnp.bfloat16)
            for m in range(NX // 16):
                first, last = max(0, 16 * m - 16), min(NX, 16 * m + 32)
                skip = first - (16 * m - 16)
                bands[s, comp * NX + first:comp * NX + last, m * LANES:(m + 1) * LANES] = base[skip:skip + last - first]


def smooth_matrix():
    distance = (index((PTS, PTS), 1) - index((PTS, PTS), 0)).astype(jnp.float32)
    bell = jnp.exp(-distance * distance / (2.0 * SMOOTH_SIGMA * SMOOTH_SIGMA))
    return (bell / jnp.sum(bell, axis=0, keepdims=True)).astype(jnp.bfloat16)


def pack_matrix():
    shape = (4 * SEND_ROWS, 4 * CAP * 16)
    row = index(shape, 0)
    slot = (row * 43691) >> 19
    six = (row * 43691) >> 18
    source = slot * 16 + (six - 2 * slot) * 8 + (row - 6 * six)
    return jnp.where(source == index(shape, 1), 1.0, 0.0).astype(jnp.bfloat16)


def x_bands():
    result = np.zeros((2, 3, NX, NX), np.float32)
    for s in range(2):
        for kind in range(3):
            for tap in range(2 * TAPS_PER_SIDE + 1):
                result[s, kind] += TAPS[kind, tap] * np.eye(NX, k=(tap - TAPS_PER_SIDE) * SPACINGS[s], dtype=np.float32)
    return result.astype(ml_dtypes.bfloat16)


def z_pass(planes, s, kinds, z):
    d = SPACINGS[s]
    results = {}
    for kind in kinds:
        total = None
        for side in range(TAPS_PER_SIDE):
            if TAPS[kind, side] == 0.0:
                continue
            shift = (side - TAPS_PER_SIDE) * d
            near, far = planes[z + BORDER - shift], planes[z + BORDER + shift]
            term = float(TAPS[kind, side]) * (near - far if kind == 1 else near + far)
            total = term if total is None else total + term
        if kind != 1:
            total = total + float(TAPS[kind, TAPS_PER_SIDE]) * planes[z + BORDER]
        results[kind] = total
    return results


def sample_kernel(
    slot_ref, rows_ref, center_ref, first_ref, second_ref, column_ref, send_hbm, fields_ref, ext, y_fields, bands, table, tiles,
    y_band, smoother, send, index_rows, sem, send_sem
):
    def copy_rows(step, side):
        return pltpu.make_async_copy(
            rows_ref.at[pl.ds(pl.multiple_of(step * STEP_TILES, STEP_TILES), STEP_TILES)], index_rows[side], sem.at[side]
        )

    copy_rows(0, 0).start()
    copy_rows(1, 1).start()

    ext[:, Y_PAD:Y_PAD + CY, :] = center_ref[...]
    even = (lax.axis_index("narrow") & 1) == 0
    ext[:, 0:Y_PAD, :] = jnp.where(even, second_ref[...], first_ref[...])
    ext[:, Y_PAD + CY:TALL, :] = jnp.where(even, first_ref[...], second_ref[...])
    fill_y_band(y_band)

    for z in range(0, DEEP, 2):
        pair = jnp.concatenate([ext[z], ext[z + 1]], axis=1)
        for s in range(2):
            out = jnp.dot(y_band[s * 3 * CY:(s + 1) * 3 * CY, :], pair, preferred_element_type=jnp.float32)
            for kind in range(3):
                y_fields[z, s, kind] = out[kind * CY:(kind + 1) * CY, 0:NX]
                y_fields[z + 1, s, kind] = out[kind * CY:(kind + 1) * CY, NX:2 * NX]

    fill_x_bands(bands)
    lower = index((ROWS, LANES), 1) < 64
    for s in range(2):
        for y in range(0, CY, 8):
            for kind_y, kinds_z in ((0, (0, 1, 2)), (1, (0, 1)), (2, (0,))):
                planes = [y_fields[z, s, kind_y, y:y + 8, :] for z in range(DEEP)]
                for z in range(SZ):
                    passed = z_pass(planes, s, kinds_z, z)
                    for comp, (_, comp_y, comp_z) in enumerate(KINDS):
                        if comp_y == kind_y:
                            fields_ref[s, z * CY + y:z * CY + y + 8, comp * NX:(comp + 1) * NX] = (
                                passed[comp_z].astype(jnp.bfloat16)
                            )
        own = lower if s == 0 else jnp.logical_not(lower)
        for m in range(0, NX // 16, 2):
            out = jnp.dot(fields_ref[s], bands[s, :, m * LANES:(m + 2) * LANES], preferred_element_type=jnp.float32)
            for half in range(2):
                here = out[:, half * LANES:(half + 1) * LANES]
                start = 8 + (m + half) * 2 * ROWS
                pltpu.store(table.at[start:start + ROWS, :], here, mask=own)
                pltpu.store(table.at[start + ROWS:start + 2 * ROWS, :], here, mask=jnp.logical_not(own))

    tiles[...] = jnp.zeros_like(tiles)
    smoother[...] = smooth_matrix()
    eye = (index((LANES, LANES), 0) == index((LANES, LANES), 1)).astype(jnp.bfloat16)
    sublane = index((8, LANES), 0)

    def advance(step, side):
        copy_rows(0, side).wait()
        for group in range(STEP_TILES // GROUP):
            blocks = []
            for tile in range(group * GROUP, (group + 1) * GROUP):
                for p in range(0, PTS, 8):
                    merged = None
                    for k in range(8):
                        row = index_rows[side][tile, p + k]
                        loaded = table[pl.ds(row + (8 - k), 8), :]
                        merged = loaded if merged is None else jnp.where(sublane == k, loaded, merged)
                    blocks.append(merged)
            flat = jnp.concatenate(blocks, axis=0).astype(jnp.bfloat16)
            turned = lax.dot_general(eye, flat, (((1,), (1,)), ((), ())), preferred_element_type=jnp.float32)
            picked = []
            for t in range(GROUP):
                column = jnp.broadcast_to(column_ref[pl.ds(step * STEP_TILES + group * GROUP + t, 1), :], (8, PTS))
                here = turned[:, t * PTS:(t + 1) * PTS]
                both = [here[0:8], here[64:72]]
                for x in range(1, 16):
                    hit = column == x
                    for s in range(2):
                        start = ((x // 8) ^ s) * 64 + (x % 8) * 8
                        both[s] = jnp.where(hit, here[start:start + 8], both[s])
                picked.append(jnp.concatenate(both, axis=0).astype(jnp.bfloat16))
            smooth = jnp.dot(
                jnp.concatenate(picked, axis=0), smoother[...], preferred_element_type=jnp.float32
            ).astype(jnp.bfloat16)
            for t in range(GROUP):
                tiles[slot_ref[step * STEP_TILES + group * GROUP + t]] = smooth[t * 16:(t + 1) * 16]
        copy_rows(jnp.minimum(step + 2, STEPS - 1), side).start()

    @pl.loop(0, STEPS // 2)
    def _(i):
        advance(2 * i, 0)
        advance(2 * i + 1, 1)

    copy_rows(0, 0).wait()
    copy_rows(0, 1).wait()
    pack = pack_matrix()
    rows = SEND_ROWS * OWNERS // PACK_PARTS
    copies = []
    for part in range(PACK_PARTS):
        for pair in range(part * 16 // PACK_PARTS, (part + 1) * 16 // PACK_PARTS):
            quads = [tiles[pair * 32 + quad * 16:pair * 32 + (quad + 1) * 16].reshape(256, PTS) for quad in range(2)]
            packed = jnp.dot(pack, jnp.concatenate(quads, axis=1), preferred_element_type=jnp.float32).astype(jnp.bfloat16)
            for quad in range(2):
                start = (pair * 2 + quad) * 4 * SEND_ROWS
                send[start:start + 4 * SEND_ROWS, :] = packed[:, quad * PTS:(quad + 1) * PTS]
        here = slice(part * rows, (part + 1) * rows)
        copy = pltpu.make_async_copy(send.at[here, :], send_hbm.at[here, :], send_sem.at[part])
        copy.start()
        copies.append(copy)
    for copy in copies:
        copy.wait()


def response_kernel(weight_ref, fields_ref, x_band_ref, out_ref):
    for s in range(2):
        parts = [
            jnp.dot(
                fields_ref[s, :, comp * NX:(comp + 1) * NX], x_band_ref[s, KINDS[comp][0]], preferred_element_type=jnp.float32
            )
            for comp in range(COMPS)
        ]
        for o in range(8):
            total = parts[0] * weight_ref[o, 0]
            for comp in range(1, COMPS):
                total = total + parts[comp] * weight_ref[o, comp]
            out_ref[s * 8 + o, 0] = total.astype(jnp.bfloat16)


def mix_kernel(mix_ref, arrived_ref, out_hbm, out, sem):
    copies = []
    for part in range(MIX_PARTS):
        pairs = 16 // MIX_PARTS
        for pair in range(part * pairs, (part + 1) * pairs):
            first = arrived_ref[pair * 8 * SEND_ROWS:(pair * 8 + 4) * SEND_ROWS]
            second = arrived_ref[(pair * 8 + 4) * SEND_ROWS:(pair * 8 + 8) * SEND_ROWS]
            here = jnp.concatenate([first, second], axis=1)
            mixed = jnp.dot(mix_ref[0], here, preferred_element_type=jnp.float32)
            mixed = (mixed + jnp.dot(mix_ref[1], here, preferred_element_type=jnp.float32)).astype(jnp.bfloat16)
            out[pair * 512:pair * 512 + 256, :] = mixed[:, 0:PTS]
            out[pair * 512 + 256:pair * 512 + 512, :] = mixed[:, PTS:2 * PTS]
        rows = slice(part * pairs * 512, (part + 1) * pairs * 512)
        copy = pltpu.make_async_copy(out.at[rows, :], out_hbm.at[rows, :], sem.at[part])
        copy.start()
        copies.append(copy)
    for copy in copies:
        copy.wait()


def orientation_weights(angles):
    polar_angle = angles[0]
    azimuth = angles[1]
    dir_x = jnp.sin(polar_angle) * jnp.cos(azimuth)
    dir_y = jnp.sin(polar_angle) * jnp.sin(azimuth)
    dir_z = jnp.cos(polar_angle)
    return RESPONSE_GAIN * jnp.stack(
        [
            dir_x * dir_x,
            dir_y * dir_y,
            dir_z * dir_z,
            2.0 * dir_x * dir_y,
            2.0 * dir_x * dir_z,
            2.0 * dir_y * dir_z,
        ],
        axis=1,
    )


def swap(value, axis, first):
    pairs = []
    for i in range(first, lax.axis_size(axis) - 1, 2):
        pairs += [(i, i + 1), (i + 1, i)]
    return lax.ppermute(value, axis, pairs)


def mix_matrix(weights):
    scales = jnp.zeros((16, 12), jnp.float32)
    scales = scales.at[0:8, 0:6].set(weights).at[8:16, 6:12].set(weights)
    rows = lax.broadcasted_iota(jnp.int32, (256, 192), 0) // 16
    columns = lax.broadcasted_iota(jnp.int32, (256, 192), 1) // 12
    full = jnp.where(rows == columns, jnp.tile(scales, (16, 16)), 0.0)
    high = full.astype(jnp.bfloat16)
    low = (full - high.astype(jnp.float32)).astype(jnp.bfloat16)
    return jnp.stack([high, low])


def per_device(volume, angles, tile_points, tile_dest):
    even_wide = (lax.axis_index("wide") & 1) == 0
    even_narrow = (lax.axis_index("narrow") & 1) == 0
    first, second = swap(volume, "wide", 0), swap(volume, "wide", 1)
    def extended(rows):
        below, above = first[:, rows], second[:, rows]
        low = jnp.where(even_wide, above, below)[SZ - BORDER:]
        high = jnp.where(even_wide, below, above)[:BORDER]
        return jnp.concatenate([low, volume[:, rows], high], axis=0)

    edge_low, edge_high = extended(slice(0, Y_PAD)), extended(slice(CY - Y_PAD, CY))
    side_first = swap(jnp.where(even_narrow, edge_high, edge_low), "narrow", 0)
    side_second = swap(jnp.where(even_narrow, edge_low, edge_high), "narrow", 1)
    first, second, side_second = lax.optimization_barrier((first, second, side_second))
    center = extended(slice(0, CY))

    table_rows = ((tile_points >> 3) & 15) * ROWS + (tile_points >> 7)
    columns = tile_points & 15
    dest = tile_dest[:, 0]
    earlier = lax.broadcasted_iota(jnp.int32, (TILES, TILES), 0)
    later = lax.broadcasted_iota(jnp.int32, (TILES, TILES), 1)
    same_owner = (dest[:, None] == dest[None, :]) & (earlier < later)
    slot = dest * CAP + jnp.sum(same_owner.astype(jnp.int32), axis=0)

    weights = orientation_weights(angles)
    mix = mix_matrix(weights)

    vmem = pl.BlockSpec(memory_space=pltpu.VMEM)
    hbm = pl.BlockSpec(memory_space=pltpu.HBM)
    send, fields = pl.pallas_call(
        sample_kernel,
        out_shape=(
            jax.ShapeDtypeStruct((OWNERS * SEND_ROWS, PTS), jnp.bfloat16),
            jax.ShapeDtypeStruct((2, ROWS, COMPS * NX), jnp.bfloat16),
        ),
        in_specs=[pl.BlockSpec(memory_space=pltpu.SMEM)] + [vmem] * 5,
        out_specs=(hbm, vmem),
        scratch_shapes=[
            pltpu.VMEM((DEEP, TALL, NX), jnp.bfloat16),
            pltpu.VMEM((DEEP, 2, 3, CY, NX), jnp.float32),
            pltpu.VMEM((2, COMPS * NX, NX * 8), jnp.bfloat16),
            pltpu.VMEM((NX // 8 * ROWS + 16, LANES), jnp.float32),
            pltpu.VMEM((SLOTS, 16, PTS), jnp.bfloat16),
            pltpu.VMEM((6 * CY, TALL), jnp.bfloat16),
            pltpu.VMEM((PTS, PTS), jnp.bfloat16),
            pltpu.VMEM((OWNERS * SEND_ROWS, PTS), jnp.bfloat16),
            [pltpu.SMEM((STEP_TILES, PTS), jnp.int32)] * 2,
            pltpu.SemaphoreType.DMA((2,)),
            pltpu.SemaphoreType.DMA((PACK_PARTS,)),
        ],
        compiler_params=pltpu.CompilerParams(vmem_limit_bytes=32 << 20),
        cost_estimate=pl.CostEstimate(flops=4_000_000_000, bytes_accessed=8_000_000, transcendentals=0),
        name="sample",
    )(
        slot, table_rows, center, side_first, side_second, columns,
    )

    arrived = lax.all_to_all(
        send.reshape(OWNERS, SEND_ROWS, PTS), ("wide", "narrow"), split_axis=0, concat_axis=0, tiled=True
    )

    responses = pl.pallas_call(
        response_kernel,
        grid=(SZ,),
        out_shape=jax.ShapeDtypeStruct((16, SZ, CY, NX), jnp.bfloat16),
        in_specs=[
            pl.BlockSpec(memory_space=pltpu.SMEM),
            pl.BlockSpec((2, CY, COMPS * NX), lambda z: (0, z, 0)),
            pl.BlockSpec((2, 3, NX, NX), lambda z: (0, 0, 0, 0)),
        ],
        out_specs=pl.BlockSpec((16, 1, CY, NX), lambda z: (0, z, 0, 0)),
        compiler_params=pltpu.CompilerParams(vmem_limit_bytes=16 << 20),
        cost_estimate=pl.CostEstimate(flops=200_000_000, bytes_accessed=4_000_000, transcendentals=0),
        name="respond",
    )(weights, fields, jnp.asarray(x_bands()))

    fibers = pl.pallas_call(
        mix_kernel,
        out_shape=jax.ShapeDtypeStruct((SLOTS * 16, PTS), jnp.bfloat16),
        in_specs=[vmem, vmem],
        out_specs=hbm,
        scratch_shapes=[pltpu.VMEM((SLOTS * 16, PTS), jnp.bfloat16), pltpu.SemaphoreType.DMA((MIX_PARTS,))],
        compiler_params=pltpu.CompilerParams(vmem_limit_bytes=16 << 20),
        cost_estimate=pl.CostEstimate(flops=1_600_000_000, bytes_accessed=4_000_000, transcendentals=0),
        name="mix",
    )(mix, arrived.reshape(OWNERS * SEND_ROWS, PTS))
    return responses, fibers.reshape(OWNERS, CAP, 16, PTS)


def solution(mesh):
    return jax.shard_map(
        per_device,
        mesh=mesh,
        in_specs=(
            P("wide", "narrow", None),
            P(),
            P(("wide", "narrow"), None),
            P(("wide", "narrow"), None),
        ),
        out_specs=(P(None, "wide", "narrow", None), P(("wide", "narrow"), None, None, None)),
        check_vma=False,
    )
```

```python
import jax
import jax.numpy as jnp
import ml_dtypes
import numpy as np
from jax import lax
from jax.experimental import pallas as pl
from jax.experimental.pallas import tpu as pltpu
from jax.sharding import PartitionSpec as P

TAPS_PER_SIDE = 3
SPACINGS = (1, 2)
CAP = 4
BORDER = 6
Y_PAD = 8
RESPONSE_GAIN = 6.0
SMOOTH_SIGMA = 4.0

SZ, CY, NX = 8, 64, 128
ROWS = SZ * CY
DEEP = SZ + 2 * BORDER
TALL = CY + 2 * Y_PAD
COMPS = 6
LANES = 128
TILES = 256
PTS = 128
STEP_TILES = 64
STEPS = TILES // STEP_TILES
GROUP = 4
PART = 512
PACK_PARTS = 4
OWNERS = 128
SLOTS = OWNERS * CAP
SEND_ROWS = CAP * 2 * COMPS
MIX_PARTS = 8

KINDS = ((2, 0, 0), (0, 2, 0), (0, 0, 2), (1, 1, 0), (1, 0, 1), (0, 1, 1))


def tap_table():
    offsets = np.arange(-TAPS_PER_SIDE, TAPS_PER_SIDE + 1).astype(np.float32)
    bell = np.exp(np.float32(-0.5) * offsets * offsets)
    normalized = bell / np.sum(bell)
    taps = np.stack([normalized, -offsets * normalized, (offsets * offsets - 1.0) * normalized])
    return taps.astype(ml_dtypes.bfloat16).astype(np.float32)


TAPS = tap_table()


def tap_values(distance, kind, spacing):
    total = jnp.zeros(distance.shape, jnp.float32)
    for tap in range(2 * TAPS_PER_SIDE + 1):
        if TAPS[kind, tap] != 0.0:
            hit = distance == (tap - TAPS_PER_SIDE) * spacing
            total = jnp.where(hit, float(TAPS[kind, tap]), total)
    return total


def index(shape, axis):
    return lax.broadcasted_iota(jnp.int32, shape, axis)


def fill_y_band(y_band):
    distance = index((CY, TALL), 0) + Y_PAD - index((CY, TALL), 1)
    for s in range(2):
        for kind in range(3):
            start = (s * 3 + kind) * CY
            y_band[start:start + CY, :] = tap_values(distance, kind, SPACINGS[s]).astype(jnp.bfloat16)


def fill_x_bands(bands):
    bands[...] = jnp.zeros_like(bands)
    column = index((48, LANES), 1)
    for s in range(2):
        local = (((column >> 6) ^ s) << 3) + ((column >> 3) & 7)
        distance = local + 16 - index((48, LANES), 0)
        taps = [tap_values(distance, kind, SPACINGS[s]) for kind in range(3)]
        for comp in range(COMPS):
            base = jnp.where((column & 7) == comp, taps[KINDS[comp][0]], 0.0).astype(jnp.bfloat16)
            for m in range(NX // 16):
                first, last = max(0, 16 * m - 16), min(NX, 16 * m + 32)
                skip = first - (16 * m - 16)
                bands[s, comp * NX + first:comp * NX + last, m * LANES:(m + 1) * LANES] = base[skip:skip + last - first]


def smooth_matrix():
    distance = (index((PTS, PTS), 1) - index((PTS, PTS), 0)).astype(jnp.float32)
    bell = jnp.exp(-distance * distance / (2.0 * SMOOTH_SIGMA * SMOOTH_SIGMA))
    return (bell / jnp.sum(bell, axis=0, keepdims=True)).astype(jnp.bfloat16)


def pack_matrix():
    shape = (4 * SEND_ROWS, 4 * CAP * 16)
    row = index(shape, 0)
    slot = (row * 43691) >> 19
    six = (row * 43691) >> 18
    source = slot * 16 + (six - 2 * slot) * 8 + (row - 6 * six)
    return jnp.where(source == index(shape, 1), 1.0, 0.0).astype(jnp.bfloat16)


def x_bands():
    result = np.zeros((2, 3, NX, NX), np.float32)
    for s in range(2):
        for kind in range(3):
            for tap in range(2 * TAPS_PER_SIDE + 1):
                result[s, kind] += TAPS[kind, tap] * np.eye(NX, k=(tap - TAPS_PER_SIDE) * SPACINGS[s], dtype=np.float32)
    return result.astype(ml_dtypes.bfloat16)


def z_pass(planes, s, kinds, z):
    d = SPACINGS[s]
    results = {}
    for kind in kinds:
        total = None
        for side in range(TAPS_PER_SIDE):
            if TAPS[kind, side] == 0.0:
                continue
            shift = (side - TAPS_PER_SIDE) * d
            near, far = planes[z + BORDER - shift], planes[z + BORDER + shift]
            term = float(TAPS[kind, side]) * (near - far if kind == 1 else near + far)
            total = term if total is None else total + term
        if kind != 1:
            total = total + float(TAPS[kind, TAPS_PER_SIDE]) * planes[z + BORDER]
        results[kind] = total
    return results


def sample_kernel(
    slot_ref, rows_ref, center_ref, first_ref, second_ref, column_ref, send_hbm, fields_ref, ext, y_fields, bands, table, tiles,
    y_band, smoother, send, index_rows, sem, send_sem
):
    def copy_rows(step, side):
        return pltpu.make_async_copy(
            rows_ref.at[pl.ds(pl.multiple_of(step * STEP_TILES, STEP_TILES), STEP_TILES)], index_rows[side], sem.at[side]
        )

    copy_rows(0, 0).start()
    copy_rows(1, 1).start()

    ext[:, Y_PAD:Y_PAD + CY, :] = center_ref[...]
    even = (lax.axis_index("narrow") & 1) == 0
    ext[:, 0:Y_PAD, :] = jnp.where(even, second_ref[...], first_ref[...])
    ext[:, Y_PAD + CY:TALL, :] = jnp.where(even, first_ref[...], second_ref[...])
    fill_y_band(y_band)

    for z in range(0, DEEP, 2):
        pair = jnp.concatenate([ext[z], ext[z + 1]], axis=1)
        for s in range(2):
            out = jnp.dot(y_band[s * 3 * CY:(s + 1) * 3 * CY, :], pair, preferred_element_type=jnp.float32)
            for kind in range(3):
                y_fields[z, s, kind] = out[kind * CY:(kind + 1) * CY, 0:NX]
                y_fields[z + 1, s, kind] = out[kind * CY:(kind + 1) * CY, NX:2 * NX]

    fill_x_bands(bands)
    lower = index((ROWS, LANES), 1) < 64
    for s in range(2):
        for y in range(0, CY, 8):
            for kind_y, kinds_z in ((0, (0, 1, 2)), (1, (0, 1)), (2, (0,))):
                planes = [y_fields[z, s, kind_y, y:y + 8, :] for z in range(DEEP)]
                for z in range(SZ):
                    passed = z_pass(planes, s, kinds_z, z)
                    for comp, (_, comp_y, comp_z) in enumerate(KINDS):
                        if comp_y == kind_y:
                            fields_ref[s, z * CY + y:z * CY + y + 8, comp * NX:(comp + 1) * NX] = (
                                passed[comp_z].astype(jnp.bfloat16)
                            )
        own = lower if s == 0 else jnp.logical_not(lower)
        for m in range(0, NX // 16, 2):
            out = jnp.dot(fields_ref[s], bands[s, :, m * LANES:(m + 2) * LANES], preferred_element_type=jnp.float32)
            for half in range(2):
                here = out[:, half * LANES:(half + 1) * LANES]
                start = 8 + (m + half) * 2 * ROWS
                pltpu.store(table.at[start:start + ROWS, :], here, mask=own)
                pltpu.store(table.at[start + ROWS:start + 2 * ROWS, :], here, mask=jnp.logical_not(own))

    tiles[...] = jnp.zeros_like(tiles)
    smoother[...] = smooth_matrix()
    eye = (index((LANES, LANES), 0) == index((LANES, LANES), 1)).astype(jnp.bfloat16)
    sublane = index((8, LANES), 0)

    def advance(step, side):
        copy_rows(0, side).wait()
        for group in range(STEP_TILES // GROUP):
            blocks = []
            for tile in range(group * GROUP, (group + 1) * GROUP):
                for p in range(0, PTS, 8):
                    merged = None
                    for k in range(8):
                        row = index_rows[side][tile, p + k]
                        loaded = table[pl.ds(row + (8 - k), 8), :]
                        merged = loaded if merged is None else jnp.where(sublane == k, loaded, merged)
                    blocks.append(merged)
            flat = jnp.concatenate(blocks, axis=0).astype(jnp.bfloat16)
            turned = lax.dot_general(eye, flat, (((1,), (1,)), ((), ())), preferred_element_type=jnp.float32)
            picked = []
            for t in range(GROUP):
                column = jnp.broadcast_to(column_ref[pl.ds(step * STEP_TILES + group * GROUP + t, 1), :], (8, PTS))
                here = turned[:, t * PTS:(t + 1) * PTS]
                both = [here[0:8], here[64:72]]
                for x in range(1, 16):
                    hit = column == x
                    for s in range(2):
                        start = ((x // 8) ^ s) * 64 + (x % 8) * 8
                        both[s] = jnp.where(hit, here[start:start + 8], both[s])
                picked.append(jnp.concatenate(both, axis=0).astype(jnp.bfloat16))
            smooth = jnp.dot(
                jnp.concatenate(picked, axis=0), smoother[...], preferred_element_type=jnp.float32
            ).astype(jnp.bfloat16)
            for t in range(GROUP):
                tiles[slot_ref[step * STEP_TILES + group * GROUP + t]] = smooth[t * 16:(t + 1) * 16]
        copy_rows(jnp.minimum(step + 2, STEPS - 1), side).start()

    @pl.loop(0, STEPS // 2)
    def _(i):
        advance(2 * i, 0)
        advance(2 * i + 1, 1)

    copy_rows(0, 0).wait()
    copy_rows(0, 1).wait()
    pack = pack_matrix()
    rows = SEND_ROWS * OWNERS // PACK_PARTS
    copies = []
    for part in range(PACK_PARTS):
        for pair in range(part * 16 // PACK_PARTS, (part + 1) * 16 // PACK_PARTS):
            quads = [tiles[pair * 32 + quad * 16:pair * 32 + (quad + 1) * 16].reshape(256, PTS) for quad in range(2)]
            packed = jnp.dot(pack, jnp.concatenate(quads, axis=1), preferred_element_type=jnp.float32).astype(jnp.bfloat16)
            for quad in range(2):
                start = (pair * 2 + quad) * 4 * SEND_ROWS
                send[start:start + 4 * SEND_ROWS, :] = packed[:, quad * PTS:(quad + 1) * PTS]
        here = slice(part * rows, (part + 1) * rows)
        copy = pltpu.make_async_copy(send.at[here, :], send_hbm.at[here, :], send_sem.at[part])
        copy.start()
        copies.append(copy)
    for copy in copies:
        copy.wait()


def response_kernel(weight_ref, fields_ref, x_band_ref, out_ref):
    for s in range(2):
        parts = [
            jnp.dot(
                fields_ref[s, :, comp * NX:(comp + 1) * NX], x_band_ref[s, KINDS[comp][0]], preferred_element_type=jnp.float32
            )
            for comp in range(COMPS)
        ]
        for o in range(8):
            total = parts[0] * weight_ref[o, 0]
            for comp in range(1, COMPS):
                total = total + parts[comp] * weight_ref[o, comp]
            out_ref[s * 8 + o, 0] = total.astype(jnp.bfloat16)


def mix_kernel(mix_ref, arrived_ref, out_hbm, out, sem):
    copies = []
    for part in range(MIX_PARTS):
        pairs = 16 // MIX_PARTS
        for pair in range(part * pairs, (part + 1) * pairs):
            first = arrived_ref[pair * 8 * SEND_ROWS:(pair * 8 + 4) * SEND_ROWS]
            second = arrived_ref[(pair * 8 + 4) * SEND_ROWS:(pair * 8 + 8) * SEND_ROWS]
            here = jnp.concatenate([first, second], axis=1)
            mixed = jnp.dot(mix_ref[0], here, preferred_element_type=jnp.float32)
            mixed = (mixed + jnp.dot(mix_ref[1], here, preferred_element_type=jnp.float32)).astype(jnp.bfloat16)
            out[pair * 512:pair * 512 + 256, :] = mixed[:, 0:PTS]
            out[pair * 512 + 256:pair * 512 + 512, :] = mixed[:, PTS:2 * PTS]
        rows = slice(part * pairs * 512, (part + 1) * pairs * 512)
        copy = pltpu.make_async_copy(out.at[rows, :], out_hbm.at[rows, :], sem.at[part])
        copy.start()
        copies.append(copy)
    for copy in copies:
        copy.wait()


def orientation_weights(angles):
    polar_angle = angles[0]
    azimuth = angles[1]
    dir_x = jnp.sin(polar_angle) * jnp.cos(azimuth)
    dir_y = jnp.sin(polar_angle) * jnp.sin(azimuth)
    dir_z = jnp.cos(polar_angle)
    return RESPONSE_GAIN * jnp.stack(
        [
            dir_x * dir_x,
            dir_y * dir_y,
            dir_z * dir_z,
            2.0 * dir_x * dir_y,
            2.0 * dir_x * dir_z,
            2.0 * dir_y * dir_z,
        ],
        axis=1,
    )


def swap(value, axis, first):
    pairs = []
    for i in range(first, lax.axis_size(axis) - 1, 2):
        pairs += [(i, i + 1), (i + 1, i)]
    return lax.ppermute(value, axis, pairs)


def mix_matrix(weights):
    scales = jnp.zeros((16, 12), jnp.float32)
    scales = scales.at[0:8, 0:6].set(weights).at[8:16, 6:12].set(weights)
    rows = lax.broadcasted_iota(jnp.int32, (256, 192), 0) // 16
    columns = lax.broadcasted_iota(jnp.int32, (256, 192), 1) // 12
    full = jnp.where(rows == columns, jnp.tile(scales, (16, 16)), 0.0)
    high = full.astype(jnp.bfloat16)
    low = (full - high.astype(jnp.float32)).astype(jnp.bfloat16)
    return jnp.stack([high, low])


def per_device(volume, angles, tile_points, tile_dest):
    even_wide = (lax.axis_index("wide") & 1) == 0
    even_narrow = (lax.axis_index("narrow") & 1) == 0
    first, second = swap(volume, "wide", 0), swap(volume, "wide", 1)
    def extended(rows):
        below, above = first[:, rows], second[:, rows]
        low = jnp.where(even_wide, above, below)[SZ - BORDER:]
        high = jnp.where(even_wide, below, above)[:BORDER]
        return jnp.concatenate([low, volume[:, rows], high], axis=0)

    edge_low, edge_high = extended(slice(0, Y_PAD)), extended(slice(CY - Y_PAD, CY))
    side_first = swap(jnp.where(even_narrow, edge_high, edge_low), "narrow", 0)
    side_second = swap(jnp.where(even_narrow, edge_low, edge_high), "narrow", 1)
    first, second, side_second = lax.optimization_barrier((first, second, side_second))
    center = extended(slice(0, CY))

    table_rows = ((tile_points >> 3) & 15) * ROWS + (tile_points >> 7)
    columns = tile_points & 15
    dest = tile_dest[:, 0]
    earlier = lax.broadcasted_iota(jnp.int32, (TILES, TILES), 0)
    later = lax.broadcasted_iota(jnp.int32, (TILES, TILES), 1)
    same_owner = (dest[:, None] == dest[None, :]) & (earlier < later)
    slot = dest * CAP + jnp.sum(same_owner.astype(jnp.int32), axis=0)

    weights = orientation_weights(angles)
    mix = mix_matrix(weights)

    vmem = pl.BlockSpec(memory_space=pltpu.VMEM)
    hbm = pl.BlockSpec(memory_space=pltpu.HBM)
    send, fields = pl.pallas_call(
        sample_kernel,
        out_shape=(
            jax.ShapeDtypeStruct((OWNERS * SEND_ROWS, PTS), jnp.bfloat16),
            jax.ShapeDtypeStruct((2, ROWS, COMPS * NX), jnp.bfloat16),
        ),
        in_specs=[pl.BlockSpec(memory_space=pltpu.SMEM)] + [vmem] * 5,
        out_specs=(hbm, vmem),
        scratch_shapes=[
            pltpu.VMEM((DEEP, TALL, NX), jnp.bfloat16),
            pltpu.VMEM((DEEP, 2, 3, CY, NX), jnp.float32),
            pltpu.VMEM((2, COMPS * NX, NX * 8), jnp.bfloat16),
            pltpu.VMEM((NX // 8 * ROWS + 16, LANES), jnp.float32),
            pltpu.VMEM((SLOTS, 16, PTS), jnp.bfloat16),
            pltpu.VMEM((6 * CY, TALL), jnp.bfloat16),
            pltpu.VMEM((PTS, PTS), jnp.bfloat16),
            pltpu.VMEM((OWNERS * SEND_ROWS, PTS), jnp.bfloat16),
            [pltpu.SMEM((STEP_TILES, PTS), jnp.int32)] * 2,
            pltpu.SemaphoreType.DMA((2,)),
            pltpu.SemaphoreType.DMA((PACK_PARTS,)),
        ],
        compiler_params=pltpu.CompilerParams(vmem_limit_bytes=32 << 20),
        cost_estimate=pl.CostEstimate(flops=4_000_000_000, bytes_accessed=8_000_000, transcendentals=0),
        name="sample",
    )(
        slot, table_rows, center, side_first, side_second, columns,
    )

    arrived = lax.all_to_all(
        send.reshape(OWNERS, SEND_ROWS, PTS), ("wide", "narrow"), split_axis=0, concat_axis=0, tiled=True
    )

    responses = pl.pallas_call(
        response_kernel,
        grid=(SZ,),
        out_shape=jax.ShapeDtypeStruct((16, SZ, CY, NX), jnp.bfloat16),
        in_specs=[
            pl.BlockSpec(memory_space=pltpu.SMEM),
            pl.BlockSpec((2, CY, COMPS * NX), lambda z: (0, z, 0)),
            pl.BlockSpec((2, 3, NX, NX), lambda z: (0, 0, 0, 0)),
        ],
        out_specs=pl.BlockSpec((16, 1, CY, NX), lambda z: (0, z, 0, 0)),
        compiler_params=pltpu.CompilerParams(vmem_limit_bytes=16 << 20),
        cost_estimate=pl.CostEstimate(flops=200_000_000, bytes_accessed=4_000_000, transcendentals=0),
        name="respond",
    )(weights, fields, jnp.asarray(x_bands()))

    fibers = pl.pallas_call(
        mix_kernel,
        out_shape=jax.ShapeDtypeStruct((SLOTS * 16, PTS), jnp.bfloat16),
        in_specs=[vmem, vmem],
        out_specs=hbm,
        scratch_shapes=[pltpu.VMEM((SLOTS * 16, PTS), jnp.bfloat16), pltpu.SemaphoreType.DMA((MIX_PARTS,))],
        compiler_params=pltpu.CompilerParams(vmem_limit_bytes=16 << 20),
        cost_estimate=pl.CostEstimate(flops=1_600_000_000, bytes_accessed=4_000_000, transcendentals=0),
        name="mix",
    )(mix, arrived.reshape(OWNERS * SEND_ROWS, PTS))
    return responses, fibers.reshape(OWNERS, CAP, 16, PTS)


def solution(mesh):
    return jax.shard_map(
        per_device,
        mesh=mesh,
        in_specs=(
            P("wide", "narrow", None),
            P(),
            P(("wide", "narrow"), None),
            P(("wide", "narrow"), None),
        ),
        out_specs=(P(None, "wide", "narrow", None), P(("wide", "narrow"), None, None, None)),
        check_vma=False,
    )
```
